32 devices in a mesh: heads: 4 (over y, x), seq: 8 (over z, core).
Axes of the slice: x: 2, y: 2, z: 4, core: 2. Of those that a mesh axis runs over, the one named last changes fastest.
Arguments:
- tokens: bfloat16 [7168, 2048], P('seq'), may hold values from -6 to 6
- w_qkv: bfloat16 [2048, 3, 2048], P(None, None, 'heads'), may hold values from -0.1875 to 0.1875
- w_out: bfloat16 [2048, 2048], P('heads'), may hold values from -0.75 to 0.75
- w_up: bfloat16 [2048, 8192], P('seq', 'heads'), may hold values from -0.125 to 0.125
- w_down: bfloat16 [8192, 2048], P('heads', 'seq'), may hold values from -0.0625 to 0.0625
- gain_attn: float32 [2048], replicated, may hold values from 0.1 to 1.9
- gain_ffn: float32 [2048], replicated, may hold values from 0.1 to 1.9
- w_router: float32 [2048, 8], replicated, may hold values from -0.25 to 0.25
- head_quarters: int32 [5], replicated, may hold values from 1 to 4, as said below
- ffn_quarters: int32 [5], replicated, may hold values from 1 to 4, as said below
- router_targets: int32 [5, 2], replicated, may hold values from 0 to 3
- cotangent: bfloat16 [7168, 2048], P('seq'), may hold values from -6 to 6
Outputs:
- output: bfloat16 [7168, 2048], P('seq')
- grad_tokens: float32 [7168, 2048], P('seq')
- grad_qkv: float32 [2048, 3, 2048], P(None, None, 'heads')
- grad_out: float32 [2048, 2048], P('heads')
- grad_up: float32 [2048, 8192], P('seq', 'heads')
- grad_down: float32 [8192, 2048], P('heads', 'seq')
- grad_gain_attn: float32 [2048], replicated
- grad_gain_ffn: float32 [2048], replicated
- grad_router: float32 [2048, 8], replicated
The draws below stay inside these ranges and needn't reach their ends.
Inputs may be any that keep to these rules, and one draw needn't show every extreme that they name: Sequence s uses the first head_quarters[s] * 4 heads; some sequence uses all heads and some a quarter of them. Sequence s uses the first ffn_quarters[s] * 2048 hidden units; some sequence uses all and some a quarter.
All inputs are finite; a program needn't handle non-finite values.
Results may differ from the reference program's by a relative error of at most 0.023.
Values may be sent and summed in bfloat16 or wider, within the bound.
No kernel may reach another device: no remote copies, remote signals or barrier semaphores. Data moves between devices by JAX's collectives and lax.ppermute only.
A program may use at most 256 MiB of HBM per device.

```python
import jax
import jax.numpy as jnp
from jax import lax

D = 2048
H = 16
HD = 128
FF = 8192
SHORT_DEV = 128
NSHORT = 3
NLONG = 2
LEVELS = 4
SEQS = 5
TOK_DEV = 896
TOKENS = 7168


def quarter_levels(key, count):
    levels = jax.random.randint(key, (count,), 1, LEVELS + 1)
    places = jax.random.permutation(jax.random.fold_in(key, 7), count)
    levels = levels.at[places[0]].set(LEVELS)
    levels = levels.at[places[1]].set(1)
    return levels.astype(jnp.int32)


def draw_head_quarters(key, part):
    return quarter_levels(jax.random.fold_in(key, 11), NSHORT + NLONG)


def draw_ffn_quarters(key, part):
    return quarter_levels(jax.random.fold_in(key, 23), NSHORT + NLONG)


def draw_router_targets(key, part):
    former = quarter_levels(jax.random.fold_in(key, 31), NSHORT + NLONG) - 1
    latter = quarter_levels(jax.random.fold_in(key, 37), NSHORT + NLONG) - 1
    return jnp.stack([former, latter], axis=1).astype(jnp.int32)


def block_levels(key, shape, cuts, smallest, largest):
    level = 1.0
    for axis_at, blocks in cuts:
        steps = jax.random.uniform(jax.random.fold_in(jax.random.fold_in(key, 6), axis_at), (blocks,), jnp.float32, smallest / len(cuts), largest / len(cuts))
        level = level * jnp.repeat(jnp.exp(steps), shape[axis_at] // blocks).reshape((-1,) + (1,) * (len(shape) - 1 - axis_at))
    return level


def scatter_about(own_key, dims, scale, bound, shards=(), kind=jnp.bfloat16):
    factor_of = block_levels(own_key, dims, shards, -0.22, 0.18) if shards else 1.0
    drawn = jax.random.normal(own_key, dims, jnp.float32) * scale * factor_of
    return jnp.minimum(jnp.maximum(drawn, -bound), bound).astype(kind)


def setup_inputs(seed: int = 0) -> dict:
    seeds = jax.random.split(jax.random.key(seed), 13)
    tokens = scatter_about(seeds[0], (TOKENS, D), 1.0, 6.0, ((0, 8),))
    w_qkv = scatter_about(seeds[1], (D, 3, H * HD), (D // 2) ** -0.5, 0.1875, ((2, 4),))
    w_out = scatter_about(seeds[2], (H * HD, D), (H * HD // 32) ** -0.5, 0.75, ((0, 4),))
    w_up = scatter_about(seeds[3], (D, FF), D ** -0.5, 0.125, ((0, 8), (1, 4)))
    w_down = scatter_about(seeds[4], (FF, D), FF ** -0.5, 0.0625, ((0, 4), (1, 8)))
    gain_attn = jnp.clip(1.0 + 0.18 * jax.random.normal(seeds[5], (D,), jnp.float32), 0.1, 1.9)
    gain_ffn = jnp.clip(1.0 + 0.18 * jax.random.normal(seeds[6], (D,), jnp.float32), 0.1, 1.9)
    w_router = scatter_about(seeds[7], (D, 2 * LEVELS), (D // 4) ** -0.5, 0.25, (), jnp.float32)
    head_quarters = draw_head_quarters(jax.random.fold_in(seeds[12], 71), 0)
    ffn_quarters = draw_ffn_quarters(jax.random.fold_in(seeds[12], 71), 0)
    router_targets = draw_router_targets(jax.random.fold_in(seeds[12], 71), 0)
    cotangent = scatter_about(seeds[11], (TOKENS, D), 1.0, 6.0, ((0, 8),))
    return dict(tokens=tokens, w_qkv=w_qkv, w_out=w_out, w_up=w_up, w_down=w_down, gain_attn=gain_attn, gain_ffn=gain_ffn, w_router=w_router, head_quarters=head_quarters, ffn_quarters=ffn_quarters, router_targets=router_targets, cotangent=cotangent)


@jax.custom_vjp
def low(v):
    return lax.optimization_barrier(v.astype(jnp.bfloat16)).astype(jnp.float32)

@jax.custom_vjp
def low_back(v):
    return v

def low_keep(v):
    return (low(v), None)

def low_pass(kept, grad):
    return (grad,)

def back_keep(v):
    return (v, None)

def back_low(kept, grad):
    return (low(grad),)
low.defvjp(low_keep, low_pass)
low_back.defvjp(back_keep, back_low)
highest = lax.Precision.HIGHEST
epsilon = 1e-05

def matmul(left, right):
    return jnp.dot(left, right, precision=highest, preferred_element_type=jnp.float32)

def normalize(values, gain):
    centered = values - lax.optimization_barrier(jnp.mean(values, axis=-1, keepdims=True))
    inverse = lax.rsqrt(lax.optimization_barrier(jnp.mean(centered * centered, axis=-1, keepdims=True)) + epsilon)
    return centered * inverse * gain

def rotate(values, cosine, sine):
    half_dim = values.shape[-1] // 2
    former = values[..., :half_dim]
    latter = values[..., half_dim:]
    return jnp.concatenate([former * cosine - latter * sine, latter * cosine + former * sine], axis=-1)

def rank_count():
    return TOKENS // TOK_DEV

def row_layout():
    ranks = rank_count()
    column = jnp.arange(TOK_DEV)[None, :]
    block_rank = jnp.arange(ranks)[:, None]
    short_rows = NSHORT * SHORT_DEV
    is_short = column < short_rows
    offset = column - short_rows
    seq_id = jnp.where(is_short, column // SHORT_DEV, NSHORT + offset // (2 * SHORT_DEV))
    seq_id = jnp.broadcast_to(seq_id, (ranks, TOK_DEV))
    position = jnp.where(is_short, block_rank * SHORT_DEV + column % SHORT_DEV, block_rank * 2 * SHORT_DEV + offset % (2 * SHORT_DEV))
    return (seq_id.reshape(-1).astype(jnp.int32), position.reshape(-1).astype(jnp.int32))

def to_shapes(values):
    ranks = rank_count()
    others = values.shape[1:]
    grid = values.reshape((ranks, TOK_DEV) + others)
    short_rows = NSHORT * SHORT_DEV
    shorter = grid[:, :short_rows].reshape((ranks, NSHORT, SHORT_DEV) + others)
    shorter = jnp.moveaxis(shorter, 0, 1).reshape((NSHORT, ranks * SHORT_DEV) + others)
    longer = grid[:, short_rows:].reshape((ranks, NLONG, 2 * SHORT_DEV) + others)
    longer = jnp.moveaxis(longer, 0, 1).reshape((NLONG, ranks * 2 * SHORT_DEV) + others)
    return (shorter, longer)

def from_shapes(shorter, longer):
    ranks = rank_count()
    others = shorter.shape[2:]
    shorter = jnp.moveaxis(shorter.reshape((NSHORT, ranks, SHORT_DEV) + others), 1, 0)
    shorter = shorter.reshape((ranks, NSHORT * SHORT_DEV) + others)
    longer = jnp.moveaxis(longer.reshape((NLONG, ranks, 2 * SHORT_DEV) + others), 1, 0)
    longer = longer.reshape((ranks, NLONG * 2 * SHORT_DEV) + others)
    return jnp.concatenate([shorter, longer], axis=1).reshape((TOKENS,) + others)

def attend(query, keys, values):
    length = query.shape[1]
    block = 512 if length % 512 == 0 else length
    scale = HD ** (-0.5)

    def one_sequence(items):
        seq_query, seq_keys, seq_values = items
        pieces = seq_query.reshape((length // block, block) + seq_query.shape[1:])
        starts = jnp.arange(length // block) * block

        def one_block(inner):
            piece, start_row = inner
            scores = low_back(jnp.einsum('qhd,khd->hqk', piece, seq_keys, precision=highest) * scale)
            allowed = jnp.arange(length)[None, :] <= (start_row + jnp.arange(block))[:, None]
            scores = jnp.where(allowed[None], scores, -1e+30)
            probs = low(jax.nn.softmax(scores, axis=-1))
            return jnp.einsum('hqk,khd->qhd', probs, seq_values, precision=highest)
        outputs = lax.map(jax.checkpoint(one_block), (pieces, starts))
        return outputs.reshape(seq_query.shape)
    return lax.map(jax.checkpoint(one_sequence), (query, keys, values))

def reference(tokens, w_qkv, w_out, w_up, w_down, gain_attn, gain_ffn, w_router, head_quarters, ffn_quarters, router_targets, cotangent):
    ranks = rank_count()
    seq_id, position = row_layout()
    member = (seq_id[:, None] == jnp.arange(SEQS)[None, :]).astype(jnp.float32)
    seq_length = jnp.where(jnp.arange(SEQS) < NSHORT, SHORT_DEV * ranks, 2 * SHORT_DEV * ranks).astype(jnp.float32)
    head_limit = head_quarters[seq_id] * (H // LEVELS)
    head_live = (jnp.arange(H)[None, :] < head_limit[:, None]).astype(jnp.float32)
    unit_limit = ffn_quarters[seq_id] * (FF // LEVELS)
    ffn_live = (jnp.arange(FF)[None, :] < unit_limit[:, None]).astype(jnp.float32)
    half_dim = HD // 2
    frequency = 10000.0 ** (-jnp.arange(half_dim, dtype=jnp.float32) * 2.0 / HD)
    angle = position.astype(jnp.float32)[:, None] * frequency[None, :]
    cosine = jnp.cos(angle)[:, None, :]
    sine = jnp.sin(angle)[:, None, :]

    def forward(inputs, weight_qkv, weight_out, weight_up, weight_down, gain_one, gain_two, weight_router):
        normed_one = normalize(inputs, gain_one)
        normed_low = low(normed_one)
        projected = matmul(normed_low, weight_qkv.reshape(D, 3 * H * HD)).reshape(TOKENS, 3, H, HD)
        query = low(rotate(low_back(projected[:, 0]), cosine, sine))
        keys = low(rotate(low_back(projected[:, 1]), cosine, sine))
        values = low(low_back(projected[:, 2]))
        short_query, long_query = to_shapes(query)
        short_keys, long_keys = to_shapes(keys)
        short_values, long_values = to_shapes(values)
        attended = from_shapes(attend(short_query, short_keys, short_values), attend(long_query, long_keys, long_values))
        heads_out = low(low_back(attended * head_live[:, :, None])).reshape(TOKENS, H * HD)
        hidden = inputs + low_back(matmul(heads_out, weight_out))
        normed_two = low(normalize(hidden, gain_two))
        upward = low_back(matmul(normed_two, weight_up))
        active = low(low_back(jnp.square(jnp.maximum(upward, 0.0)) * ffn_live))
        result = hidden + low_back(matmul(active, weight_down))
        pooled = matmul(member.T, normed_one) * lax.rsqrt(seq_length)[:, None]
        logits = matmul(pooled, weight_router)
        loss = jnp.zeros((), jnp.float32)
        for group in range(2):
            group_logits = logits[:, LEVELS * group:LEVELS * (group + 1)]
            chosen = (jnp.arange(LEVELS)[None, :] == router_targets[:, group][:, None]).astype(jnp.float32)
            picked = lax.optimization_barrier(jnp.sum(group_logits * chosen, axis=1))
            loss = loss + jnp.sum(jax.nn.logsumexp(group_logits, axis=1) - picked)
        return (result, loss)
    primals = (tokens.astype(jnp.float32), w_qkv.astype(jnp.float32), w_out.astype(jnp.float32), w_up.astype(jnp.float32), w_down.astype(jnp.float32), gain_attn, gain_ffn, w_router)
    (result, loss), pullback = jax.vjp(forward, *primals)
    grads = pullback((cotangent.astype(jnp.float32), jnp.ones_like(loss)))
    return (result.astype(jnp.bfloat16), grads[0], grads[1], grads[2], grads[3], grads[4], grads[5], grads[6], grads[7])
```

```python
import functools

import jax
import jax.numpy as jnp
from jax import lax
from jax.experimental import pallas as pl
from jax.experimental.pallas import tpu as pltpu
from jax.sharding import PartitionSpec as P

D = 2048
H = 16
HD = 128
FF = 8192
SHORT_DEV = 128
NSHORT = 3
NLONG = 2
LEVELS = 4
SEQS = 5
CHUNKS = NSHORT + 2 * NLONG

epsilon = 1e-05
highest = lax.Precision.HIGHEST
f32 = jnp.float32
bf16 = jnp.bfloat16
SCALE = HD ** (-0.5)


def dot(left, right):
    return jnp.dot(left, right, preferred_element_type=f32)


def contract(left, right, left_dim, right_dim):
    return lax.dot_general(
        left, right, (((left_dim,), (right_dim,)), ((), ())), preferred_element_type=f32
    )


def normalize_parts(values):
    centered = values - jnp.mean(values, axis=-1, keepdims=True)
    inverse = lax.rsqrt(jnp.mean(centered * centered, axis=-1, keepdims=True) + epsilon)
    return (centered * inverse, inverse)


def normalize_back(grad_normed, normed_hat, inverse, gain):
    grad_hat = grad_normed * gain
    middle = (
        grad_hat
        - jnp.mean(grad_hat, axis=-1, keepdims=True)
        - normed_hat * jnp.mean(grad_hat * normed_hat, axis=-1, keepdims=True)
    )
    return (inverse * middle, jnp.sum(grad_normed * normed_hat, axis=0))


def flip(values, axis, size, bit):
    return lax.ppermute(values, axis, [(i, i ^ bit) for i in range(size)])


def butterfly(values, axis, size):
    bit = 1
    while bit < size:
        values = values + flip(values, axis, size, bit)
        bit *= 2
    return values


def key_copies(scal, own, others, keys_short, keys_long, sems, members, heads):
    head, member = scal[0], scal[1]
    copies = []
    for part in range(members):
        source = own if part == 0 else others[(part - 1) * heads : part * heads]
        whose = lax.rem(member + part, members)
        for slot in range(heads):
            block = (head ^ slot) * members + whose
            number = len(copies)
            copies.append(
                pltpu.make_async_copy(
                    source[slot].at[0:NSHORT], keys_short.at[:, block], sems.at[number]
                )
            )
            for index in range(NLONG):
                first = NSHORT + 2 * index
                number = len(copies)
                copies.append(
                    pltpu.make_async_copy(
                        source[slot].at[first : first + 2],
                        keys_long.at[index, block],
                        sems.at[number],
                    )
                )
    return copies


def row_copies(scal, slots, held, sems, heads, outward):
    head = scal[0]
    copies = []
    for slot in range(heads):
        ends = (slots[slot], held.at[head ^ slot])
        if outward:
            ends = ends[::-1]
        copies.append(pltpu.make_async_copy(ends[0], ends[1], sems.at[slot]))
    return copies


def sequence_loop(work):
    def short(index, carry):
        work(0, index, index, 1, index)
        return carry

    def long(index, carry):
        work(1, index, NSHORT + 2 * index, 2, NSHORT + index)
        return carry

    lax.fori_loop(0, NSHORT, short, 0)
    lax.fori_loop(0, NLONG, long, 0)


def allowed_mask(member, members, size):
    key_at = lax.broadcasted_iota(jnp.int32, (members * size, size), 0)
    query_at = lax.broadcasted_iota(jnp.int32, (members * size, size), 1) + member * size
    return key_at <= query_at


def attend_kernel(heads, members, scal, *refs):
    count = heads
    query_slots = refs[:count]
    own = refs[count : 2 * count]
    others = refs[2 * count : (1 + members) * count]
    rest = refs[(1 + members) * count :]
    out_slots = rest[:count]
    log_ref = rest[count]
    queries, keys_short, keys_long, mixed, row_sems, key_sems = rest[count + 1 :]
    copies = row_copies(scal, query_slots, queries, row_sems, heads, False)
    copies += key_copies(scal, own, others, keys_short, keys_long, key_sems, members, heads)
    for copy in copies:
        copy.start()
    for copy in copies:
        copy.wait()

    def work(kind, index, first, chunks, live_at):
        size = chunks * SHORT_DEV
        live = scal[2 + live_at].astype(f32)
        mask = allowed_mask(scal[1], members, size)
        for place in range(heads):
            span = (place + 1) * members
            if kind == 0:
                block = keys_short[index, 0:span]
            else:
                block = keys_long[index, 0:span]
            block = block.reshape(span * size, 2 * HD)
            keys, values = block[:, :HD], block[:, HD:]
            query = queries[place, pl.ds(first, chunks)].reshape(size, HD)
            scores = contract(keys, query, 1, 1) * SCALE
            edge = place * members * size
            last = jnp.where(mask, scores[edge:], -1e30)
            largest = jnp.max(last, axis=0, keepdims=True)
            if place:
                early = scores[:edge]
                largest = jnp.maximum(largest, jnp.max(early, axis=0, keepdims=True))
            raised = jnp.exp(last - largest)
            total = jnp.sum(raised, axis=0, keepdims=True)
            low = raised.astype(bf16)
            turned = contract(values[edge:], low, 0, 0)
            if place:
                raised = jnp.exp(early - largest)
                total = total + jnp.sum(raised, axis=0, keepdims=True)
                turned = turned + contract(values[:edge], raised.astype(bf16), 0, 0)
            turned = turned * (live / total)
            mixed[place, pl.ds(first, chunks)] = (
                turned.T.astype(bf16).reshape(chunks, SHORT_DEV, HD)
            )
            logs = largest + jnp.log(total)
            for chunk in range(chunks):
                log_ref[place, first + chunk] = logs[:, chunk * SHORT_DEV : (chunk + 1) * SHORT_DEV]

    sequence_loop(work)
    copies = row_copies(scal, out_slots, mixed, row_sems, heads, True)
    for copy in copies:
        copy.start()
    for copy in copies:
        copy.wait()


def attend_forward(scal, query_slots, own, others, heads, members):
    blocks = heads * members
    anywhere = pl.BlockSpec(memory_space=pl.ANY)
    result = pl.pallas_call(
        functools.partial(attend_kernel, heads, members),
        out_shape=[jax.ShapeDtypeStruct((CHUNKS, SHORT_DEV, HD), bf16)] * heads
        + [jax.ShapeDtypeStruct((heads, CHUNKS, 1, SHORT_DEV), f32)],
        in_specs=[pl.BlockSpec(memory_space=pltpu.SMEM)]
        + [anywhere] * (len(query_slots) + len(own) + len(others)),
        out_specs=[anywhere] * heads + [pl.BlockSpec(memory_space=pltpu.VMEM)],
        scratch_shapes=[
            pltpu.VMEM((heads, CHUNKS, SHORT_DEV, HD), bf16),
            pltpu.VMEM((NSHORT, blocks, SHORT_DEV, 2 * HD), bf16),
            pltpu.VMEM((NLONG, blocks, 2, SHORT_DEV, 2 * HD), bf16),
            pltpu.VMEM((heads, CHUNKS, SHORT_DEV, HD), bf16),
            pltpu.SemaphoreType.DMA((heads,)),
            pltpu.SemaphoreType.DMA((3 * blocks,)),
        ],
        compiler_params=pltpu.CompilerParams(vmem_limit_bytes=56 << 20),
        cost_estimate=pl.CostEstimate(
            flops=4 * 10**9, bytes_accessed=7 << 20, transcendentals=4 * 10**6
        ),
        name="attend_forward",
    )(scal, *query_slots, *own, *others)
    return (result[:heads], result[heads])


def back_kernel(heads, members, scal, *refs):
    count = heads
    query_slots = refs[:count]
    own = refs[count : 2 * count]
    others = refs[2 * count : (1 + members) * count]
    rest = refs[(1 + members) * count :]
    grad_slots = rest[:count]
    log_ref = rest[count]
    rest = rest[count + 1 :]
    query_out = rest[:count]
    pair_out = rest[count : (1 + members) * count]
    scratch = rest[(1 + members) * count :]
    queries, keys_short, keys_long, grads, sum_short, sum_long = scratch[:6]
    low_short, low_long, row_sems, grad_sems, key_sems = scratch[6:]
    copies = row_copies(scal, query_slots, queries, row_sems, heads, False)
    copies += row_copies(scal, grad_slots, grads, grad_sems, heads, False)
    copies += key_copies(scal, own, others, keys_short, keys_long, key_sems, members, heads)
    for copy in copies:
        copy.start()
    for copy in copies:
        copy.wait()

    def work(kind, index, first, chunks, live_at):
        size = chunks * SHORT_DEV
        live = scal[2 + live_at].astype(bf16)
        mask = allowed_mask(scal[1], members, size)
        if kind == 0:
            keys_ref, sum_ref, low_ref = keys_short, sum_short, low_short
        else:
            keys_ref, sum_ref, low_ref = keys_long, sum_long, low_long
        for place in reversed(range(heads)):
            span = (place + 1) * members
            block = keys_ref[index, 0:span].reshape(span * size, 2 * HD)
            keys, values = block[:, :HD], block[:, HD:]
            query = queries[place, pl.ds(first, chunks)].reshape(size, HD)
            grad = grads[place, pl.ds(first, chunks)].reshape(size, HD) * live
            logs = jnp.concatenate(
                [log_ref[place, first + chunk] for chunk in range(chunks)], axis=1
            )
            probs = jnp.exp(contract(keys, query, 1, 1) * SCALE - logs)
            edge = place * members * size
            last = jnp.where(mask, probs[edge:], 0.0)
            probs = jnp.concatenate([probs[:edge], last], axis=0) if place else last
            grad_probs = contract(values, grad, 1, 1)
            delta = jnp.sum(probs * grad_probs, axis=0, keepdims=True)
            grad_scores = (probs * (grad_probs - delta)).astype(bf16)
            grad_value = dot(probs.astype(bf16), grad)
            grad_key = dot(grad_scores, query) * SCALE
            turned = contract(keys, grad_scores, 0, 0) * SCALE
            queries[place, pl.ds(first, chunks)] = (
                turned.T.astype(bf16).reshape(chunks, SHORT_DEV, HD)
            )
            pair = jnp.concatenate([grad_key, grad_value], axis=1)
            if place == heads - 1:
                sum_ref[...] = pair
            else:
                sum_ref[0 : span * size] += pair
        low_ref[index] = sum_ref[...].astype(bf16).reshape(low_ref.shape[1:])

    sequence_loop(work)
    copies = row_copies(scal, query_out, queries, row_sems, heads, True)
    head, member = scal[0], scal[1]
    number = 0
    for part in range(members):
        whose = lax.rem(member + part, members)
        for slot in range(heads):
            block = (head ^ slot) * members + whose
            target = pair_out[part * heads + slot]
            copies.append(
                pltpu.make_async_copy(
                    low_short.at[:, block], target.at[0:NSHORT], key_sems.at[number]
                )
            )
            number += 1
            for index in range(NLONG):
                first = NSHORT + 2 * index
                copies.append(
                    pltpu.make_async_copy(
                        low_long.at[index, block],
                        target.at[first : first + 2],
                        key_sems.at[number],
                    )
                )
                number += 1
    for copy in copies:
        copy.start()
    for copy in copies:
        copy.wait()


def attend_backward(scal, query_slots, own, others, grad_slots, logs, heads, members):
    blocks = heads * members
    anywhere = pl.BlockSpec(memory_space=pl.ANY)
    result = pl.pallas_call(
        functools.partial(back_kernel, heads, members),
        out_shape=[jax.ShapeDtypeStruct((CHUNKS, SHORT_DEV, HD), bf16)] * heads
        + [jax.ShapeDtypeStruct((CHUNKS, SHORT_DEV, 2 * HD), bf16)] * blocks,
        in_specs=[pl.BlockSpec(memory_space=pltpu.SMEM)]
        + [anywhere] * (2 * heads + blocks)
        + [pl.BlockSpec(memory_space=pltpu.VMEM)],
        out_specs=[anywhere] * (heads + blocks),
        scratch_shapes=[
            pltpu.VMEM((heads, CHUNKS, SHORT_DEV, HD), bf16),
            pltpu.VMEM((NSHORT, blocks, SHORT_DEV, 2 * HD), bf16),
            pltpu.VMEM((NLONG, blocks, 2, SHORT_DEV, 2 * HD), bf16),
            pltpu.VMEM((heads, CHUNKS, SHORT_DEV, HD), bf16),
            pltpu.VMEM((blocks * SHORT_DEV, 2 * HD), f32),
            pltpu.VMEM((2 * blocks * SHORT_DEV, 2 * HD), f32),
            pltpu.VMEM((NSHORT, blocks, SHORT_DEV, 2 * HD), bf16),
            pltpu.VMEM((NLONG, blocks, 2, SHORT_DEV, 2 * HD), bf16),
            pltpu.SemaphoreType.DMA((heads,)),
            pltpu.SemaphoreType.DMA((heads,)),
            pltpu.SemaphoreType.DMA((3 * blocks,)),
        ],
        compiler_params=pltpu.CompilerParams(vmem_limit_bytes=60 << 20),
        cost_estimate=pl.CostEstimate(
            flops=10**10, bytes_accessed=12 << 20, transcendentals=4 * 10**6
        ),
        name="attend_backward",
    )(scal, *query_slots, *own, *others, *grad_slots, logs)
    return (result[:heads], result[heads:])


def local(
    tokens,
    w_qkv,
    w_out,
    w_up,
    w_down,
    gain_attn,
    gain_ffn,
    w_router,
    head_quarters,
    ffn_quarters,
    router_targets,
    cotangent,
):
    rows = tokens.shape[0]
    seq_rank = lax.axis_index("seq")
    seq_count = lax.axis_size("seq")
    head_rank = lax.axis_index("heads")
    head_count = lax.axis_size("heads")
    head_width = w_out.shape[0]
    ffn_width = w_up.shape[1]
    heads = head_width // HD
    members = seq_count // heads
    place, member = seq_rank // members, seq_rank % members
    share = rows // head_count
    short_rows = NSHORT * SHORT_DEV

    def across(values, slot):
        pairs = [
            (h * members + m, (h ^ slot) * members + m)
            for h in range(heads)
            for m in range(members)
        ]
        return lax.ppermute(values, "seq", pairs)

    def among(values, step):
        pairs = [
            (h * members + (m + step) % members, h * members + m)
            for h in range(heads)
            for m in range(members)
        ]
        return lax.ppermute(values, "seq", pairs)

    def swap(values, slot):
        return flip(values, "heads", head_count, slot)

    def own_rows(values, slot):
        return lax.dynamic_slice_in_dim(values, (head_rank ^ slot) * share, share, 0)

    def scatter_heads(parts):
        return [parts[0]] + [
            swap(parts[slot].astype(bf16), slot).astype(f32) for slot in range(1, head_count)
        ]

    def gather_heads(values):
        return [values] + [swap(values, slot) for slot in range(1, head_count)]

    def in_order(slots, kind):
        full = jnp.zeros((rows,) + slots[0].shape[1:], kind)
        for slot in range(head_count):
            full = lax.dynamic_update_slice_in_dim(
                full, slots[slot].astype(kind), (head_rank ^ slot) * share, 0
            )
        return full

    full_up = lax.all_gather(w_up, "seq", axis=0, tiled=True)
    full_down = lax.all_gather(w_down, "seq", axis=1, tiled=True)

    column = jnp.arange(rows)
    is_short = column < short_rows
    offset = column - short_rows
    seq_id = jnp.where(is_short, column // SHORT_DEV, NSHORT + offset // (2 * SHORT_DEV))
    position = jnp.where(
        is_short,
        seq_rank * SHORT_DEV + column % SHORT_DEV,
        seq_rank * 2 * SHORT_DEV + offset % (2 * SHORT_DEV),
    )
    in_seq = seq_id[:, None] == jnp.arange(SEQS)[None, :]
    seq_length = jnp.where(
        jnp.arange(SEQS) < NSHORT, SHORT_DEV * seq_count, 2 * SHORT_DEV * seq_count
    ).astype(f32)
    ffn_level = jnp.sum(jnp.where(in_seq, ffn_quarters[None, :], 0), axis=1)
    half_dim = HD // 2
    frequency = 10000.0 ** (-jnp.arange(half_dim, dtype=f32) * 2.0 / HD)
    angle = position.astype(f32)[:, None] * frequency[None, :]
    cosine = jnp.cos(angle)
    sine = jnp.sin(angle)
    my_head = head_rank * heads + place
    head_live = (my_head < head_quarters * (H // LEVELS)).astype(jnp.int32)
    scal = jnp.concatenate([jnp.stack([place, member]).astype(jnp.int32), head_live])

    tokens_wide = tokens.astype(f32)
    hat_one, _ = normalize_parts(tokens_wide)
    normed_one = hat_one * gain_attn
    normed_low = normed_one.astype(bf16)
    pool_short = jnp.sum(normed_one[:short_rows].reshape(NSHORT, SHORT_DEV, D), axis=1)
    pool_long = jnp.sum(normed_one[short_rows:].reshape(NLONG, 2 * SHORT_DEV, D), axis=1)
    flat_qkv = w_qkv.reshape(D, -1)
    projected = dot(normed_low, flat_qkv).reshape(rows, 3, head_width)

    def turn(values, back):
        former, latter = values[..., :half_dim], values[..., half_dim:]
        spin = -sine if back else sine
        return jnp.concatenate(
            [former * cosine - latter * spin, latter * cosine + former * spin], axis=-1
        )

    query_slots, pair_slots = [], []
    for slot in range(heads):
        start = (place ^ slot) * HD
        piece = lax.dynamic_slice_in_dim(projected, start, HD, 2)
        query = turn(piece[:, 0], False).astype(bf16)
        pair = jnp.concatenate([turn(piece[:, 1], False), piece[:, 2]], axis=1).astype(bf16)
        query = query.reshape(CHUNKS, SHORT_DEV, HD)
        pair = pair.reshape(CHUNKS, SHORT_DEV, 2 * HD)
        query_slots.append(across(query, slot) if slot else query)
        pair_slots.append(across(pair, slot) if slot else pair)
    other_slots = [
        among(pair_slots[slot], step) for step in range(1, members) for slot in range(heads)
    ]
    mixed_slots, logs = attend_forward(
        scal, query_slots, pair_slots, other_slots, heads, members
    )
    mixed_slots = [across(v, slot) if slot else v for slot, v in enumerate(mixed_slots)]
    mixed_slots = [v.reshape(rows, HD) for v in mixed_slots]
    heads_out = jnp.zeros((rows, head_width), bf16)
    for slot in range(heads):
        heads_out = lax.dynamic_update_slice_in_dim(
            heads_out, mixed_slots[slot], (place ^ slot) * HD, 1
        )

    pooled_sum = jnp.concatenate([pool_short, pool_long], axis=0)
    pooled = butterfly(pooled_sum, "seq", seq_count) * lax.rsqrt(seq_length)[:, None]

    heads_rel = [own_rows(heads_out, slot) for slot in range(head_count)]
    attn_parts = scatter_heads([dot(v, w_out) for v in heads_rel])
    tokens_own = own_rows(tokens, 0).astype(f32)
    hidden = tokens_own + sum(attn_parts[1:], attn_parts[0])
    hat_two, inverse_two = normalize_parts(hidden)
    normed_two = jnp.concatenate(gather_heads((hat_two * gain_ffn).astype(bf16)), axis=0)

    cotangent_rel = jnp.concatenate(
        [own_rows(cotangent, slot) for slot in range(head_count)], axis=0
    )
    level_rel = jnp.concatenate([own_rows(ffn_level, slot) for slot in range(head_count)])
    unit_index = head_rank * ffn_width + jnp.arange(ffn_width)
    ffn_live = (unit_index[None, :] < (level_rel * (FF // LEVELS))[:, None]).astype(f32)
    upward = dot(normed_two, full_up)
    kept = jnp.maximum(upward, 0.0)
    active = (jnp.square(kept) * ffn_live).astype(bf16)
    grad_active = contract(cotangent_rel, full_down, 1, 1).astype(bf16).astype(f32)
    grad_upward = (grad_active * ffn_live * 2.0 * kept).astype(bf16)
    two_parts = scatter_heads(
        [
            contract(grad_upward[slot * share : (slot + 1) * share], full_up, 1, 1)
            for slot in range(head_count)
        ]
    )
    ffn_parts = scatter_heads(
        [
            dot(active[slot * share : (slot + 1) * share], full_down)
            for slot in range(head_count)
        ]
    )
    grad_up_part = contract(normed_two, grad_upward, 0, 0).astype(bf16)
    grad_down_part = contract(active, cotangent_rel, 0, 0).astype(bf16)
    grad_up = lax.psum_scatter(grad_up_part, "seq", scatter_dimension=0, tiled=True).astype(f32)
    grad_down = lax.psum_scatter(
        grad_down_part, "seq", scatter_dimension=1, tiled=True
    ).astype(f32)

    grad_two = sum(two_parts[1:], two_parts[0])
    back_two, gain_two = normalize_back(grad_two, hat_two, inverse_two, gain_ffn)
    grad_hidden = own_rows(cotangent, 0).astype(f32) + back_two
    grad_attn = gather_heads(grad_hidden.astype(bf16))
    grad_heads = in_order([contract(v, w_out, 1, 1).astype(bf16) for v in grad_attn], bf16)
    grad_slots = []
    for slot in range(heads):
        piece = lax.dynamic_slice_in_dim(grad_heads, (place ^ slot) * HD, HD, 1)
        piece = piece.reshape(CHUNKS, SHORT_DEV, HD)
        grad_slots.append(across(piece, slot) if slot else piece)
    grad_out_part = contract(
        jnp.concatenate(heads_rel, axis=0), jnp.concatenate(grad_attn, axis=0), 0, 0
    ).astype(bf16)
    output_own = (hidden + sum(ffn_parts[1:], ffn_parts[0])).astype(bf16)
    output = in_order(gather_heads(output_own), bf16)

    grad_query_slots, grad_pair_slots = attend_backward(
        scal, query_slots, pair_slots, other_slots, grad_slots, logs, heads, members
    )
    grad_query_slots = [across(v, slot) if slot else v for slot, v in enumerate(grad_query_slots)]
    pair_sums = []
    for slot in range(heads):
        total = grad_pair_slots[slot].astype(f32)
        for step in range(1, members):
            sent = grad_pair_slots[step * heads + slot]
            total = total + among(sent, members - step).astype(f32)
        total = total.astype(bf16)
        pair_sums.append(across(total, slot) if slot else total)
    grad_projected = jnp.zeros((rows, 3, head_width), bf16)
    for slot in range(heads):
        start = (place ^ slot) * HD
        grad_query = turn(grad_query_slots[slot].reshape(rows, HD).astype(f32), True)
        pair = pair_sums[slot].reshape(rows, 2 * HD)
        grad_key = turn(pair[:, :HD].astype(f32), True)
        piece = jnp.stack([grad_query.astype(bf16), grad_key.astype(bf16), pair[:, HD:]], axis=1)
        grad_projected = lax.dynamic_update_slice_in_dim(grad_projected, piece, start, 2)
    grad_projected = grad_projected.reshape(rows, 3 * head_width)
    one_parts = scatter_heads(
        [contract(own_rows(grad_projected, slot), flat_qkv, 1, 1) for slot in range(head_count)]
    )
    grad_qkv_part = contract(normed_low, grad_projected, 0, 0).astype(bf16)

    logits = jnp.dot(pooled, w_router, precision=highest, preferred_element_type=f32)
    logit_grads = []
    for group in range(2):
        group_logits = logits[:, LEVELS * group : LEVELS * (group + 1)]
        raised = jnp.exp(group_logits - jnp.max(group_logits, axis=1, keepdims=True))
        chosen = (jnp.arange(LEVELS)[None, :] == router_targets[:, group][:, None]).astype(f32)
        logit_grads.append(raised / jnp.sum(raised, axis=1, keepdims=True) - chosen)
    grad_logits = jnp.concatenate(logit_grads, axis=1)
    grad_router = jnp.dot(pooled.T, grad_logits, precision=highest, preferred_element_type=f32)
    grad_pooled = (
        jnp.dot(grad_logits, w_router.T, precision=highest, preferred_element_type=f32)
        * lax.rsqrt(seq_length)[:, None]
    )

    member_own = own_rows(in_seq.astype(f32), 0)
    grad_one = sum(one_parts[1:], one_parts[0]) + jnp.dot(
        member_own, grad_pooled, precision=highest, preferred_element_type=f32
    )
    hat_own, inverse_own = normalize_parts(tokens_own)
    back_one, gain_one = normalize_back(grad_one, hat_own, inverse_own, gain_attn)
    grad_tokens = in_order(gather_heads((grad_hidden + back_one).astype(bf16)), f32)
    gains = jnp.stack([gain_one, gain_two])
    gains = butterfly(butterfly(gains, "heads", head_count), "seq", seq_count)
    grad_qkv = lax.psum(grad_qkv_part, "seq").astype(f32).reshape(D, 3, head_width)
    grad_out = lax.psum(grad_out_part, "seq").astype(f32)
    return (
        output,
        grad_tokens,
        grad_qkv,
        grad_out,
        grad_up,
        grad_down,
        gains[0],
        gains[1],
        grad_router,
    )


def solution(mesh):
    return jax.shard_map(
        local,
        mesh=mesh,
        in_specs=(
            P("seq", None),
            P(None, None, "heads"),
            P("heads", None),
            P("seq", "heads"),
            P("heads", "seq"),
            P(),
            P(),
            P(),
            P(),
            P(),
            P(),
            P("seq", None),
        ),
        out_specs=(
            P("seq", None),
            P("seq", None),
            P(None, None, "heads"),
            P("heads", None),
            P("seq", "heads"),
            P("heads", "seq"),
            P(),
            P(),
            P(),
        ),
        check_vma=False,
    )
```

```python
import functools

import jax
import jax.numpy as jnp
from jax import lax
from jax.experimental import pallas as pl
from jax.experimental.pallas import tpu as pltpu
from jax.sharding import PartitionSpec as P

D = 2048
H = 16
HD = 128
FF = 8192
SHORT_DEV = 128
NSHORT = 3
NLONG = 2
LEVELS = 4
SEQS = 5
CHUNKS = NSHORT + 2 * NLONG

epsilon = 1e-05
highest = lax.Precision.HIGHEST
f32 = jnp.float32
bf16 = jnp.bfloat16
SCALE = HD ** (-0.5)


def dot(left, right):
    return jnp.dot(left, right, preferred_element_type=f32)


def contract(left, right, left_dim, right_dim):
    return lax.dot_general(
        left, right, (((left_dim,), (right_dim,)), ((), ())), preferred_element_type=f32
    )


def normalize_parts(values):
    centered = values - jnp.mean(values, axis=-1, keepdims=True)
    inverse = lax.rsqrt(jnp.mean(centered * centered, axis=-1, keepdims=True) + epsilon)
    return (centered * inverse, inverse)


def normalize_back(grad_normed, normed_hat, inverse, gain):
    grad_hat = grad_normed * gain
    middle = (
        grad_hat
        - jnp.mean(grad_hat, axis=-1, keepdims=True)
        - normed_hat * jnp.mean(grad_hat * normed_hat, axis=-1, keepdims=True)
    )
    return (inverse * middle, jnp.sum(grad_normed * normed_hat, axis=0))


def flip(values, axis, size, bit):
    return lax.ppermute(values, axis, [(i, i ^ bit) for i in range(size)])


def butterfly(values, axis, size):
    bit = 1
    while bit < size:
        values = values + flip(values, axis, size, bit)
        bit *= 2
    return values


def key_copies(scal, own, others, keys_short, keys_long, sems, members, heads):
    head, member = scal[0], scal[1]
    copies = []
    for part in range(members):
        source = own if part == 0 else others[(part - 1) * heads : part * heads]
        whose = lax.rem(member + part, members)
        for slot in range(heads):
            block = (head ^ slot) * members + whose
            number = len(copies)
            copies.append(
                pltpu.make_async_copy(
                    source[slot].at[0:NSHORT], keys_short.at[:, block], sems.at[number]
                )
            )
            for index in range(NLONG):
                first = NSHORT + 2 * index
                number = len(copies)
                copies.append(
                    pltpu.make_async_copy(
                        source[slot].at[first : first + 2],
                        keys_long.at[index, block],
                        sems.at[number],
                    )
                )
    return copies


def row_copies(scal, slots, held, sems, heads, outward):
    head = scal[0]
    copies = []
    for slot in range(heads):
        ends = (slots[slot], held.at[head ^ slot])
        if outward:
            ends = ends[::-1]
        copies.append(pltpu.make_async_copy(ends[0], ends[1], sems.at[slot]))
    return copies


def sequence_loop(work):
    def short(index, carry):
        work(0, index, index, 1, index)
        return carry

    def long(index, carry):
        work(1, index, NSHORT + 2 * index, 2, NSHORT + index)
        return carry

    lax.fori_loop(0, NSHORT, short, 0)
    lax.fori_loop(0, NLONG, long, 0)


def allowed_mask(member, members, size):
    key_at = lax.broadcasted_iota(jnp.int32, (members * size, size), 0)
    query_at = lax.broadcasted_iota(jnp.int32, (members * size, size), 1) + member * size
    return key_at <= query_at


def attend_kernel(heads, members, scal, *refs):
    count = heads
    query_slots = refs[:count]
    own = refs[count : 2 * count]
    others = refs[2 * count : (1 + members) * count]
    rest = refs[(1 + members) * count :]
    out_slots = rest[:count]
    log_ref = rest[count]
    queries, keys_short, keys_long, mixed, row_sems, key_sems = rest[count + 1 :]
    copies = row_copies(scal, query_slots, queries, row_sems, heads, False)
    copies += key_copies(scal, own, others, keys_short, keys_long, key_sems, members, heads)
    for copy in copies:
        copy.start()
    for copy in copies:
        copy.wait()

    def work(kind, index, first, chunks, live_at):
        size = chunks * SHORT_DEV
        live = scal[2 + live_at].astype(f32)
        mask = allowed_mask(scal[1], members, size)
        for place in range(heads):
            span = (place + 1) * members
            if kind == 0:
                block = keys_short[index, 0:span]
            else:
                block = keys_long[index, 0:span]
            block = block.reshape(span * size, 2 * HD)
            keys, values = block[:, :HD], block[:, HD:]
            query = queries[place, pl.ds(first, chunks)].reshape(size, HD)
            scores = contract(keys, query, 1, 1) * SCALE
            edge = place * members * size
            last = jnp.where(mask, scores[edge:], -1e30)
            largest = jnp.max(last, axis=0, keepdims=True)
            if place:
                early = scores[:edge]
                largest = jnp.maximum(largest, jnp.max(early, axis=0, keepdims=True))
            raised = jnp.exp(last - largest)
            total = jnp.sum(raised, axis=0, keepdims=True)
            low = raised.astype(bf16)
            turned = contract(values[edge:], low, 0, 0)
            if place:
                raised = jnp.exp(early - largest)
                total = total + jnp.sum(raised, axis=0, keepdims=True)
                turned = turned + contract(values[:edge], raised.astype(bf16), 0, 0)
            turned = turned * (live / total)
            mixed[place, pl.ds(first, chunks)] = (
                turned.T.astype(bf16).reshape(chunks, SHORT_DEV, HD)
            )
            logs = largest + jnp.log(total)
            for chunk in range(chunks):
                log_ref[place, first + chunk] = logs[:, chunk * SHORT_DEV : (chunk + 1) * SHORT_DEV]

    sequence_loop(work)
    copies = row_copies(scal, out_slots, mixed, row_sems, heads, True)
    for copy in copies:
        copy.start()
    for copy in copies:
        copy.wait()


def attend_forward(scal, query_slots, own, others, heads, members):
    blocks = heads * members
    anywhere = pl.BlockSpec(memory_space=pl.ANY)
    result = pl.pallas_call(
        functools.partial(attend_kernel, heads, members),
        out_shape=[jax.ShapeDtypeStruct((CHUNKS, SHORT_DEV, HD), bf16)] * heads
        + [jax.ShapeDtypeStruct((heads, CHUNKS, 1, SHORT_DEV), f32)],
        in_specs=[pl.BlockSpec(memory_space=pltpu.SMEM)]
        + [anywhere] * (len(query_slots) + len(own) + len(others)),
        out_specs=[anywhere] * heads + [pl.BlockSpec(memory_space=pltpu.VMEM)],
        scratch_shapes=[
            pltpu.VMEM((heads, CHUNKS, SHORT_DEV, HD), bf16),
            pltpu.VMEM((NSHORT, blocks, SHORT_DEV, 2 * HD), bf16),
            pltpu.VMEM((NLONG, blocks, 2, SHORT_DEV, 2 * HD), bf16),
            pltpu.VMEM((heads, CHUNKS, SHORT_DEV, HD), bf16),
            pltpu.SemaphoreType.DMA((heads,)),
            pltpu.SemaphoreType.DMA((3 * blocks,)),
        ],
        compiler_params=pltpu.CompilerParams(vmem_limit_bytes=56 << 20),
        cost_estimate=pl.CostEstimate(
            flops=4 * 10**9, bytes_accessed=7 << 20, transcendentals=4 * 10**6
        ),
        name="attend_forward",
    )(scal, *query_slots, *own, *others)
    return (result[:heads], result[heads])


def back_kernel(heads, members, scal, *refs):
    count = heads
    query_slots = refs[:count]
    own = refs[count : 2 * count]
    others = refs[2 * count : (1 + members) * count]
    rest = refs[(1 + members) * count :]
    grad_slots = rest[:count]
    log_ref = rest[count]
    rest = rest[count + 1 :]
    query_out = rest[:count]
    pair_out = rest[count : (1 + members) * count]
    scratch = rest[(1 + members) * count :]
    queries, keys_short, keys_long, grads, sum_short, sum_long = scratch[:6]
    low_short, low_long, row_sems, grad_sems, key_sems = scratch[6:]
    copies = row_copies(scal, query_slots, queries, row_sems, heads, False)
    copies += row_copies(scal, grad_slots, grads, grad_sems, heads, False)
    copies += key_copies(scal, own, others, keys_short, keys_long, key_sems, members, heads)
    for copy in copies:
        copy.start()
    for copy in copies:
        copy.wait()

    def work(kind, index, first, chunks, live_at):
        size = chunks * SHORT_DEV
        live = scal[2 + live_at].astype(bf16)
        mask = allowed_mask(scal[1], members, size)
        if kind == 0:
            keys_ref, sum_ref, low_ref = keys_short, sum_short, low_short
        else:
            keys_ref, sum_ref, low_ref = keys_long, sum_long, low_long
        for place in reversed(range(heads)):
            span = (place + 1) * members
            block = keys_ref[index, 0:span].reshape(span * size, 2 * HD)
            keys, values = block[:, :HD], block[:, HD:]
            query = queries[place, pl.ds(first, chunks)].reshape(size, HD)
            grad = grads[place, pl.ds(first, chunks)].reshape(size, HD) * live
            logs = jnp.concatenate(
                [log_ref[place, first + chunk] for chunk in range(chunks)], axis=1
            )
            probs = jnp.exp(contract(keys, query, 1, 1) * SCALE - logs)
            edge = place * members * size
            last = jnp.where(mask, probs[edge:], 0.0)
            probs = jnp.concatenate([probs[:edge], last], axis=0) if place else last
            grad_probs = contract(values, grad, 1, 1)
            delta = jnp.sum(probs * grad_probs, axis=0, keepdims=True)
            grad_scores = (probs * (grad_probs - delta)).astype(bf16)
            grad_value = dot(probs.astype(bf16), grad)
            grad_key = dot(grad_scores, query) * SCALE
            turned = contract(keys, grad_scores, 0, 0) * SCALE
            queries[place, pl.ds(first, chunks)] = (
                turned.T.astype(bf16).reshape(chunks, SHORT_DEV, HD)
            )
            pair = jnp.concatenate([grad_key, grad_value], axis=1)
            if place == heads - 1:
                sum_ref[...] = pair
            else:
                sum_ref[0 : span * size] += pair
        low_ref[index] = sum_ref[...].astype(bf16).reshape(low_ref.shape[1:])

    sequence_loop(work)
    copies = row_copies(scal, query_out, queries, row_sems, heads, True)
    head, member = scal[0], scal[1]
    number = 0
    for part in range(members):
        whose = lax.rem(member + part, members)
        for slot in range(heads):
            block = (head ^ slot) * members + whose
            target = pair_out[part * heads + slot]
            copies.append(
                pltpu.make_async_copy(
                    low_short.at[:, block], target.at[0:NSHORT], key_sems.at[number]
                )
            )
            number += 1
            for index in range(NLONG):
                first = NSHORT + 2 * index
                copies.append(
                    pltpu.make_async_copy(
                        low_long.at[index, block],
                        target.at[first : first + 2],
                        key_sems.at[number],
                    )
                )
                number += 1
    for copy in copies:
        copy.start()
    for copy in copies:
        copy.wait()


def attend_backward(scal, query_slots, own, others, grad_slots, logs, heads, members):
    blocks = heads * members
    anywhere = pl.BlockSpec(memory_space=pl.ANY)
    result = pl.pallas_call(
        functools.partial(back_kernel, heads, members),
        out_shape=[jax.ShapeDtypeStruct((CHUNKS, SHORT_DEV, HD), bf16)] * heads
        + [jax.ShapeDtypeStruct((CHUNKS, SHORT_DEV, 2 * HD), bf16)] * blocks,
        in_specs=[pl.BlockSpec(memory_space=pltpu.SMEM)]
        + [anywhere] * (2 * heads + blocks)
        + [pl.BlockSpec(memory_space=pltpu.VMEM)],
        out_specs=[anywhere] * (heads + blocks),
        scratch_shapes=[
            pltpu.VMEM((heads, CHUNKS, SHORT_DEV, HD), bf16),
            pltpu.VMEM((NSHORT, blocks, SHORT_DEV, 2 * HD), bf16),
            pltpu.VMEM((NLONG, blocks, 2, SHORT_DEV, 2 * HD), bf16),
            pltpu.VMEM((heads, CHUNKS, SHORT_DEV, HD), bf16),
            pltpu.VMEM((blocks * SHORT_DEV, 2 * HD), f32),
            pltpu.VMEM((2 * blocks * SHORT_DEV, 2 * HD), f32),
            pltpu.VMEM((NSHORT, blocks, SHORT_DEV, 2 * HD), bf16),
            pltpu.VMEM((NLONG, blocks, 2, SHORT_DEV, 2 * HD), bf16),
            pltpu.SemaphoreType.DMA((heads,)),
            pltpu.SemaphoreType.DMA((heads,)),
            pltpu.SemaphoreType.DMA((3 * blocks,)),
        ],
        compiler_params=pltpu.CompilerParams(vmem_limit_bytes=60 << 20),
        cost_estimate=pl.CostEstimate(
            flops=10**10, bytes_accessed=12 << 20, transcendentals=4 * 10**6
        ),
        name="attend_backward",
    )(scal, *query_slots, *own, *others, *grad_slots, logs)
    return (result[:heads], result[heads:])


def rotate_rows(values, cosine, sine):
    return values * cosine + pltpu.roll(values, HD // 2, 1) * sine


def project_kernel(heads, scal, tokens, gain, cosine, sine, weights, *refs):
    query_slots, pair_slots = refs[:heads], refs[heads : 2 * heads]
    normed, pooled = refs[2 * heads : 2 * heads + 2]
    held_weights, acc, queries, pairs, in_sems, out_sems = refs[2 * heads + 2 :]
    head = scal[0]
    loads = [
        pltpu.make_async_copy(weights.at[part], held_weights.at[part], in_sems.at[part])
        for part in range(3)
    ]
    for load in loads:
        load.start()
    pooled[...] = jnp.zeros(pooled.shape, f32)

    def norm(chunk, carry):
        here = pl.ds(pl.multiple_of(chunk * SHORT_DEV, SHORT_DEV), SHORT_DEV)
        hat, _ = normalize_parts(tokens[here, :].astype(f32))
        values = hat * gain[...]
        normed[here, :] = values.astype(bf16)
        at = jnp.where(chunk < NSHORT, chunk, NSHORT + (chunk - NSHORT) // 2)
        rows = lax.broadcasted_iota(jnp.int32, pooled.shape, 0)
        added = jnp.sum(values, axis=0, keepdims=True)
        pooled[...] += jnp.where(rows == at, added, 0.0)
        return carry

    lax.fori_loop(0, CHUNKS, norm, 0)
    stores = []
    for part in range(3):
        loads[part].wait()
        acc[...] = dot(normed[...], held_weights[part])

        def spread(chunk, carry):
            here = pl.ds(pl.multiple_of(chunk * SHORT_DEV, SHORT_DEV), SHORT_DEV)
            for index in range(heads):
                values = acc[here, index * HD : (index + 1) * HD]
                if part < 2:
                    values = rotate_rows(values, cosine[here, :], sine[here, :])
                if part == 0:
                    queries[index, chunk] = values.astype(bf16)
                elif part == 1:
                    pairs[index, chunk, :, :HD] = values.astype(bf16)
                else:
                    pairs[index, chunk, :, HD:] = values.astype(bf16)
            return carry

        lax.fori_loop(0, CHUNKS, spread, 0)
        if part != 1:
            held, outs = (queries, query_slots) if part == 0 else (pairs, pair_slots)
            for slot in range(heads):
                copy = pltpu.make_async_copy(
                    held.at[head ^ slot], outs[slot], out_sems.at[len(stores)]
                )
                copy.start()
                stores.append(copy)
    for store in stores:
        store.wait()


def project(scal, tokens, gain, cosine, sine, weights):
    rows = tokens.shape[0]
    width = weights.shape[2]
    heads = width // HD
    anywhere = pl.BlockSpec(memory_space=pl.ANY)
    inside = pl.BlockSpec(memory_space=pltpu.VMEM)
    result = pl.pallas_call(
        functools.partial(project_kernel, heads),
        out_shape=[jax.ShapeDtypeStruct((CHUNKS, SHORT_DEV, HD), bf16)] * heads
        + [jax.ShapeDtypeStruct((CHUNKS, SHORT_DEV, 2 * HD), bf16)] * heads
        + [jax.ShapeDtypeStruct((rows, D), bf16), jax.ShapeDtypeStruct((8, D), f32)],
        in_specs=[pl.BlockSpec(memory_space=pltpu.SMEM)] + [inside] * 4 + [anywhere],
        out_specs=[anywhere] * (2 * heads) + [inside] * 2,
        scratch_shapes=[
            pltpu.VMEM((3, D, width), bf16),
            pltpu.VMEM((rows, width), f32),
            pltpu.VMEM((heads, CHUNKS, SHORT_DEV, HD), bf16),
            pltpu.VMEM((heads, CHUNKS, SHORT_DEV, 2 * HD), bf16),
            pltpu.SemaphoreType.DMA((3,)),
            pltpu.SemaphoreType.DMA((2 * heads,)),
        ],
        compiler_params=pltpu.CompilerParams(vmem_limit_bytes=50 << 20),
        cost_estimate=pl.CostEstimate(
            flops=6 * rows * D * width, bytes_accessed=16 << 20, transcendentals=rows
        ),
        name="project",
    )(scal, tokens, gain, cosine, sine, weights)
    return (result[:heads], result[heads : 2 * heads], result[2 * heads], result[2 * heads + 1])


def gather_kernel(heads, scal, cosine, sine, *refs):
    query_slots, pair_slots = refs[:heads], refs[heads : 2 * heads]
    out_query, out_key, out_value = refs[2 * heads : 2 * heads + 3]
    queries, pairs, sems = refs[2 * heads + 3 :]
    copies = []
    for held, slots in ((queries, query_slots), (pairs, pair_slots)):
        for slot in range(heads):
            copy = pltpu.make_async_copy(
                slots[slot], held.at[scal[0] ^ slot], sems.at[len(copies)]
            )
            copy.start()
            copies.append(copy)
    for copy in copies:
        copy.wait()

    def spread(chunk, carry):
        here = pl.ds(pl.multiple_of(chunk * SHORT_DEV, SHORT_DEV), SHORT_DEV)
        for index in range(heads):
            there = slice(index * HD, (index + 1) * HD)
            values = queries[index, chunk].astype(f32)
            values = rotate_rows(values, cosine[here, :], sine[here, :])
            out_query[here, there] = values.astype(bf16)
            values = pairs[index, chunk, :, :HD].astype(f32)
            values = rotate_rows(values, cosine[here, :], sine[here, :])
            out_key[here, there] = values.astype(bf16)
            out_value[here, there] = pairs[index, chunk, :, HD:]
        return carry

    lax.fori_loop(0, CHUNKS, spread, 0)


def gather_grads(scal, cosine, sine, query_slots, pair_slots):
    heads = len(query_slots)
    rows = CHUNKS * SHORT_DEV
    anywhere = pl.BlockSpec(memory_space=pl.ANY)
    inside = pl.BlockSpec(memory_space=pltpu.VMEM)
    return pl.pallas_call(
        functools.partial(gather_kernel, heads),
        out_shape=[jax.ShapeDtypeStruct((rows, heads * HD), bf16)] * 3,
        in_specs=[pl.BlockSpec(memory_space=pltpu.SMEM)]
        + [inside] * 2
        + [anywhere] * (2 * heads),
        out_specs=[inside] * 3,
        scratch_shapes=[
            pltpu.VMEM((heads, CHUNKS, SHORT_DEV, HD), bf16),
            pltpu.VMEM((heads, CHUNKS, SHORT_DEV, 2 * HD), bf16),
            pltpu.SemaphoreType.DMA((2 * heads,)),
        ],
        compiler_params=pltpu.CompilerParams(vmem_limit_bytes=24 << 20),
        cost_estimate=pl.CostEstimate(
            flops=10 * rows * heads * HD, bytes_accessed=6 << 20, transcendentals=0
        ),
        name="gather_grads",
    )(scal, cosine, sine, *query_slots, *pair_slots)


def local(
    tokens,
    w_qkv,
    w_out,
    w_up,
    w_down,
    gain_attn,
    gain_ffn,
    w_router,
    head_quarters,
    ffn_quarters,
    router_targets,
    cotangent,
):
    rows = tokens.shape[0]
    seq_rank = lax.axis_index("seq")
    seq_count = lax.axis_size("seq")
    head_rank = lax.axis_index("heads")
    head_count = lax.axis_size("heads")
    head_width = w_out.shape[0]
    ffn_width = w_up.shape[1]
    heads = head_width // HD
    members = seq_count // heads
    place, member = seq_rank // members, seq_rank % members
    share = rows // head_count
    short_rows = NSHORT * SHORT_DEV

    def across(values, slot):
        pairs = [
            (h * members + m, (h ^ slot) * members + m)
            for h in range(heads)
            for m in range(members)
        ]
        return lax.ppermute(values, "seq", pairs)

    def among(values, step):
        pairs = [
            (h * members + (m + step) % members, h * members + m)
            for h in range(heads)
            for m in range(members)
        ]
        return lax.ppermute(values, "seq", pairs)

    def swap(values, slot):
        return flip(values, "heads", head_count, slot)

    def own_rows(values, slot):
        return lax.dynamic_slice_in_dim(values, (head_rank ^ slot) * share, share, 0)

    def scatter_heads(parts):
        return [parts[0]] + [
            swap(parts[slot].astype(bf16), slot).astype(f32) for slot in range(1, head_count)
        ]

    def gather_heads(values):
        return [values] + [swap(values, slot) for slot in range(1, head_count)]

    def in_order(slots, kind):
        full = jnp.zeros((rows,) + slots[0].shape[1:], kind)
        for slot in range(head_count):
            full = lax.dynamic_update_slice_in_dim(
                full, slots[slot].astype(kind), (head_rank ^ slot) * share, 0
            )
        return full

    def placed(slots, key, axis):
        size = slots[0].shape[axis]
        shape = list(slots[0].shape)
        shape[axis] = size * len(slots)
        full = jnp.zeros(shape, slots[0].dtype)
        for slot, values in enumerate(slots):
            full = lax.dynamic_update_slice_in_dim(full, values, (key ^ slot) * size, axis)
        return full

    def after(values, *others):
        return lax.optimization_barrier((values,) + others)[0]

    full_down = lax.all_gather(w_down, "seq", axis=1, tiled=True)
    full_up = lax.all_gather(w_up, "seq", axis=0, tiled=True)
    all_out = jnp.concatenate(gather_heads(w_out), axis=0)

    column = jnp.arange(rows)
    is_short = column < short_rows
    offset = column - short_rows
    seq_id = jnp.where(is_short, column // SHORT_DEV, NSHORT + offset // (2 * SHORT_DEV))
    position = jnp.where(
        is_short,
        seq_rank * SHORT_DEV + column % SHORT_DEV,
        seq_rank * 2 * SHORT_DEV + offset % (2 * SHORT_DEV),
    )
    in_seq = seq_id[:, None] == jnp.arange(SEQS)[None, :]
    seq_length = jnp.where(
        jnp.arange(SEQS) < NSHORT, SHORT_DEV * seq_count, 2 * SHORT_DEV * seq_count
    ).astype(f32)
    ffn_level = jnp.sum(jnp.where(in_seq, ffn_quarters[None, :], 0), axis=1)
    half_dim = HD // 2
    frequency = 10000.0 ** (-jnp.arange(half_dim, dtype=f32) * 2.0 / HD)
    angle = position.astype(f32)[:, None] * frequency[None, :]
    cosine = jnp.cos(angle)
    sine = jnp.sin(angle)
    cosine = jnp.concatenate([cosine, cosine], axis=1)
    sine = jnp.concatenate([-sine, sine], axis=1)
    my_head = head_rank * heads + place
    head_live = (my_head < head_quarters * (H // LEVELS)).astype(jnp.int32)
    scal = jnp.concatenate([jnp.stack([place, member]).astype(jnp.int32), head_live])

    sent_queries, sent_pairs, normed_low, pooled_sum = project(
        scal, tokens, gain_attn[None, :], cosine, sine, w_qkv.transpose(1, 0, 2)
    )
    pooled_sum = pooled_sum[:SEQS]
    query_slots = [across(v, slot) if slot else v for slot, v in enumerate(sent_queries)]
    pair_slots = [across(v, slot) if slot else v for slot, v in enumerate(sent_pairs)]
    other_slots = [
        among(pair_slots[slot], step) for step in range(1, members) for slot in range(heads)
    ]
    pooled = butterfly(pooled_sum, "seq", seq_count) * lax.rsqrt(seq_length)[:, None]

    logits = jnp.dot(pooled, w_router, precision=highest, preferred_element_type=f32)
    logit_grads = []
    for group in range(2):
        group_logits = logits[:, LEVELS * group : LEVELS * (group + 1)]
        raised = jnp.exp(group_logits - jnp.max(group_logits, axis=1, keepdims=True))
        chosen = (jnp.arange(LEVELS)[None, :] == router_targets[:, group][:, None]).astype(f32)
        logit_grads.append(raised / jnp.sum(raised, axis=1, keepdims=True) - chosen)
    grad_logits = jnp.concatenate(logit_grads, axis=1)
    grad_router = jnp.dot(pooled.T, grad_logits, precision=highest, preferred_element_type=f32)
    grad_pooled = (
        jnp.dot(grad_logits, w_router.T, precision=highest, preferred_element_type=f32)
        * lax.rsqrt(seq_length)[:, None]
    )

    member_own = own_rows(in_seq.astype(f32), 0)
    grad_pooled_own = jnp.dot(
        member_own, grad_pooled, precision=highest, preferred_element_type=f32
    )
    tokens_own = own_rows(tokens, 0).astype(f32)
    hat_own, inverse_own = normalize_parts(tokens_own)

    mixed_slots, logs = attend_forward(
        scal, query_slots, pair_slots, other_slots, heads, members
    )
    mixed_slots = [across(v, slot) if slot else v for slot, v in enumerate(mixed_slots)]
    mixed_slots, grad_router, grad_pooled_own, hat_own, inverse_own = lax.optimization_barrier(
        (mixed_slots, grad_router, grad_pooled_own, hat_own, inverse_own)
    )
    mixed_slots = [v.reshape(rows, HD) for v in mixed_slots]
    heads_out = placed(mixed_slots, place, 1)

    heads_rel = [own_rows(heads_out, slot) for slot in range(head_count)]
    heads_own = jnp.concatenate(
        [heads_rel[0]] + [swap(heads_rel[slot], slot) for slot in range(1, head_count)], axis=1
    )
    hidden = tokens_own + dot(heads_own, all_out)
    hat_two, inverse_two = normalize_parts(hidden)
    normed_two = gather_heads((hat_two * gain_ffn).astype(bf16))

    cotangent_rel = jnp.concatenate(
        [own_rows(cotangent, slot) for slot in range(head_count)], axis=0
    )
    level_rel = jnp.concatenate([own_rows(ffn_level, slot) for slot in range(head_count)])
    unit_index = head_rank * ffn_width + jnp.arange(ffn_width)
    ffn_live = (unit_index[None, :] < (level_rel * (FF // LEVELS))[:, None]).astype(f32)
    grad_active = contract(cotangent_rel, full_down, 1, 1).astype(bf16)
    normed_two, grad_active = lax.optimization_barrier((normed_two, grad_active))
    normed_two = jnp.concatenate(normed_two, axis=0)
    upward = dot(normed_two, full_up)
    kept = jnp.maximum(upward, 0.0)
    active = (jnp.square(kept) * ffn_live).astype(bf16)
    grad_upward = (grad_active.astype(f32) * ffn_live * 2.0 * kept).astype(bf16)
    grad_down_part = contract(active, cotangent_rel, 0, 0).astype(bf16)
    grad_upward, grad_down_part = lax.optimization_barrier((grad_upward, grad_down_part))
    grad_down = lax.psum_scatter(
        grad_down_part, "seq", scatter_dimension=1, tiled=True
    ).astype(f32)
    two_parts = [
        contract(grad_upward[slot * share : (slot + 1) * share], full_up, 1, 1)
        for slot in range(head_count)
    ]
    two_parts = scatter_heads(two_parts)
    grad_up_part = contract(normed_two, grad_upward, 0, 0).astype(bf16)
    two_parts, grad_up_part = lax.optimization_barrier((two_parts, grad_up_part))
    grad_up = lax.psum_scatter(grad_up_part, "seq", scatter_dimension=0, tiled=True).astype(f32)

    grad_two = sum(two_parts[1:], two_parts[0])
    back_two, gain_two = normalize_back(grad_two, hat_two, inverse_two, gain_ffn)
    grad_hidden = own_rows(cotangent, 0).astype(f32) + back_two
    grad_attn_own = grad_hidden.astype(bf16)
    grad_mixed = contract(grad_attn_own, all_out, 1, 1).astype(bf16)
    grad_mixed = [
        grad_mixed[:, slot * head_width : (slot + 1) * head_width] for slot in range(head_count)
    ]
    grad_mixed = [grad_mixed[0]] + [
        swap(grad_mixed[slot], slot) for slot in range(1, head_count)
    ]
    grad_heads = placed(grad_mixed, head_rank, 0)
    grad_slots = []
    for slot in range(heads):
        piece = lax.dynamic_slice_in_dim(grad_heads, (place ^ slot) * HD, HD, 1)
        piece = piece.reshape(CHUNKS, SHORT_DEV, HD)
        grad_slots.append(across(piece, slot) if slot else piece)
    grad_attn = gather_heads(after(grad_attn_own, grad_heads))
    grad_attn = jnp.concatenate(grad_attn, axis=0)
    grad_out_part = contract(jnp.concatenate(heads_rel, axis=0), grad_attn, 0, 0).astype(bf16)
    ffn_parts = [
        dot(active[slot * share : (slot + 1) * share], full_down) for slot in range(head_count)
    ]
    ffn_parts = [ffn_parts[0]] + [v.astype(bf16) for v in ffn_parts[1:]]
    grad_slots, ffn_parts = lax.optimization_barrier((grad_slots, ffn_parts))

    grad_query_slots, grad_pair_slots = attend_backward(
        scal, query_slots, pair_slots, other_slots, grad_slots, logs, heads, members
    )
    grad_query_slots = [across(v, slot) if slot else v for slot, v in enumerate(grad_query_slots)]
    pair_sums = []
    for slot in range(heads):
        total = grad_pair_slots[slot].astype(f32)
        for step in range(1, members):
            sent = grad_pair_slots[step * heads + slot]
            total = total + among(sent, members - step).astype(f32)
        total = total.astype(bf16)
        pair_sums.append(across(total, slot) if slot else total)
    grad_query_slots, pair_sums, grad_out_part = lax.optimization_barrier(
        (grad_query_slots, pair_sums, grad_out_part)
    )
    grad_projected = gather_grads(scal, cosine, -sine, grad_query_slots, pair_sums)
    one_parts = scatter_heads(
        [
            sum(
                contract(own_rows(grad_projected[part], slot), w_qkv[:, part], 1, 1)
                for part in range(3)
            )
            for slot in range(head_count)
        ]
    )
    grad_parts = [contract(normed_low, v, 0, 0).astype(bf16) for v in grad_projected]
    grad_parts = [after(v, grad_down, grad_up) for v in grad_parts + [grad_out_part]]
    grad_parts = [v.astype(f32) for v in lax.psum(grad_parts, "seq")]
    grad_qkv = jnp.stack(grad_parts[:3], axis=1)
    grad_out = grad_parts[3]
    ffn_parts = [ffn_parts[0]] + [
        swap(ffn_parts[slot], slot).astype(f32) for slot in range(1, head_count)
    ]
    output_own = (hidden + sum(ffn_parts[1:], ffn_parts[0])).astype(bf16)
    output = in_order(gather_heads(output_own), bf16)

    grad_one = sum(one_parts[1:], one_parts[0]) + grad_pooled_own
    back_one, gain_one = normalize_back(grad_one, hat_own, inverse_own, gain_attn)
    grad_tokens = in_order(gather_heads((grad_hidden + back_one).astype(bf16)), f32)
    gains = jnp.stack([gain_one, gain_two])
    gains = butterfly(butterfly(gains, "heads", head_count), "seq", seq_count)
    return (
        output,
        grad_tokens,
        grad_qkv,
        grad_out,
        grad_up,
        grad_down,
        gains[0],
        gains[1],
        grad_router,
    )


def solution(mesh):
    return jax.shard_map(
        local,
        mesh=mesh,
        in_specs=(
            P("seq", None),
            P(None, None, "heads"),
            P("heads", None),
            P("seq", "heads"),
            P("heads", "seq"),
            P(),
            P(),
            P(),
            P(),
            P(),
            P(),
            P("seq", None),
        ),
        out_specs=(
            P("seq", None),
            P("seq", None),
            P(None, None, "heads"),
            P("heads", None),
            P("seq", "heads"),
            P("heads", "seq"),
            P(),
            P(),
            P(),
        ),
        check_vma=False,
    )
```

```python
import functools

import jax
import jax.numpy as jnp
from jax import lax
from jax.experimental import pallas as pl
from jax.experimental.pallas import tpu as pltpu
from jax.sharding import PartitionSpec as P

D = 2048
H = 16
HD = 128
FF = 8192
SHORT_DEV = 128
NSHORT = 3
NLONG = 2
LEVELS = 4
SEQS = 5
CHUNKS = NSHORT + 2 * NLONG

epsilon = 1e-05
highest = lax.Precision.HIGHEST
f32 = jnp.float32
bf16 = jnp.bfloat16
SCALE = HD ** (-0.5)


def dot(left, right):
    return jnp.dot(left, right, preferred_element_type=f32)


def contract(left, right, left_dim, right_dim):
    return lax.dot_general(
        left, right, (((left_dim,), (right_dim,)), ((), ())), preferred_element_type=f32
    )


def normalize_parts(values):
    centered = values - jnp.mean(values, axis=-1, keepdims=True)
    inverse = lax.rsqrt(jnp.mean(centered * centered, axis=-1, keepdims=True) + epsilon)
    return (centered * inverse, inverse)


def normalize_back(grad_normed, normed_hat, inverse, gain):
    grad_hat = grad_normed * gain
    middle = (
        grad_hat
        - jnp.mean(grad_hat, axis=-1, keepdims=True)
        - normed_hat * jnp.mean(grad_hat * normed_hat, axis=-1, keepdims=True)
    )
    return (inverse * middle, jnp.sum(grad_normed * normed_hat, axis=0))


def flip(values, axis, size, bit):
    return lax.ppermute(values, axis, [(i, i ^ bit) for i in range(size)])


def butterfly(values, axis, size):
    bit = 1
    while bit < size:
        values = values + flip(values, axis, size, bit)
        bit *= 2
    return values


def key_copies(scal, own, others, keys_short, keys_long, sems, members, heads):
    head, member = scal[0], scal[1]
    copies = []
    for part in range(members):
        source = own if part == 0 else others[(part - 1) * heads : part * heads]
        whose = lax.rem(member + part, members)
        for slot in range(heads):
            block = (head ^ slot) * members + whose
            number = len(copies)
            copies.append(
                pltpu.make_async_copy(
                    source[slot].at[0:NSHORT, :, HD:], keys_short.at[:, block], sems.at[number]
                )
            )
            for index in range(NLONG):
                first = NSHORT + 2 * index
                number = len(copies)
                copies.append(
                    pltpu.make_async_copy(
                        source[slot].at[first : first + 2, :, HD:],
                        keys_long.at[index, block],
                        sems.at[number],
                    )
                )
    return copies


def row_copies(scal, slots, held, sems, heads, outward):
    head = scal[0]
    copies = []
    for slot in range(heads):
        ends = (slots[slot].at[:, :, 0:HD], held.at[head ^ slot])
        if outward:
            ends = ends[::-1]
        copies.append(pltpu.make_async_copy(ends[0], ends[1], sems.at[slot]))
    return copies


def sequence_loop(work):
    def short(index, carry):
        work(0, index, index, 1, index)
        return carry

    def long(index, carry):
        work(1, index, NSHORT + 2 * index, 2, NSHORT + index)
        return carry

    lax.fori_loop(0, NSHORT, short, 0)
    lax.fori_loop(0, NLONG, long, 0)


def allowed_mask(member, members, size):
    key_at = lax.broadcasted_iota(jnp.int32, (members * size, size), 0)
    query_at = lax.broadcasted_iota(jnp.int32, (members * size, size), 1) + member * size
    return key_at <= query_at


def attend_kernel(heads, members, scal, *refs):
    count = heads
    own = refs[:count]
    others = refs[count : members * count]
    rest = refs[members * count :]
    out_slots = rest[:count]
    log_ref = rest[count]
    queries, keys_short, keys_long, mixed, row_sems, key_sems = rest[count + 1 :]
    copies = row_copies(scal, own, queries, row_sems, heads, False)
    copies += key_copies(scal, own, others, keys_short, keys_long, key_sems, members, heads)
    for copy in copies:
        copy.start()
    for copy in copies:
        copy.wait()

    def work(kind, index, first, chunks, live_at):
        size = chunks * SHORT_DEV
        live = scal[2 + live_at].astype(f32)
        mask = allowed_mask(scal[1], members, size)
        for place in range(heads):
            span = (place + 1) * members
            if kind == 0:
                block = keys_short[index, 0:span]
            else:
                block = keys_long[index, 0:span]
            block = block.reshape(span * size, 2 * HD)
            keys, values = block[:, :HD], block[:, HD:]
            query = queries[place, pl.ds(first, chunks)].reshape(size, HD)
            scores = contract(keys, query, 1, 1) * SCALE
            edge = place * members * size
            last = jnp.where(mask, scores[edge:], -1e30)
            largest = jnp.max(last, axis=0, keepdims=True)
            if place:
                early = scores[:edge]
                largest = jnp.maximum(largest, jnp.max(early, axis=0, keepdims=True))
            raised = jnp.exp(last - largest)
            total = jnp.sum(raised, axis=0, keepdims=True)
            low = raised.astype(bf16)
            turned = contract(values[edge:], low, 0, 0)
            if place:
                raised = jnp.exp(early - largest)
                total = total + jnp.sum(raised, axis=0, keepdims=True)
                turned = turned + contract(values[:edge], raised.astype(bf16), 0, 0)
            turned = turned * (live / total)
            mixed[place, pl.ds(first, chunks)] = (
                turned.T.astype(bf16).reshape(chunks, SHORT_DEV, HD)
            )
            logs = largest + jnp.log(total)
            for chunk in range(chunks):
                log_ref[place, first + chunk] = logs[:, chunk * SHORT_DEV : (chunk + 1) * SHORT_DEV]

    sequence_loop(work)
    copies = row_copies(scal, out_slots, mixed, row_sems, heads, True)
    for copy in copies:
        copy.start()
    for copy in copies:
        copy.wait()


def attend_forward(scal, own, others, heads, members):
    blocks = heads * members
    anywhere = pl.BlockSpec(memory_space=pl.ANY)
    result = pl.pallas_call(
        functools.partial(attend_kernel, heads, members),
        out_shape=[jax.ShapeDtypeStruct((CHUNKS, SHORT_DEV, HD), bf16)] * heads
        + [jax.ShapeDtypeStruct((heads, CHUNKS, 1, SHORT_DEV), f32)],
        in_specs=[pl.BlockSpec(memory_space=pltpu.SMEM)]
        + [anywhere] * (len(own) + len(others)),
        out_specs=[anywhere] * heads + [pl.BlockSpec(memory_space=pltpu.VMEM)],
        scratch_shapes=[
            pltpu.VMEM((heads, CHUNKS, SHORT_DEV, HD), bf16),
            pltpu.VMEM((NSHORT, blocks, SHORT_DEV, 2 * HD), bf16),
            pltpu.VMEM((NLONG, blocks, 2, SHORT_DEV, 2 * HD), bf16),
            pltpu.VMEM((heads, CHUNKS, SHORT_DEV, HD), bf16),
            pltpu.SemaphoreType.DMA((heads,)),
            pltpu.SemaphoreType.DMA((3 * blocks,)),
        ],
        compiler_params=pltpu.CompilerParams(vmem_limit_bytes=56 << 20),
        cost_estimate=pl.CostEstimate(
            flops=4 * 10**9, bytes_accessed=7 << 20, transcendentals=4 * 10**6
        ),
        name="attend_forward",
    )(scal, *own, *others)
    return (result[:heads], result[heads])


def back_kernel(heads, members, scal, *refs):
    count = heads
    own = refs[:count]
    others = refs[count : members * count]
    rest = refs[members * count :]
    grad_slots = rest[:count]
    log_ref = rest[count]
    rest = rest[count + 1 :]
    own_out = rest[:count]
    other_out = rest[count : count + members - 1]
    scratch = rest[count + members - 1 :]
    queries, keys_short, keys_long, grads, sum_short, sum_long = scratch[:6]
    low_short, low_long, zeros, row_sems, grad_sems, key_sems, zero_sems = scratch[6:]
    copies = row_copies(scal, own, queries, row_sems, heads, False)
    copies += row_copies(scal, grad_slots, grads, grad_sems, heads, False)
    copies += key_copies(scal, own, others, keys_short, keys_long, key_sems, members, heads)
    for copy in copies:
        copy.start()
    zeros[...] = jnp.zeros(zeros.shape, bf16)
    blanks = [
        pltpu.make_async_copy(
            zeros, other_out[part].at[slot, :, :, 0:HD], zero_sems.at[part * heads + slot]
        )
        for part in range(members - 1)
        for slot in range(heads)
    ]
    for copy in blanks:
        copy.start()
    for copy in copies:
        copy.wait()

    def work(kind, index, first, chunks, live_at):
        size = chunks * SHORT_DEV
        live = scal[2 + live_at].astype(bf16)
        mask = allowed_mask(scal[1], members, size)
        if kind == 0:
            keys_ref, sum_ref, low_ref = keys_short, sum_short, low_short
        else:
            keys_ref, sum_ref, low_ref = keys_long, sum_long, low_long
        for place in reversed(range(heads)):
            span = (place + 1) * members
            block = keys_ref[index, 0:span].reshape(span * size, 2 * HD)
            keys, values = block[:, :HD], block[:, HD:]
            query = queries[place, pl.ds(first, chunks)].reshape(size, HD)
            grad = grads[place, pl.ds(first, chunks)].reshape(size, HD) * live
            logs = jnp.concatenate(
                [log_ref[place, first + chunk] for chunk in range(chunks)], axis=1
            )
            probs = jnp.exp(contract(keys, query, 1, 1) * SCALE - logs)
            edge = place * members * size
            last = jnp.where(mask, probs[edge:], 0.0)
            probs = jnp.concatenate([probs[:edge], last], axis=0) if place else last
            grad_probs = contract(values, grad, 1, 1)
            delta = jnp.sum(probs * grad_probs, axis=0, keepdims=True)
            grad_scores = (probs * (grad_probs - delta)).astype(bf16)
            grad_value = dot(probs.astype(bf16), grad)
            grad_key = dot(grad_scores, query) * SCALE
            turned = contract(keys, grad_scores, 0, 0) * SCALE
            queries[place, pl.ds(first, chunks)] = (
                turned.T.astype(bf16).reshape(chunks, SHORT_DEV, HD)
            )
            pair = jnp.concatenate([grad_key, grad_value], axis=1)
            if place == heads - 1:
                sum_ref[...] = pair
            else:
                sum_ref[0 : span * size] += pair
        low_ref[index] = sum_ref[...].astype(bf16).reshape(low_ref.shape[1:])

    sequence_loop(work)
    copies = row_copies(scal, own_out, queries, row_sems, heads, True)
    head, member = scal[0], scal[1]
    number = 0
    for part in range(members):
        whose = lax.rem(member + part, members)
        for slot in range(heads):
            block = (head ^ slot) * members + whose
            target = own_out[slot] if part == 0 else other_out[part - 1].at[slot]
            copies.append(
                pltpu.make_async_copy(
                    low_short.at[:, block], target.at[0:NSHORT, :, HD:], key_sems.at[number]
                )
            )
            number += 1
            for index in range(NLONG):
                first = NSHORT + 2 * index
                copies.append(
                    pltpu.make_async_copy(
                        low_long.at[index, block],
                        target.at[first : first + 2, :, HD:],
                        key_sems.at[number],
                    )
                )
                number += 1
    for copy in copies:
        copy.start()
    for copy in blanks + copies:
        copy.wait()


def attend_backward(scal, own, others, grad_slots, logs, heads, members):
    blocks = heads * members
    anywhere = pl.BlockSpec(memory_space=pl.ANY)
    result = pl.pallas_call(
        functools.partial(back_kernel, heads, members),
        out_shape=[jax.ShapeDtypeStruct((CHUNKS, SHORT_DEV, 3 * HD), bf16)] * heads
        + [jax.ShapeDtypeStruct((heads, CHUNKS, SHORT_DEV, 3 * HD), bf16)] * (members - 1),
        in_specs=[pl.BlockSpec(memory_space=pltpu.SMEM)]
        + [anywhere] * (heads + blocks)
        + [pl.BlockSpec(memory_space=pltpu.VMEM)],
        out_specs=[anywhere] * (heads + members - 1),
        scratch_shapes=[
            pltpu.VMEM((heads, CHUNKS, SHORT_DEV, HD), bf16),
            pltpu.VMEM((NSHORT, blocks, SHORT_DEV, 2 * HD), bf16),
            pltpu.VMEM((NLONG, blocks, 2, SHORT_DEV, 2 * HD), bf16),
            pltpu.VMEM((heads, CHUNKS, SHORT_DEV, HD), bf16),
            pltpu.VMEM((blocks * SHORT_DEV, 2 * HD), f32),
            pltpu.VMEM((2 * blocks * SHORT_DEV, 2 * HD), f32),
            pltpu.VMEM((NSHORT, blocks, SHORT_DEV, 2 * HD), bf16),
            pltpu.VMEM((NLONG, blocks, 2, SHORT_DEV, 2 * HD), bf16),
            pltpu.VMEM((CHUNKS, SHORT_DEV, HD), bf16),
            pltpu.SemaphoreType.DMA((heads,)),
            pltpu.SemaphoreType.DMA((heads,)),
            pltpu.SemaphoreType.DMA((3 * blocks,)),
            pltpu.SemaphoreType.DMA(((members - 1) * heads,)),
        ],
        compiler_params=pltpu.CompilerParams(vmem_limit_bytes=60 << 20),
        cost_estimate=pl.CostEstimate(
            flops=10**10, bytes_accessed=12 << 20, transcendentals=4 * 10**6
        ),
        name="attend_backward",
    )(scal, *own, *others, *grad_slots, logs)
    return (result[:heads], result[heads:])


def rotate_rows(values, cosine, sine):
    return values * cosine + pltpu.roll(values, HD // 2, 1) * sine


def project_kernel(heads, scal, tokens, gain, cosine, sine, weights, *refs):
    slots = refs[:heads]
    normed, pooled = refs[heads : heads + 2]
    held_weights, acc, held, in_sems, out_sems = refs[heads + 2 :]
    head = scal[0]
    loads = [
        pltpu.make_async_copy(weights.at[part], held_weights.at[part], in_sems.at[part])
        for part in range(3)
    ]
    for load in loads:
        load.start()
    pooled[...] = jnp.zeros(pooled.shape, f32)

    def norm(chunk, carry):
        here = pl.ds(pl.multiple_of(chunk * SHORT_DEV, SHORT_DEV), SHORT_DEV)
        hat, _ = normalize_parts(tokens[here, :].astype(f32))
        values = hat * gain[...]
        normed[here, :] = values.astype(bf16)
        at = jnp.where(chunk < NSHORT, chunk, NSHORT + (chunk - NSHORT) // 2)
        rows = lax.broadcasted_iota(jnp.int32, pooled.shape, 0)
        added = jnp.sum(values, axis=0, keepdims=True)
        pooled[...] += jnp.where(rows == at, added, 0.0)
        return carry

    lax.fori_loop(0, CHUNKS, norm, 0)
    for part in range(3):
        loads[part].wait()
        acc[...] = dot(normed[...], held_weights[part])

        def spread(chunk, carry):
            here = pl.ds(pl.multiple_of(chunk * SHORT_DEV, SHORT_DEV), SHORT_DEV)
            for index in range(heads):
                values = acc[here, index * HD : (index + 1) * HD]
                if part < 2:
                    values = rotate_rows(values, cosine[here, :], sine[here, :])
                held[index, chunk, :, part * HD : (part + 1) * HD] = values.astype(bf16)
            return carry

        lax.fori_loop(0, CHUNKS, spread, 0)
    stores = [
        pltpu.make_async_copy(held.at[head ^ slot], slots[slot], out_sems.at[slot])
        for slot in range(heads)
    ]
    for store in stores:
        store.start()
    for store in stores:
        store.wait()


def project(scal, tokens, gain, cosine, sine, weights):
    rows = tokens.shape[0]
    width = weights.shape[2]
    heads = width // HD
    anywhere = pl.BlockSpec(memory_space=pl.ANY)
    inside = pl.BlockSpec(memory_space=pltpu.VMEM)
    result = pl.pallas_call(
        functools.partial(project_kernel, heads),
        out_shape=[jax.ShapeDtypeStruct((CHUNKS, SHORT_DEV, 3 * HD), bf16)] * heads
        + [jax.ShapeDtypeStruct((rows, D), bf16), jax.ShapeDtypeStruct((8, D), f32)],
        in_specs=[pl.BlockSpec(memory_space=pltpu.SMEM)] + [inside] * 4 + [anywhere],
        out_specs=[anywhere] * heads + [inside] * 2,
        scratch_shapes=[
            pltpu.VMEM((3, D, width), bf16),
            pltpu.VMEM((rows, width), f32),
            pltpu.VMEM((heads, CHUNKS, SHORT_DEV, 3 * HD), bf16),
            pltpu.SemaphoreType.DMA((3,)),
            pltpu.SemaphoreType.DMA((heads,)),
        ],
        compiler_params=pltpu.CompilerParams(vmem_limit_bytes=50 << 20),
        cost_estimate=pl.CostEstimate(
            flops=6 * rows * D * width, bytes_accessed=16 << 20, transcendentals=rows
        ),
        name="project",
    )(scal, tokens, gain, cosine, sine, weights)
    return (result[:heads], result[heads], result[heads + 1])


def gather_kernel(heads, scal, cosine, sine, *refs):
    slots = refs[:heads]
    out, held, sems = refs[heads:]
    copies = [
        pltpu.make_async_copy(slots[slot], held.at[scal[0] ^ slot], sems.at[slot])
        for slot in range(heads)
    ]
    for copy in copies:
        copy.start()
    for copy in copies:
        copy.wait()

    def spread(chunk, carry):
        here = pl.ds(pl.multiple_of(chunk * SHORT_DEV, SHORT_DEV), SHORT_DEV)
        for index in range(heads):
            for part in range(3):
                values = held[index, chunk, :, part * HD : (part + 1) * HD]
                if part < 2:
                    values = rotate_rows(values.astype(f32), cosine[here, :], sine[here, :])
                at = (part * heads + index) * HD
                out[here, at : at + HD] = values.astype(bf16)
        return carry

    lax.fori_loop(0, CHUNKS, spread, 0)


def gather_grads(scal, cosine, sine, slots):
    heads = len(slots)
    rows = CHUNKS * SHORT_DEV
    inside = pl.BlockSpec(memory_space=pltpu.VMEM)
    return pl.pallas_call(
        functools.partial(gather_kernel, heads),
        out_shape=jax.ShapeDtypeStruct((rows, 3 * heads * HD), bf16),
        in_specs=[pl.BlockSpec(memory_space=pltpu.SMEM)]
        + [inside] * 2
        + [pl.BlockSpec(memory_space=pl.ANY)] * heads,
        out_specs=inside,
        scratch_shapes=[
            pltpu.VMEM((heads, CHUNKS, SHORT_DEV, 3 * HD), bf16),
            pltpu.SemaphoreType.DMA((heads,)),
        ],
        compiler_params=pltpu.CompilerParams(vmem_limit_bytes=24 << 20),
        cost_estimate=pl.CostEstimate(
            flops=10 * rows * heads * HD, bytes_accessed=6 << 20, transcendentals=0
        ),
        name="gather_grads",
    )(scal, cosine, sine, *slots)


def local(
    tokens,
    w_qkv,
    w_out,
    w_up,
    w_down,
    gain_attn,
    gain_ffn,
    w_router,
    head_quarters,
    ffn_quarters,
    router_targets,
    cotangent,
):
    rows = tokens.shape[0]
    seq_rank = lax.axis_index("seq")
    seq_count = lax.axis_size("seq")
    head_rank = lax.axis_index("heads")
    head_count = lax.axis_size("heads")
    head_width = w_out.shape[0]
    ffn_width = w_up.shape[1]
    heads = head_width // HD
    members = seq_count // heads
    place, member = seq_rank // members, seq_rank % members
    share = rows // head_count
    short_rows = NSHORT * SHORT_DEV

    def across(values, slot):
        pairs = [
            (h * members + m, (h ^ slot) * members + m)
            for h in range(heads)
            for m in range(members)
        ]
        return lax.ppermute(values, "seq", pairs)

    def exchange(slots):
        sent = [across(slots[slot], slot) for slot in reversed(range(1, heads))]
        return [slots[0]] + sent[::-1]

    def among(values, step):
        pairs = [
            (h * members + (m + step) % members, h * members + m)
            for h in range(heads)
            for m in range(members)
        ]
        return lax.ppermute(values, "seq", pairs)

    def swap(values, slot):
        return flip(values, "heads", head_count, slot)

    def own_rows(values, slot):
        return lax.dynamic_slice_in_dim(values, (head_rank ^ slot) * share, share, 0)

    def scatter_heads(parts):
        return [parts[0]] + [
            swap(parts[slot].astype(bf16), slot) for slot in range(1, head_count)
        ]

    def gather_heads(values):
        return [values] + [swap(values, slot) for slot in range(1, head_count)]

    def gather_doubling(values):
        slots = [values]
        bit = 1
        while bit < head_count:
            slots = slots + [swap(v, bit) for v in slots]
            bit *= 2
        return slots

    def in_order(slots, kind):
        full = jnp.zeros((rows,) + slots[0].shape[1:], kind)
        for slot in range(head_count):
            full = lax.dynamic_update_slice_in_dim(
                full, slots[slot].astype(kind), (head_rank ^ slot) * share, 0
            )
        return full

    def placed(slots, key, axis):
        size = slots[0].shape[axis]
        shape = list(slots[0].shape)
        shape[axis] = size * len(slots)
        full = jnp.zeros(shape, slots[0].dtype)
        for slot, values in enumerate(slots):
            full = lax.dynamic_update_slice_in_dim(full, values, (key ^ slot) * size, axis)
        return full

    full_up = lax.all_gather(w_up, "seq", axis=0, tiled=True)
    full_out = lax.all_gather(w_out, "heads", axis=0, tiled=True)

    column = jnp.arange(rows)
    is_short = column < short_rows
    offset = column - short_rows
    seq_id = jnp.where(is_short, column // SHORT_DEV, NSHORT + offset // (2 * SHORT_DEV))
    position = jnp.where(
        is_short,
        seq_rank * SHORT_DEV + column % SHORT_DEV,
        seq_rank * 2 * SHORT_DEV + offset % (2 * SHORT_DEV),
    )
    in_seq = seq_id[:, None] == jnp.arange(SEQS)[None, :]
    seq_length = jnp.where(
        jnp.arange(SEQS) < NSHORT, SHORT_DEV * seq_count, 2 * SHORT_DEV * seq_count
    ).astype(f32)
    ffn_level = jnp.sum(jnp.where(in_seq, ffn_quarters[None, :], 0), axis=1)
    half_dim = HD // 2
    frequency = 10000.0 ** (-jnp.arange(half_dim, dtype=f32) * 2.0 / HD)
    angle = position.astype(f32)[:, None] * frequency[None, :]
    cosine = jnp.cos(angle)
    sine = jnp.sin(angle)
    cosine = jnp.concatenate([cosine, cosine], axis=1)
    sine = jnp.concatenate([-sine, sine], axis=1)
    my_head = head_rank * heads + place
    head_live = (my_head < head_quarters * (H // LEVELS)).astype(jnp.int32)
    scal = jnp.concatenate([jnp.stack([place, member]).astype(jnp.int32), head_live])

    slots, normed_low, pooled = project(
        scal, tokens, gain_attn[None, :], cosine, sine, w_qkv.transpose(1, 0, 2)
    )
    full_down = lax.all_gather(w_down, "seq", axis=1, tiled=True)
    slots = exchange(slots)
    other_slots = [among(v, step) for step in range(1, members) for v in slots]
    tokens_own = own_rows(tokens, 0).astype(f32)
    hat_own, inverse_own = normalize_parts(tokens_own)
    hops = []
    bit = 1
    while bit < seq_count:
        hops.append(bit)
        bit *= 2

    def hop(values, bits):
        for bit in bits:
            values = values + flip(values, "seq", seq_count, bit)
        return values

    pooled = hop(pooled[:SEQS], hops[:-2])
    slots, other_slots, hat_own, inverse_own, pooled = lax.optimization_barrier(
        (slots, other_slots, hat_own, inverse_own, pooled)
    )
    pooled = hop(pooled, hops[-2:-1])
    mixed_slots, logs = attend_forward(scal, slots, other_slots, heads, members)
    mixed_slots = [across(v, slot) if slot else v for slot, v in enumerate(mixed_slots)]
    mixed_slots, pooled = lax.optimization_barrier((mixed_slots, pooled))
    pooled = hop(pooled, hops[-1:])
    mixed_slots = [v.reshape(rows, HD) for v in mixed_slots]
    heads_out = placed(mixed_slots, place, 1)

    heads_rel = [own_rows(heads_out, slot) for slot in range(head_count)]
    heads_own = placed(
        [heads_rel[0]] + [swap(heads_rel[slot], slot) for slot in range(1, head_count)],
        head_rank,
        1,
    )
    hidden = tokens_own + dot(heads_own, full_out)
    hat_two, inverse_two = normalize_parts(hidden)
    normed_two = gather_heads((hat_two * gain_ffn).astype(bf16))

    cotangent_rel = jnp.concatenate(
        [own_rows(cotangent, slot) for slot in range(head_count)], axis=0
    )
    level_rel = jnp.concatenate([own_rows(ffn_level, slot) for slot in range(head_count)])
    unit_index = head_rank * ffn_width + jnp.arange(ffn_width)
    ffn_live = (unit_index[None, :] < (level_rel * (FF // LEVELS))[:, None]).astype(f32)
    normed_two, pooled = lax.optimization_barrier((normed_two, pooled))
    normed_two = jnp.concatenate(normed_two, axis=0)
    upward = dot(normed_two, full_up)
    kept = jnp.maximum(upward, 0.0)
    active = (jnp.square(kept) * ffn_live).astype(bf16)
    grad_down_part = contract(active, cotangent_rel, 0, 0).astype(bf16)
    cotangent_rel, kept, grad_down_part = lax.optimization_barrier(
        (cotangent_rel, kept, grad_down_part)
    )
    grad_active = contract(cotangent_rel, full_down, 1, 1).astype(bf16)
    grad_upward = (grad_active.astype(f32) * ffn_live * 2.0 * kept).astype(bf16)
    grad_down = lax.psum_scatter(grad_down_part, "seq", scatter_dimension=1, tiled=True)
    two_parts = [
        contract(grad_upward[slot * share : (slot + 1) * share], full_up, 1, 1)
        for slot in range(head_count)
    ]
    two_parts = scatter_heads(two_parts)
    grad_up_part = contract(normed_two, grad_upward, 0, 0).astype(bf16)

    pooled = pooled * lax.rsqrt(seq_length)[:, None]
    logits = jnp.dot(pooled, w_router, precision=highest, preferred_element_type=f32)
    logit_grads = []
    for group in range(2):
        group_logits = logits[:, LEVELS * group : LEVELS * (group + 1)]
        raised = jnp.exp(group_logits - jnp.max(group_logits, axis=1, keepdims=True))
        chosen = (jnp.arange(LEVELS)[None, :] == router_targets[:, group][:, None]).astype(f32)
        logit_grads.append(raised / jnp.sum(raised, axis=1, keepdims=True) - chosen)
    grad_logits = jnp.concatenate(logit_grads, axis=1)
    grad_router = jnp.dot(pooled.T, grad_logits, precision=highest, preferred_element_type=f32)
    grad_pooled = (
        jnp.dot(grad_logits, w_router.T, precision=highest, preferred_element_type=f32)
        * lax.rsqrt(seq_length)[:, None]
    )
    member_own = own_rows(in_seq.astype(f32), 0)
    grad_pooled_own = jnp.dot(
        member_own, grad_pooled, precision=highest, preferred_element_type=f32
    )
    two_parts, grad_up_part, grad_router, grad_pooled_own = lax.optimization_barrier(
        (two_parts, grad_up_part, grad_router, grad_pooled_own)
    )
    grad_up = lax.psum_scatter(grad_up_part, "seq", scatter_dimension=0, tiled=True)

    grad_two = sum([v.astype(f32) for v in two_parts[1:]], two_parts[0])
    back_two, gain_two = normalize_back(grad_two, hat_two, inverse_two, gain_ffn)
    grad_hidden = own_rows(cotangent, 0).astype(f32) + back_two
    grad_attn_own = grad_hidden.astype(bf16)
    grad_mixed = contract(grad_attn_own, full_out, 1, 1).astype(bf16)
    grad_mixed = [
        lax.dynamic_slice_in_dim(grad_mixed, (head_rank ^ slot) * head_width, head_width, 1)
        for slot in range(head_count)
    ]
    active, grad_mixed = lax.optimization_barrier((active, grad_mixed))
    grad_mixed = [grad_mixed[0]] + [
        swap(grad_mixed[slot], slot) for slot in range(1, head_count)
    ]
    grad_heads = placed(grad_mixed, head_rank, 0)
    grad_slots = []
    for slot in range(heads):
        piece = lax.dynamic_slice_in_dim(grad_heads, (place ^ slot) * HD, HD, 1)
        piece = piece.reshape(CHUNKS, SHORT_DEV, HD)
        grad_slots.append(across(piece, slot) if slot else piece)
    ffn_parts = [
        dot(active[slot * share : (slot + 1) * share], full_down) for slot in range(head_count)
    ]
    ffn_parts = scatter_heads(ffn_parts)

    own_grads, other_grads = attend_backward(
        scal, slots, other_slots, grad_slots, logs, heads, members
    )
    own_grads, other_grads, ffn_parts[:-1] = lax.optimization_barrier(
        (own_grads, other_grads, ffn_parts[:-1])
    )
    other_grads = [
        among(v, members - step) for step, v in zip(range(1, members), other_grads)
    ]
    sums = []
    for slot in range(heads):
        total = own_grads[slot].astype(f32)
        sums.append(sum([v[slot].astype(f32) for v in other_grads], total).astype(bf16))
    sums, grad_attn_own = lax.optimization_barrier((sums, grad_attn_own))
    sums = exchange(sums)
    grad_attn = gather_heads(grad_attn_own)
    grad_attn = jnp.concatenate(grad_attn, axis=0)
    grad_out_part = contract(jnp.concatenate(heads_rel, axis=0), grad_attn, 0, 0).astype(bf16)
    sums, grad_out_part = lax.optimization_barrier((sums, grad_out_part))
    grad_projected = gather_grads(scal, cosine, -sine, sums)
    grad_qkv_part = contract(normed_low, grad_projected, 0, 0).astype(bf16)
    grad_projected, grad_qkv_part, grad_out_part, grad_down, grad_up = lax.optimization_barrier(
        (grad_projected, grad_qkv_part, grad_out_part, grad_down, grad_up)
    )
    totals = [
        lax.psum_scatter(v, "seq", scatter_dimension=0, tiled=True)
        for v in (grad_qkv_part, grad_out_part)
    ]
    grad_down, grad_up = grad_down.astype(f32), grad_up.astype(f32)
    one_parts = scatter_heads(
        [
            sum(
                contract(
                    own_rows(grad_projected, slot)[:, part * head_width : (part + 1) * head_width],
                    w_qkv[:, part],
                    1,
                    1,
                )
                for part in range(3)
            )
            for slot in range(head_count)
        ]
    )
    one_parts, totals, ffn_parts = lax.optimization_barrier((one_parts, totals, ffn_parts))
    totals = [lax.all_gather(v, "seq", axis=0, tiled=True) for v in totals]
    grad_qkv = jnp.stack(
        [
            totals[0][:, part * head_width : (part + 1) * head_width].astype(f32)
            for part in range(3)
        ],
        axis=1,
    )
    grad_out = totals[1].astype(f32)
    output_own = (
        hidden + sum([v.astype(f32) for v in ffn_parts[1:]], ffn_parts[0])
    ).astype(bf16)
    output = in_order(gather_doubling(output_own), bf16)

    grad_one = sum([v.astype(f32) for v in one_parts[1:]], one_parts[0]) + grad_pooled_own
    back_one, gain_one = normalize_back(grad_one, hat_own, inverse_own, gain_attn)
    token_slots = gather_heads((grad_hidden + back_one).astype(bf16))
    token_slots, gains = lax.optimization_barrier(
        (token_slots, jnp.stack([gain_one, gain_two]))
    )
    grad_tokens = in_order(token_slots, f32)
    gains = butterfly(butterfly(gains, "heads", head_count), "seq", seq_count)
    return (
        output,
        grad_tokens,
        grad_qkv,
        grad_out,
        grad_up,
        grad_down,
        gains[0],
        gains[1],
        grad_router,
    )


def solution(mesh):
    return jax.shard_map(
        local,
        mesh=mesh,
        in_specs=(
            P("seq", None),
            P(None, None, "heads"),
            P("heads", None),
            P("seq", "heads"),
            P("heads", "seq"),
            P(),
            P(),
            P(),
            P(),
            P(),
            P(),
            P("seq", None),
        ),
        out_specs=(
            P("seq", None),
            P("seq", None),
            P(None, None, "heads"),
            P("heads", None),
            P("seq", "heads"),
            P("heads", "seq"),
            P(),
            P(),
            P(),
        ),
        check_vma=False,
    )
```

```python
import functools

import jax
import jax.numpy as jnp
from jax import lax
from jax.experimental import pallas as pl
from jax.experimental.pallas import tpu as pltpu
from jax.sharding import PartitionSpec as P

D = 2048
H = 16
HD = 128
FF = 8192
SHORT_DEV = 128
NSHORT = 3
NLONG = 2
LEVELS = 4
SEQS = 5
CHUNKS = NSHORT + 2 * NLONG

epsilon = 1e-05
highest = lax.Precision.HIGHEST
f32 = jnp.float32
bf16 = jnp.bfloat16
SCALE = HD ** (-0.5)


def dot(left, right):
    return jnp.dot(left, right, preferred_element_type=f32)


def contract(left, right, left_dim, right_dim):
    return lax.dot_general(
        left, right, (((left_dim,), (right_dim,)), ((), ())), preferred_element_type=f32
    )


def normalize_parts(values):
    centered = values - jnp.mean(values, axis=-1, keepdims=True)
    inverse = lax.rsqrt(jnp.mean(centered * centered, axis=-1, keepdims=True) + epsilon)
    return (centered * inverse, inverse)


def normalize_back(grad_normed, normed_hat, inverse, gain):
    grad_hat = grad_normed * gain
    middle = (
        grad_hat
        - jnp.mean(grad_hat, axis=-1, keepdims=True)
        - normed_hat * jnp.mean(grad_hat * normed_hat, axis=-1, keepdims=True)
    )
    return (inverse * middle, jnp.sum(grad_normed * normed_hat, axis=0))


def flip(values, axis, size, bit):
    return lax.ppermute(values, axis, [(i, i ^ bit) for i in range(size)])


def butterfly(values, axis, size):
    bit = 1
    while bit < size:
        values = values + flip(values, axis, size, bit)
        bit *= 2
    return values


def key_copies(scal, own, others, keys_short, keys_long, sems, members, heads):
    head, member = scal[0], scal[1]
    copies = []
    for part in range(members):
        source = own if part == 0 else others[(part - 1) * heads : part * heads]
        whose = lax.rem(member + part, members)
        for slot in range(heads):
            block = (head ^ slot) * members + whose
            number = len(copies)
            copies.append(
                pltpu.make_async_copy(
                    source[slot].at[0:NSHORT, :, HD:], keys_short.at[:, block], sems.at[number]
                )
            )
            for index in range(NLONG):
                first = NSHORT + 2 * index
                number = len(copies)
                copies.append(
                    pltpu.make_async_copy(
                        source[slot].at[first : first + 2, :, HD:],
                        keys_long.at[index, block],
                        sems.at[number],
                    )
                )
    return copies


def row_copies(scal, slots, held, sems, heads, outward):
    head = scal[0]
    copies = []
    for slot in range(heads):
        ends = (slots[slot].at[:, :, 0:HD], held.at[head ^ slot])
        if outward:
            ends = ends[::-1]
        copies.append(pltpu.make_async_copy(ends[0], ends[1], sems.at[slot]))
    return copies


def sequence_loop(work):
    def short(index, carry):
        work(0, index, index, 1, index)
        return carry

    def long(index, carry):
        work(1, index, NSHORT + 2 * index, 2, NSHORT + index)
        return carry

    lax.fori_loop(0, NSHORT, short, 0)
    lax.fori_loop(0, NLONG, long, 0)


def allowed_mask(member, members, size):
    key_at = lax.broadcasted_iota(jnp.int32, (members * size, size), 0)
    query_at = lax.broadcasted_iota(jnp.int32, (members * size, size), 1) + member * size
    return key_at <= query_at


def attend_kernel(heads, members, scal, *refs):
    count = heads
    own = refs[:count]
    others = refs[count : members * count]
    rest = refs[members * count :]
    out_slots = rest[:count]
    log_ref = rest[count]
    queries, keys_short, keys_long, mixed, row_sems, key_sems = rest[count + 1 :]
    copies = row_copies(scal, own, queries, row_sems, heads, False)
    copies += key_copies(scal, own, others, keys_short, keys_long, key_sems, members, heads)
    for copy in copies:
        copy.start()
    for copy in copies:
        copy.wait()

    def work(kind, index, first, chunks, live_at):
        size = chunks * SHORT_DEV
        live = scal[2 + live_at].astype(f32)
        mask = allowed_mask(scal[1], members, size)
        for place in range(heads):
            span = (place + 1) * members
            if kind == 0:
                block = keys_short[index, 0:span]
            else:
                block = keys_long[index, 0:span]
            block = block.reshape(span * size, 2 * HD)
            keys, values = block[:, :HD], block[:, HD:]
            query = queries[place, pl.ds(first, chunks)].reshape(size, HD)
            scores = contract(keys, query, 1, 1) * SCALE
            edge = place * members * size
            last = jnp.where(mask, scores[edge:], -1e30)
            largest = jnp.max(last, axis=0, keepdims=True)
            if place:
                early = scores[:edge]
                largest = jnp.maximum(largest, jnp.max(early, axis=0, keepdims=True))
            raised = jnp.exp(last - largest)
            total = jnp.sum(raised, axis=0, keepdims=True)
            low = raised.astype(bf16)
            turned = contract(values[edge:], low, 0, 0)
            if place:
                raised = jnp.exp(early - largest)
                total = total + jnp.sum(raised, axis=0, keepdims=True)
                turned = turned + contract(values[:edge], raised.astype(bf16), 0, 0)
            turned = turned * (live / total)
            mixed[place, pl.ds(first, chunks)] = (
                turned.T.astype(bf16).reshape(chunks, SHORT_DEV, HD)
            )
            logs = largest + jnp.log(total)
            for chunk in range(chunks):
                log_ref[place, first + chunk] = logs[:, chunk * SHORT_DEV : (chunk + 1) * SHORT_DEV]

    sequence_loop(work)
    copies = row_copies(scal, out_slots, mixed, row_sems, heads, True)
    for copy in copies:
        copy.start()
    for copy in copies:
        copy.wait()


def attend_forward(scal, own, others, heads, members):
    blocks = heads * members
    anywhere = pl.BlockSpec(memory_space=pl.ANY)
    result = pl.pallas_call(
        functools.partial(attend_kernel, heads, members),
        out_shape=[jax.ShapeDtypeStruct((CHUNKS, SHORT_DEV, HD), bf16)] * heads
        + [jax.ShapeDtypeStruct((heads, CHUNKS, 1, SHORT_DEV), f32)],
        in_specs=[pl.BlockSpec(memory_space=pltpu.SMEM)]
        + [anywhere] * (len(own) + len(others)),
        out_specs=[anywhere] * heads + [pl.BlockSpec(memory_space=pltpu.VMEM)],
        scratch_shapes=[
            pltpu.VMEM((heads, CHUNKS, SHORT_DEV, HD), bf16),
            pltpu.VMEM((NSHORT, blocks, SHORT_DEV, 2 * HD), bf16),
            pltpu.VMEM((NLONG, blocks, 2, SHORT_DEV, 2 * HD), bf16),
            pltpu.VMEM((heads, CHUNKS, SHORT_DEV, HD), bf16),
            pltpu.SemaphoreType.DMA((heads,)),
            pltpu.SemaphoreType.DMA((3 * blocks,)),
        ],
        compiler_params=pltpu.CompilerParams(vmem_limit_bytes=56 << 20),
        cost_estimate=pl.CostEstimate(
            flops=4 * 10**9, bytes_accessed=7 << 20, transcendentals=4 * 10**6
        ),
        name="attend_forward",
    )(scal, *own, *others)
    return (result[:heads], result[heads])


def back_kernel(heads, members, scal, *refs):
    count = heads
    own = refs[:count]
    others = refs[count : members * count]
    rest = refs[members * count :]
    grad_slots = rest[:count]
    log_ref = rest[count]
    rest = rest[count + 1 :]
    own_out = rest[:count]
    other_out = rest[count : count + members - 1]
    scratch = rest[count + members - 1 :]
    queries, keys_short, keys_long, grads, sum_short, sum_long = scratch[:6]
    low_short, low_long, zeros, row_sems, grad_sems, key_sems, zero_sems = scratch[6:]
    copies = row_copies(scal, own, queries, row_sems, heads, False)
    copies += row_copies(scal, grad_slots, grads, grad_sems, heads, False)
    copies += key_copies(scal, own, others, keys_short, keys_long, key_sems, members, heads)
    for copy in copies:
        copy.start()
    zeros[...] = jnp.zeros(zeros.shape, bf16)
    blanks = [
        pltpu.make_async_copy(
            zeros, other_out[part].at[slot, :, :, 0:HD], zero_sems.at[part * heads + slot]
        )
        for part in range(members - 1)
        for slot in range(heads)
    ]
    for copy in blanks:
        copy.start()
    for copy in copies:
        copy.wait()

    def work(kind, index, first, chunks, live_at):
        size = chunks * SHORT_DEV
        live = scal[2 + live_at].astype(bf16)
        mask = allowed_mask(scal[1], members, size)
        if kind == 0:
            keys_ref, sum_ref, low_ref = keys_short, sum_short, low_short
        else:
            keys_ref, sum_ref, low_ref = keys_long, sum_long, low_long
        for place in reversed(range(heads)):
            span = (place + 1) * members
            block = keys_ref[index, 0:span].reshape(span * size, 2 * HD)
            keys, values = block[:, :HD], block[:, HD:]
            query = queries[place, pl.ds(first, chunks)].reshape(size, HD)
            grad = grads[place, pl.ds(first, chunks)].reshape(size, HD) * live
            logs = jnp.concatenate(
                [log_ref[place, first + chunk] for chunk in range(chunks)], axis=1
            )
            probs = jnp.exp(contract(keys, query, 1, 1) * SCALE - logs)
            edge = place * members * size
            last = jnp.where(mask, probs[edge:], 0.0)
            probs = jnp.concatenate([probs[:edge], last], axis=0) if place else last
            grad_probs = contract(values, grad, 1, 1)
            delta = jnp.sum(probs * grad_probs, axis=0, keepdims=True)
            grad_scores = (probs * (grad_probs - delta)).astype(bf16)
            grad_value = dot(probs.astype(bf16), grad)
            grad_key = dot(grad_scores, query) * SCALE
            turned = contract(keys, grad_scores, 0, 0) * SCALE
            queries[place, pl.ds(first, chunks)] = (
                turned.T.astype(bf16).reshape(chunks, SHORT_DEV, HD)
            )
            pair = jnp.concatenate([grad_key, grad_value], axis=1)
            if place == heads - 1:
                sum_ref[...] = pair
            else:
                sum_ref[0 : span * size] += pair
        low_ref[index] = sum_ref[...].astype(bf16).reshape(low_ref.shape[1:])

    sequence_loop(work)
    copies = row_copies(scal, own_out, queries, row_sems, heads, True)
    head, member = scal[0], scal[1]
    number = 0
    for part in range(members):
        whose = lax.rem(member + part, members)
        for slot in range(heads):
            block = (head ^ slot) * members + whose
            target = own_out[slot] if part == 0 else other_out[part - 1].at[slot]
            copies.append(
                pltpu.make_async_copy(
                    low_short.at[:, block], target.at[0:NSHORT, :, HD:], key_sems.at[number]
                )
            )
            number += 1
            for index in range(NLONG):
                first = NSHORT + 2 * index
                copies.append(
                    pltpu.make_async_copy(
                        low_long.at[index, block],
                        target.at[first : first + 2, :, HD:],
                        key_sems.at[number],
                    )
                )
                number += 1
    for copy in copies:
        copy.start()
    for copy in blanks + copies:
        copy.wait()


def attend_backward(scal, own, others, grad_slots, logs, heads, members):
    blocks = heads * members
    anywhere = pl.BlockSpec(memory_space=pl.ANY)
    result = pl.pallas_call(
        functools.partial(back_kernel, heads, members),
        out_shape=[jax.ShapeDtypeStruct((CHUNKS, SHORT_DEV, 3 * HD), bf16)] * heads
        + [jax.ShapeDtypeStruct((heads, CHUNKS, SHORT_DEV, 3 * HD), bf16)] * (members - 1),
        in_specs=[pl.BlockSpec(memory_space=pltpu.SMEM)]
        + [anywhere] * (heads + blocks)
        + [pl.BlockSpec(memory_space=pltpu.VMEM)],
        out_specs=[anywhere] * (heads + members - 1),
        scratch_shapes=[
            pltpu.VMEM((heads, CHUNKS, SHORT_DEV, HD), bf16),
            pltpu.VMEM((NSHORT, blocks, SHORT_DEV, 2 * HD), bf16),
            pltpu.VMEM((NLONG, blocks, 2, SHORT_DEV, 2 * HD), bf16),
            pltpu.VMEM((heads, CHUNKS, SHORT_DEV, HD), bf16),
            pltpu.VMEM((blocks * SHORT_DEV, 2 * HD), f32),
            pltpu.VMEM((2 * blocks * SHORT_DEV, 2 * HD), f32),
            pltpu.VMEM((NSHORT, blocks, SHORT_DEV, 2 * HD), bf16),
            pltpu.VMEM((NLONG, blocks, 2, SHORT_DEV, 2 * HD), bf16),
            pltpu.VMEM((CHUNKS, SHORT_DEV, HD), bf16),
            pltpu.SemaphoreType.DMA((heads,)),
            pltpu.SemaphoreType.DMA((heads,)),
            pltpu.SemaphoreType.DMA((3 * blocks,)),
            pltpu.SemaphoreType.DMA(((members - 1) * heads,)),
        ],
        compiler_params=pltpu.CompilerParams(vmem_limit_bytes=60 << 20),
        cost_estimate=pl.CostEstimate(
            flops=10**10, bytes_accessed=12 << 20, transcendentals=4 * 10**6
        ),
        name="attend_backward",
    )(scal, *own, *others, *grad_slots, logs)
    return (result[:heads], result[heads:])


def rotate_rows(values, cosine, sine):
    return values * cosine + pltpu.roll(values, HD // 2, 1) * sine


def project_kernel(heads, scal, tokens, gain, cosine, sine, weights, *refs):
    slots = refs[:heads]
    normed, pooled = refs[heads : heads + 2]
    held_weights, acc, held, in_sems, out_sems = refs[heads + 2 :]
    head = scal[0]
    loads = [
        pltpu.make_async_copy(weights.at[part], held_weights.at[part], in_sems.at[part])
        for part in range(3)
    ]
    for load in loads:
        load.start()
    pooled[...] = jnp.zeros(pooled.shape, f32)

    def norm(chunk, carry):
        here = pl.ds(pl.multiple_of(chunk * SHORT_DEV, SHORT_DEV), SHORT_DEV)
        hat, _ = normalize_parts(tokens[here, :].astype(f32))
        values = hat * gain[...]
        normed[here, :] = values.astype(bf16)
        at = jnp.where(chunk < NSHORT, chunk, NSHORT + (chunk - NSHORT) // 2)
        rows = lax.broadcasted_iota(jnp.int32, pooled.shape, 0)
        added = jnp.sum(values, axis=0, keepdims=True)
        pooled[...] += jnp.where(rows == at, added, 0.0)
        return carry

    lax.fori_loop(0, CHUNKS, norm, 0)
    for part in range(3):
        loads[part].wait()
        acc[...] = dot(normed[...], held_weights[part])

        def spread(chunk, carry):
            here = pl.ds(pl.multiple_of(chunk * SHORT_DEV, SHORT_DEV), SHORT_DEV)
            for index in range(heads):
                values = acc[here, index * HD : (index + 1) * HD]
                if part < 2:
                    values = rotate_rows(values, cosine[here, :], sine[here, :])
                held[index, chunk, :, part * HD : (part + 1) * HD] = values.astype(bf16)
            return carry

        lax.fori_loop(0, CHUNKS, spread, 0)
    stores = [
        pltpu.make_async_copy(held.at[head ^ slot], slots[slot], out_sems.at[slot])
        for slot in range(heads)
    ]
    for store in stores:
        store.start()
    for store in stores:
        store.wait()


def project(scal, tokens, gain, cosine, sine, weights):
    rows = tokens.shape[0]
    width = weights.shape[2]
    heads = width // HD
    anywhere = pl.BlockSpec(memory_space=pl.ANY)
    inside = pl.BlockSpec(memory_space=pltpu.VMEM)
    result = pl.pallas_call(
        functools.partial(project_kernel, heads),
        out_shape=[jax.ShapeDtypeStruct((CHUNKS, SHORT_DEV, 3 * HD), bf16)] * heads
        + [jax.ShapeDtypeStruct((rows, D), bf16), jax.ShapeDtypeStruct((8, D), f32)],
        in_specs=[pl.BlockSpec(memory_space=pltpu.SMEM)] + [inside] * 4 + [anywhere],
        out_specs=[anywhere] * heads + [inside] * 2,
        scratch_shapes=[
            pltpu.VMEM((3, D, width), bf16),
            pltpu.VMEM((rows, width), f32),
            pltpu.VMEM((heads, CHUNKS, SHORT_DEV, 3 * HD), bf16),
            pltpu.SemaphoreType.DMA((3,)),
            pltpu.SemaphoreType.DMA((heads,)),
        ],
        compiler_params=pltpu.CompilerParams(vmem_limit_bytes=50 << 20),
        cost_estimate=pl.CostEstimate(
            flops=6 * rows * D * width, bytes_accessed=16 << 20, transcendentals=rows
        ),
        name="project",
    )(scal, tokens, gain, cosine, sine, weights)
    return (result[:heads], result[heads], result[heads + 1])


def gather_kernel(heads, scal, cosine, sine, *refs):
    slots = refs[:heads]
    out, held, sems = refs[heads:]
    copies = [
        pltpu.make_async_copy(slots[slot], held.at[scal[0] ^ slot], sems.at[slot])
        for slot in range(heads)
    ]
    for copy in copies:
        copy.start()
    for copy in copies:
        copy.wait()

    def spread(chunk, carry):
        here = pl.ds(pl.multiple_of(chunk * SHORT_DEV, SHORT_DEV), SHORT_DEV)
        for index in range(heads):
            for part in range(3):
                values = held[index, chunk, :, part * HD : (part + 1) * HD]
                if part < 2:
                    values = rotate_rows(values.astype(f32), cosine[here, :], sine[here, :])
                at = (part * heads + index) * HD
                out[here, at : at + HD] = values.astype(bf16)
        return carry

    lax.fori_loop(0, CHUNKS, spread, 0)


def gather_grads(scal, cosine, sine, slots):
    heads = len(slots)
    rows = CHUNKS * SHORT_DEV
    inside = pl.BlockSpec(memory_space=pltpu.VMEM)
    return pl.pallas_call(
        functools.partial(gather_kernel, heads),
        out_shape=jax.ShapeDtypeStruct((rows, 3 * heads * HD), bf16),
        in_specs=[pl.BlockSpec(memory_space=pltpu.SMEM)]
        + [inside] * 2
        + [pl.BlockSpec(memory_space=pl.ANY)] * heads,
        out_specs=inside,
        scratch_shapes=[
            pltpu.VMEM((heads, CHUNKS, SHORT_DEV, 3 * HD), bf16),
            pltpu.SemaphoreType.DMA((heads,)),
        ],
        compiler_params=pltpu.CompilerParams(vmem_limit_bytes=24 << 20),
        cost_estimate=pl.CostEstimate(
            flops=10 * rows * heads * HD, bytes_accessed=6 << 20, transcendentals=0
        ),
        name="gather_grads",
    )(scal, cosine, sine, *slots)


def local(
    tokens,
    w_qkv,
    w_out,
    w_up,
    w_down,
    gain_attn,
    gain_ffn,
    w_router,
    head_quarters,
    ffn_quarters,
    router_targets,
    cotangent,
):
    rows = tokens.shape[0]
    seq_rank = lax.axis_index("seq")
    seq_count = lax.axis_size("seq")
    head_rank = lax.axis_index("heads")
    head_count = lax.axis_size("heads")
    head_width = w_out.shape[0]
    ffn_width = w_up.shape[1]
    heads = head_width // HD
    members = seq_count // heads
    place, member = seq_rank // members, seq_rank % members
    share = rows // head_count
    short_rows = NSHORT * SHORT_DEV

    def across(values, slot):
        pairs = [
            (h * members + m, (h ^ slot) * members + m)
            for h in range(heads)
            for m in range(members)
        ]
        return lax.ppermute(values, "seq", pairs)

    def exchange(slots):
        sent = [across(slots[slot], slot) for slot in reversed(range(1, heads))]
        return [slots[0]] + sent[::-1]

    def among(values, step):
        pairs = [
            (h * members + (m + step) % members, h * members + m)
            for h in range(heads)
            for m in range(members)
        ]
        return lax.ppermute(values, "seq", pairs)

    def swap(values, slot):
        return flip(values, "heads", head_count, slot)

    def own_rows(values, slot):
        return lax.dynamic_slice_in_dim(values, (head_rank ^ slot) * share, share, 0)

    def scatter_heads(parts):
        return [parts[0]] + [
            swap(parts[slot].astype(bf16), slot) for slot in range(1, head_count)
        ]

    def gather_heads(values):
        return [values] + [swap(values, slot) for slot in range(1, head_count)]

    def gather_doubling(values):
        slots = [values]
        bit = 1
        while bit < head_count:
            slots = slots + [swap(v, bit) for v in slots]
            bit *= 2
        return slots

    def in_order(slots, kind):
        full = jnp.zeros((rows,) + slots[0].shape[1:], kind)
        for slot in range(head_count):
            full = lax.dynamic_update_slice_in_dim(
                full, slots[slot].astype(kind), (head_rank ^ slot) * share, 0
            )
        return full

    def placed(slots, key, axis):
        size = slots[0].shape[axis]
        shape = list(slots[0].shape)
        shape[axis] = size * len(slots)
        full = jnp.zeros(shape, slots[0].dtype)
        for slot, values in enumerate(slots):
            full = lax.dynamic_update_slice_in_dim(full, values, (key ^ slot) * size, axis)
        return full

    full_up = lax.all_gather(w_up, "seq", axis=0, tiled=True)
    out_slots = gather_heads(w_out)

    column = jnp.arange(rows)
    is_short = column < short_rows
    offset = column - short_rows
    seq_id = jnp.where(is_short, column // SHORT_DEV, NSHORT + offset // (2 * SHORT_DEV))
    position = jnp.where(
        is_short,
        seq_rank * SHORT_DEV + column % SHORT_DEV,
        seq_rank * 2 * SHORT_DEV + offset % (2 * SHORT_DEV),
    )
    in_seq = seq_id[:, None] == jnp.arange(SEQS)[None, :]
    seq_length = jnp.where(
        jnp.arange(SEQS) < NSHORT, SHORT_DEV * seq_count, 2 * SHORT_DEV * seq_count
    ).astype(f32)
    ffn_level = jnp.sum(jnp.where(in_seq, ffn_quarters[None, :], 0), axis=1)
    half_dim = HD // 2
    frequency = 10000.0 ** (-jnp.arange(half_dim, dtype=f32) * 2.0 / HD)
    angle = position.astype(f32)[:, None] * frequency[None, :]
    cosine = jnp.cos(angle)
    sine = jnp.sin(angle)
    cosine = jnp.concatenate([cosine, cosine], axis=1)
    sine = jnp.concatenate([-sine, sine], axis=1)
    my_head = head_rank * heads + place
    head_live = (my_head < head_quarters * (H // LEVELS)).astype(jnp.int32)
    scal = jnp.concatenate([jnp.stack([place, member]).astype(jnp.int32), head_live])

    slots, normed_low, pooled = project(
        scal, tokens, gain_attn[None, :], cosine, sine, w_qkv.transpose(1, 0, 2)
    )
    full_down = lax.all_gather(w_down, "seq", axis=1, tiled=True)
    slots = exchange(slots)
    other_slots = [among(v, step) for step in range(1, members) for v in slots]
    tokens_own = own_rows(tokens, 0).astype(f32)
    hat_own, inverse_own = normalize_parts(tokens_own)
    hops = []
    bit = 1
    while bit < seq_count:
        hops.append(bit)
        bit *= 2

    def hop(values, bits):
        for bit in bits:
            values = values + flip(values, "seq", seq_count, bit)
        return values

    pooled = hop(pooled[:SEQS], hops[:-2])
    slots, other_slots, out_slots[:-1], hat_own, inverse_own, pooled = lax.optimization_barrier(
        (slots, other_slots, out_slots[:-1], hat_own, inverse_own, pooled)
    )
    full_out = jnp.concatenate(out_slots, axis=0)
    pooled = hop(pooled, hops[-2:-1])
    mixed_slots, logs = attend_forward(scal, slots, other_slots, heads, members)
    mixed_slots = [across(v, slot) if slot else v for slot, v in enumerate(mixed_slots)]
    mixed_slots, pooled = lax.optimization_barrier((mixed_slots, pooled))
    pooled = hop(pooled, hops[-1:])
    mixed_slots = [v.reshape(rows, HD) for v in mixed_slots]
    heads_out = placed(mixed_slots, place, 1)

    heads_rel = [own_rows(heads_out, slot) for slot in range(head_count)]
    heads_own = jnp.concatenate(
        [heads_rel[0]] + [swap(heads_rel[slot], slot) for slot in range(1, head_count)], axis=1
    )
    hidden = tokens_own + dot(heads_own, full_out)
    hat_two, inverse_two = normalize_parts(hidden)
    normed_two = gather_heads((hat_two * gain_ffn).astype(bf16))

    cotangent_rel = jnp.concatenate(
        [own_rows(cotangent, slot) for slot in range(head_count)], axis=0
    )
    level_rel = jnp.concatenate([own_rows(ffn_level, slot) for slot in range(head_count)])
    unit_index = head_rank * ffn_width + jnp.arange(ffn_width)
    ffn_live = (unit_index[None, :] < (level_rel * (FF // LEVELS))[:, None]).astype(f32)
    normed_two, pooled = lax.optimization_barrier((normed_two, pooled))
    normed_two = jnp.concatenate(normed_two, axis=0)
    upward = dot(normed_two, full_up)
    kept = jnp.maximum(upward, 0.0)
    active = (jnp.square(kept) * ffn_live).astype(bf16)
    grad_down_part = contract(active, cotangent_rel, 0, 0).astype(bf16)
    cotangent_rel, kept, grad_down_part = lax.optimization_barrier(
        (cotangent_rel, kept, grad_down_part)
    )
    grad_active = contract(cotangent_rel, full_down, 1, 1).astype(bf16)
    grad_upward = (grad_active.astype(f32) * ffn_live * 2.0 * kept).astype(bf16)
    grad_down = lax.psum_scatter(grad_down_part, "seq", scatter_dimension=1, tiled=True)
    two_parts = [
        contract(grad_upward[slot * share : (slot + 1) * share], full_up, 1, 1)
        for slot in range(head_count)
    ]
    two_parts = scatter_heads(two_parts)
    grad_up_part = contract(normed_two, grad_upward, 0, 0).astype(bf16)

    pooled = pooled * lax.rsqrt(seq_length)[:, None]
    logits = jnp.dot(pooled, w_router, precision=highest, preferred_element_type=f32)
    logit_grads = []
    for group in range(2):
        group_logits = logits[:, LEVELS * group : LEVELS * (group + 1)]
        raised = jnp.exp(group_logits - jnp.max(group_logits, axis=1, keepdims=True))
        chosen = (jnp.arange(LEVELS)[None, :] == router_targets[:, group][:, None]).astype(f32)
        logit_grads.append(raised / jnp.sum(raised, axis=1, keepdims=True) - chosen)
    grad_logits = jnp.concatenate(logit_grads, axis=1)
    grad_router = jnp.dot(pooled.T, grad_logits, precision=highest, preferred_element_type=f32)
    grad_pooled = (
        jnp.dot(grad_logits, w_router.T, precision=highest, preferred_element_type=f32)
        * lax.rsqrt(seq_length)[:, None]
    )
    member_own = own_rows(in_seq.astype(f32), 0)
    grad_pooled_own = jnp.dot(
        member_own, grad_pooled, precision=highest, preferred_element_type=f32
    )
    two_parts, grad_up_part, grad_router, grad_pooled_own = lax.optimization_barrier(
        (two_parts, grad_up_part, grad_router, grad_pooled_own)
    )
    grad_up = lax.psum_scatter(grad_up_part, "seq", scatter_dimension=0, tiled=True)

    grad_two = sum([v.astype(f32) for v in two_parts[1:]], two_parts[0])
    back_two, gain_two = normalize_back(grad_two, hat_two, inverse_two, gain_ffn)
    grad_hidden = own_rows(cotangent, 0).astype(f32) + back_two
    grad_attn_own = grad_hidden.astype(bf16)
    grad_mixed = contract(grad_attn_own, full_out, 1, 1).astype(bf16)
    grad_mixed = [
        grad_mixed[:, slot * head_width : (slot + 1) * head_width] for slot in range(head_count)
    ]
    active, grad_mixed = lax.optimization_barrier((active, grad_mixed))
    grad_mixed = [grad_mixed[0]] + [
        swap(grad_mixed[slot], slot) for slot in range(1, head_count)
    ]
    grad_heads = placed(grad_mixed, head_rank, 0)
    grad_heads, grad_attn_own = lax.optimization_barrier((grad_heads, grad_attn_own))
    grad_attn = gather_heads(grad_attn_own)
    grad_slots = []
    for slot in range(heads):
        piece = lax.dynamic_slice_in_dim(grad_heads, (place ^ slot) * HD, HD, 1)
        piece = piece.reshape(CHUNKS, SHORT_DEV, HD)
        grad_slots.append(across(piece, slot) if slot else piece)
    ffn_parts = [
        dot(active[slot * share : (slot + 1) * share], full_down) for slot in range(head_count)
    ]
    ffn_parts[1:] = [v.astype(bf16) for v in ffn_parts[1:]]
    grad_slots, ffn_parts = lax.optimization_barrier((grad_slots, ffn_parts))

    own_grads, other_grads = attend_backward(
        scal, slots, other_slots, grad_slots, logs, heads, members
    )
    own_grads, other_grads, grad_attn[:-1] = lax.optimization_barrier(
        (own_grads, other_grads, grad_attn[:-1])
    )
    other_grads = [
        among(v, members - step) for step, v in zip(range(1, members), other_grads)
    ]
    sums = []
    for slot in range(heads):
        total = own_grads[slot].astype(f32)
        sums.append(sum([v[slot].astype(f32) for v in other_grads], total).astype(bf16))
    sums, ffn_parts = lax.optimization_barrier((sums, ffn_parts))
    sums = exchange(sums)
    ffn_parts = scatter_heads(ffn_parts)
    grad_attn = jnp.concatenate(grad_attn, axis=0)
    grad_out_part = contract(jnp.concatenate(heads_rel, axis=0), grad_attn, 0, 0).astype(bf16)
    grad_out_part, grad_down, grad_up, sums, ffn_parts[:-1] = lax.optimization_barrier(
        (grad_out_part, grad_down, grad_up, sums, ffn_parts[:-1])
    )
    total_out = lax.psum_scatter(grad_out_part, "seq", scatter_dimension=0, tiled=True)
    grad_projected = gather_grads(scal, cosine, -sine, sums)
    grad_qkv_part = contract(normed_low, grad_projected, 0, 0).astype(bf16)
    grad_projected, grad_qkv_part, total_out, ffn_parts = lax.optimization_barrier(
        (grad_projected, grad_qkv_part, total_out, ffn_parts)
    )
    total_qkv = lax.psum_scatter(grad_qkv_part, "seq", scatter_dimension=0, tiled=True)
    grad_down, grad_up = grad_down.astype(f32), grad_up.astype(f32)
    one_parts = scatter_heads(
        [
            sum(
                contract(
                    own_rows(grad_projected, slot)[:, part * head_width : (part + 1) * head_width],
                    w_qkv[:, part],
                    1,
                    1,
                )
                for part in range(3)
            )
            for slot in range(head_count)
        ]
    )
    one_parts, total_qkv = lax.optimization_barrier((one_parts, total_qkv))
    totals = [lax.all_gather(v, "seq", axis=0, tiled=True) for v in (total_qkv, total_out)]
    grad_qkv = jnp.stack(
        [
            totals[0][:, part * head_width : (part + 1) * head_width].astype(f32)
            for part in range(3)
        ],
        axis=1,
    )
    grad_out = totals[1].astype(f32)
    output_own = (
        hidden + sum([v.astype(f32) for v in ffn_parts[1:]], ffn_parts[0])
    ).astype(bf16)
    output = in_order(gather_doubling(output_own), bf16)

    grad_one = sum([v.astype(f32) for v in one_parts[1:]], one_parts[0]) + grad_pooled_own
    back_one, gain_one = normalize_back(grad_one, hat_own, inverse_own, gain_attn)
    token_slots = gather_heads((grad_hidden + back_one).astype(bf16))
    token_slots, gains = lax.optimization_barrier(
        (token_slots, jnp.stack([gain_one, gain_two]))
    )
    grad_tokens = in_order(token_slots, f32)
    gains = butterfly(butterfly(gains, "heads", head_count), "seq", seq_count)
    return (
        output,
        grad_tokens,
        grad_qkv,
        grad_out,
        grad_up,
        grad_down,
        gains[0],
        gains[1],
        grad_router,
    )


def solution(mesh):
    return jax.shard_map(
        local,
        mesh=mesh,
        in_specs=(
            P("seq", None),
            P(None, None, "heads"),
            P("heads", None),
            P("seq", "heads"),
            P("heads", "seq"),
            P(),
            P(),
            P(),
            P(),
            P(),
            P(),
            P("seq", None),
        ),
        out_specs=(
            P("seq", None),
            P("seq", None),
            P(None, None, "heads"),
            P("heads", None),
            P("seq", "heads"),
            P("heads", "seq"),
            P(),
            P(),
            P(),
        ),
        check_vma=False,
    )
```

```python
import functools

import jax
import jax.numpy as jnp
from jax import lax
from jax.experimental import pallas as pl
from jax.experimental.pallas import tpu as pltpu
from jax.sharding import PartitionSpec as P

D = 2048
H = 16
HD = 128
FF = 8192
SHORT_DEV = 128
NSHORT = 3
NLONG = 2
LEVELS = 4
SEQS = 5
CHUNKS = NSHORT + 2 * NLONG

epsilon = 1e-05
highest = lax.Precision.HIGHEST
f32 = jnp.float32
bf16 = jnp.bfloat16
SCALE = HD ** (-0.5)


def dot(left, right):
    return jnp.dot(left, right, preferred_element_type=f32)


def contract(left, right, left_dim, right_dim):
    return lax.dot_general(
        left, right, (((left_dim,), (right_dim,)), ((), ())), preferred_element_type=f32
    )


def normalize_parts(values):
    centered = values - jnp.mean(values, axis=-1, keepdims=True)
    inverse = lax.rsqrt(jnp.mean(centered * centered, axis=-1, keepdims=True) + epsilon)
    return (centered * inverse, inverse)


def normalize_back(grad_normed, normed_hat, inverse, gain):
    grad_hat = grad_normed * gain
    middle = (
        grad_hat
        - jnp.mean(grad_hat, axis=-1, keepdims=True)
        - normed_hat * jnp.mean(grad_hat * normed_hat, axis=-1, keepdims=True)
    )
    return (inverse * middle, jnp.sum(grad_normed * normed_hat, axis=0))


def flip(values, axis, size, bit):
    return lax.ppermute(values, axis, [(i, i ^ bit) for i in range(size)])


def butterfly(values, axis, size):
    bit = 1
    while bit < size:
        values = values + flip(values, axis, size, bit)
        bit *= 2
    return values


def key_copies(scal, own, others, keys_short, keys_long, sems, members, heads):
    head, member = scal[0], scal[1]
    copies = []
    for part in range(members):
        source = own if part == 0 else others[(part - 1) * heads : part * heads]
        whose = lax.rem(member + part, members)
        for slot in range(heads):
            block = (head ^ slot) * members + whose
            number = len(copies)
            copies.append(
                pltpu.make_async_copy(
                    source[slot].at[0:NSHORT, :, HD:], keys_short.at[:, block], sems.at[number]
                )
            )
            for index in range(NLONG):
                first = NSHORT + 2 * index
                number = len(copies)
                copies.append(
                    pltpu.make_async_copy(
                        source[slot].at[first : first + 2, :, HD:],
                        keys_long.at[index, block],
                        sems.at[number],
                    )
                )
    return copies


def row_copies(scal, slots, held, sems, heads, outward):
    head = scal[0]
    copies = []
    for slot in range(heads):
        ends = (slots[slot].at[:, :, 0:HD], held.at[head ^ slot])
        if outward:
            ends = ends[::-1]
        copies.append(pltpu.make_async_copy(ends[0], ends[1], sems.at[slot]))
    return copies


def sequence_loop(work):
    def short(index, carry):
        work(0, index, index, 1, index)
        return carry

    def long(index, carry):
        work(1, index, NSHORT + 2 * index, 2, NSHORT + index)
        return carry

    lax.fori_loop(0, NSHORT, short, 0)
    lax.fori_loop(0, NLONG, long, 0)


def allowed_mask(member, members, size):
    key_at = lax.broadcasted_iota(jnp.int32, (members * size, size), 0)
    query_at = lax.broadcasted_iota(jnp.int32, (members * size, size), 1) + member * size
    return key_at <= query_at


def attend_kernel(heads, members, scal, *refs):
    count = heads
    own = refs[:count]
    others = refs[count : members * count]
    rest = refs[members * count :]
    out_slots = rest[:count]
    log_ref = rest[count]
    queries, keys_short, keys_long, mixed, row_sems, key_sems = rest[count + 1 :]
    copies = row_copies(scal, own, queries, row_sems, heads, False)
    copies += key_copies(scal, own, others, keys_short, keys_long, key_sems, members, heads)
    for copy in copies:
        copy.start()
    for copy in copies:
        copy.wait()

    def work(kind, index, first, chunks, live_at):
        size = chunks * SHORT_DEV
        live = scal[2 + live_at].astype(f32)
        mask = allowed_mask(scal[1], members, size)
        for place in range(heads):
            span = (place + 1) * members
            if kind == 0:
                block = keys_short[index, 0:span]
            else:
                block = keys_long[index, 0:span]
            block = block.reshape(span * size, 2 * HD)
            keys, values = block[:, :HD], block[:, HD:]
            query = queries[place, pl.ds(first, chunks)].reshape(size, HD)
            scores = contract(keys, query, 1, 1) * SCALE
            edge = place * members * size
            last = jnp.where(mask, scores[edge:], -1e30)
            largest = jnp.max(last, axis=0, keepdims=True)
            if place:
                early = scores[:edge]
                largest = jnp.maximum(largest, jnp.max(early, axis=0, keepdims=True))
            raised = jnp.exp(last - largest)
            total = jnp.sum(raised, axis=0, keepdims=True)
            low = raised.astype(bf16)
            turned = contract(values[edge:], low, 0, 0)
            if place:
                raised = jnp.exp(early - largest)
                total = total + jnp.sum(raised, axis=0, keepdims=True)
                turned = turned + contract(values[:edge], raised.astype(bf16), 0, 0)
            turned = turned * (live / total)
            mixed[place, pl.ds(first, chunks)] = (
                turned.T.astype(bf16).reshape(chunks, SHORT_DEV, HD)
            )
            logs = largest + jnp.log(total)
            for chunk in range(chunks):
                log_ref[place, first + chunk] = logs[:, chunk * SHORT_DEV : (chunk + 1) * SHORT_DEV]

    sequence_loop(work)
    copies = row_copies(scal, out_slots, mixed, row_sems, heads, True)
    for copy in copies:
        copy.start()
    for copy in copies:
        copy.wait()


def attend_forward(scal, own, others, heads, members):
    blocks = heads * members
    anywhere = pl.BlockSpec(memory_space=pl.ANY)
    result = pl.pallas_call(
        functools.partial(attend_kernel, heads, members),
        out_shape=[jax.ShapeDtypeStruct((CHUNKS, SHORT_DEV, HD), bf16)] * heads
        + [jax.ShapeDtypeStruct((heads, CHUNKS, 1, SHORT_DEV), f32)],
        in_specs=[pl.BlockSpec(memory_space=pltpu.SMEM)]
        + [anywhere] * (len(own) + len(others)),
        out_specs=[anywhere] * heads + [pl.BlockSpec(memory_space=pltpu.VMEM)],
        scratch_shapes=[
            pltpu.VMEM((heads, CHUNKS, SHORT_DEV, HD), bf16),
            pltpu.VMEM((NSHORT, blocks, SHORT_DEV, 2 * HD), bf16),
            pltpu.VMEM((NLONG, blocks, 2, SHORT_DEV, 2 * HD), bf16),
            pltpu.VMEM((heads, CHUNKS, SHORT_DEV, HD), bf16),
            pltpu.SemaphoreType.DMA((heads,)),
            pltpu.SemaphoreType.DMA((3 * blocks,)),
        ],
        compiler_params=pltpu.CompilerParams(vmem_limit_bytes=56 << 20),
        cost_estimate=pl.CostEstimate(
            flops=4 * 10**9, bytes_accessed=7 << 20, transcendentals=4 * 10**6
        ),
        name="attend_forward",
    )(scal, *own, *others)
    return (result[:heads], result[heads])


def back_kernel(heads, members, scal, *refs):
    count = heads
    own = refs[:count]
    others = refs[count : members * count]
    rest = refs[members * count :]
    grad_slots = rest[:count]
    log_ref = rest[count]
    rest = rest[count + 1 :]
    own_out = rest[:count]
    other_out = rest[count : count + members - 1]
    scratch = rest[count + members - 1 :]
    queries, keys_short, keys_long, grads, sum_short, sum_long = scratch[:6]
    low_short, low_long, zeros, row_sems, grad_sems, key_sems, zero_sems = scratch[6:]
    copies = row_copies(scal, own, queries, row_sems, heads, False)
    copies += row_copies(scal, grad_slots, grads, grad_sems, heads, False)
    copies += key_copies(scal, own, others, keys_short, keys_long, key_sems, members, heads)
    for copy in copies:
        copy.start()
    zeros[...] = jnp.zeros(zeros.shape, bf16)
    blanks = [
        pltpu.make_async_copy(
            zeros, other_out[part].at[slot, :, :, 0:HD], zero_sems.at[part * heads + slot]
        )
        for part in range(members - 1)
        for slot in range(heads)
    ]
    for copy in blanks:
        copy.start()
    for copy in copies:
        copy.wait()

    def work(kind, index, first, chunks, live_at):
        size = chunks * SHORT_DEV
        live = scal[2 + live_at].astype(bf16)
        mask = allowed_mask(scal[1], members, size)
        if kind == 0:
            keys_ref, sum_ref, low_ref = keys_short, sum_short, low_short
        else:
            keys_ref, sum_ref, low_ref = keys_long, sum_long, low_long
        for place in reversed(range(heads)):
            span = (place + 1) * members
            block = keys_ref[index, 0:span].reshape(span * size, 2 * HD)
            keys, values = block[:, :HD], block[:, HD:]
            query = queries[place, pl.ds(first, chunks)].reshape(size, HD)
            grad = grads[place, pl.ds(first, chunks)].reshape(size, HD) * live
            logs = jnp.concatenate(
                [log_ref[place, first + chunk] for chunk in range(chunks)], axis=1
            )
            probs = jnp.exp(contract(keys, query, 1, 1) * SCALE - logs)
            edge = place * members * size
            last = jnp.where(mask, probs[edge:], 0.0)
            probs = jnp.concatenate([probs[:edge], last], axis=0) if place else last
            grad_probs = contract(values, grad, 1, 1)
            delta = jnp.sum(probs * grad_probs, axis=0, keepdims=True)
            grad_scores = (probs * (grad_probs - delta)).astype(bf16)
            grad_value = dot(probs.astype(bf16), grad)
            grad_key = dot(grad_scores, query) * SCALE
            turned = contract(keys, grad_scores, 0, 0) * SCALE
            queries[place, pl.ds(first, chunks)] = (
                turned.T.astype(bf16).reshape(chunks, SHORT_DEV, HD)
            )
            pair = jnp.concatenate([grad_key, grad_value], axis=1)
            if place == heads - 1:
                sum_ref[...] = pair
            else:
                sum_ref[0 : span * size] += pair
        low_ref[index] = sum_ref[...].astype(bf16).reshape(low_ref.shape[1:])

    sequence_loop(work)
    copies = row_copies(scal, own_out, queries, row_sems, heads, True)
    head, member = scal[0], scal[1]
    number = 0
    for part in range(members):
        whose = lax.rem(member + part, members)
        for slot in range(heads):
            block = (head ^ slot) * members + whose
            target = own_out[slot] if part == 0 else other_out[part - 1].at[slot]
            copies.append(
                pltpu.make_async_copy(
                    low_short.at[:, block], target.at[0:NSHORT, :, HD:], key_sems.at[number]
                )
            )
            number += 1
            for index in range(NLONG):
                first = NSHORT + 2 * index
                copies.append(
                    pltpu.make_async_copy(
                        low_long.at[index, block],
                        target.at[first : first + 2, :, HD:],
                        key_sems.at[number],
                    )
                )
                number += 1
    for copy in copies:
        copy.start()
    for copy in blanks + copies:
        copy.wait()


def attend_backward(scal, own, others, grad_slots, logs, heads, members):
    blocks = heads * members
    anywhere = pl.BlockSpec(memory_space=pl.ANY)
    result = pl.pallas_call(
        functools.partial(back_kernel, heads, members),
        out_shape=[jax.ShapeDtypeStruct((CHUNKS, SHORT_DEV, 3 * HD), bf16)] * heads
        + [jax.ShapeDtypeStruct((heads, CHUNKS, SHORT_DEV, 3 * HD), bf16)] * (members - 1),
        in_specs=[pl.BlockSpec(memory_space=pltpu.SMEM)]
        + [anywhere] * (heads + blocks)
        + [pl.BlockSpec(memory_space=pltpu.VMEM)],
        out_specs=[anywhere] * (heads + members - 1),
        scratch_shapes=[
            pltpu.VMEM((heads, CHUNKS, SHORT_DEV, HD), bf16),
            pltpu.VMEM((NSHORT, blocks, SHORT_DEV, 2 * HD), bf16),
            pltpu.VMEM((NLONG, blocks, 2, SHORT_DEV, 2 * HD), bf16),
            pltpu.VMEM((heads, CHUNKS, SHORT_DEV, HD), bf16),
            pltpu.VMEM((blocks * SHORT_DEV, 2 * HD), f32),
            pltpu.VMEM((2 * blocks * SHORT_DEV, 2 * HD), f32),
            pltpu.VMEM((NSHORT, blocks, SHORT_DEV, 2 * HD), bf16),
            pltpu.VMEM((NLONG, blocks, 2, SHORT_DEV, 2 * HD), bf16),
            pltpu.VMEM((CHUNKS, SHORT_DEV, HD), bf16),
            pltpu.SemaphoreType.DMA((heads,)),
            pltpu.SemaphoreType.DMA((heads,)),
            pltpu.SemaphoreType.DMA((3 * blocks,)),
            pltpu.SemaphoreType.DMA(((members - 1) * heads,)),
        ],
        compiler_params=pltpu.CompilerParams(vmem_limit_bytes=60 << 20),
        cost_estimate=pl.CostEstimate(
            flops=10**10, bytes_accessed=12 << 20, transcendentals=4 * 10**6
        ),
        name="attend_backward",
    )(scal, *own, *others, *grad_slots, logs)
    return (result[:heads], result[heads:])


def rotate_rows(values, cosine, sine):
    return values * cosine + pltpu.roll(values, HD // 2, 1) * sine


def project_kernel(heads, scal, tokens, gain, cosine, sine, weights, *refs):
    slots = refs[:heads]
    normed, pooled = refs[heads : heads + 2]
    held_weights, acc, held, in_sems, out_sems = refs[heads + 2 :]
    head = scal[0]
    loads = [
        pltpu.make_async_copy(weights.at[part], held_weights.at[part], in_sems.at[part])
        for part in range(3)
    ]
    for load in loads:
        load.start()
    pooled[...] = jnp.zeros(pooled.shape, f32)

    def norm(chunk, carry):
        here = pl.ds(pl.multiple_of(chunk * SHORT_DEV, SHORT_DEV), SHORT_DEV)
        hat, _ = normalize_parts(tokens[here, :].astype(f32))
        values = hat * gain[...]
        normed[here, :] = values.astype(bf16)
        at = jnp.where(chunk < NSHORT, chunk, NSHORT + (chunk - NSHORT) // 2)
        rows = lax.broadcasted_iota(jnp.int32, pooled.shape, 0)
        added = jnp.sum(values, axis=0, keepdims=True)
        pooled[...] += jnp.where(rows == at, added, 0.0)
        return carry

    lax.fori_loop(0, CHUNKS, norm, 0)
    for part in range(3):
        loads[part].wait()
        acc[...] = dot(normed[...], held_weights[part])

        def spread(chunk, carry):
            here = pl.ds(pl.multiple_of(chunk * SHORT_DEV, SHORT_DEV), SHORT_DEV)
            for index in range(heads):
                values = acc[here, index * HD : (index + 1) * HD]
                if part < 2:
                    values = rotate_rows(values, cosine[here, :], sine[here, :])
                held[index, chunk, :, part * HD : (part + 1) * HD] = values.astype(bf16)
            return carry

        lax.fori_loop(0, CHUNKS, spread, 0)
    stores = [
        pltpu.make_async_copy(held.at[head ^ slot], slots[slot], out_sems.at[slot])
        for slot in range(heads)
    ]
    for store in stores:
        store.start()
    for store in stores:
        store.wait()


def project(scal, tokens, gain, cosine, sine, weights):
    rows = tokens.shape[0]
    width = weights.shape[2]
    heads = width // HD
    anywhere = pl.BlockSpec(memory_space=pl.ANY)
    inside = pl.BlockSpec(memory_space=pltpu.VMEM)
    result = pl.pallas_call(
        functools.partial(project_kernel, heads),
        out_shape=[jax.ShapeDtypeStruct((CHUNKS, SHORT_DEV, 3 * HD), bf16)] * heads
        + [jax.ShapeDtypeStruct((rows, D), bf16), jax.ShapeDtypeStruct((8, D), f32)],
        in_specs=[pl.BlockSpec(memory_space=pltpu.SMEM)] + [inside] * 4 + [anywhere],
        out_specs=[anywhere] * heads + [inside] * 2,
        scratch_shapes=[
            pltpu.VMEM((3, D, width), bf16),
            pltpu.VMEM((rows, width), f32),
            pltpu.VMEM((heads, CHUNKS, SHORT_DEV, 3 * HD), bf16),
            pltpu.SemaphoreType.DMA((3,)),
            pltpu.SemaphoreType.DMA((heads,)),
        ],
        compiler_params=pltpu.CompilerParams(vmem_limit_bytes=50 << 20),
        cost_estimate=pl.CostEstimate(
            flops=6 * rows * D * width, bytes_accessed=16 << 20, transcendentals=rows
        ),
        name="project",
    )(scal, tokens, gain, cosine, sine, weights)
    return (result[:heads], result[heads], result[heads + 1])


def gather_kernel(heads, scal, cosine, sine, *refs):
    slots = refs[:heads]
    out, held, sems = refs[heads:]
    copies = [
        pltpu.make_async_copy(slots[slot], held.at[scal[0] ^ slot], sems.at[slot])
        for slot in range(heads)
    ]
    for copy in copies:
        copy.start()
    for copy in copies:
        copy.wait()

    def spread(chunk, carry):
        here = pl.ds(pl.multiple_of(chunk * SHORT_DEV, SHORT_DEV), SHORT_DEV)
        for index in range(heads):
            for part in range(3):
                values = held[index, chunk, :, part * HD : (part + 1) * HD]
                if part < 2:
                    values = rotate_rows(values.astype(f32), cosine[here, :], sine[here, :])
                at = (part * heads + index) * HD
                out[here, at : at + HD] = values.astype(bf16)
        return carry

    lax.fori_loop(0, CHUNKS, spread, 0)


def gather_grads(scal, cosine, sine, slots):
    heads = len(slots)
    rows = CHUNKS * SHORT_DEV
    inside = pl.BlockSpec(memory_space=pltpu.VMEM)
    return pl.pallas_call(
        functools.partial(gather_kernel, heads),
        out_shape=jax.ShapeDtypeStruct((rows, 3 * heads * HD), bf16),
        in_specs=[pl.BlockSpec(memory_space=pltpu.SMEM)]
        + [inside] * 2
        + [pl.BlockSpec(memory_space=pl.ANY)] * heads,
        out_specs=inside,
        scratch_shapes=[
            pltpu.VMEM((heads, CHUNKS, SHORT_DEV, 3 * HD), bf16),
            pltpu.SemaphoreType.DMA((heads,)),
        ],
        compiler_params=pltpu.CompilerParams(vmem_limit_bytes=24 << 20),
        cost_estimate=pl.CostEstimate(
            flops=10 * rows * heads * HD, bytes_accessed=6 << 20, transcendentals=0
        ),
        name="gather_grads",
    )(scal, cosine, sine, *slots)


def local(
    tokens,
    w_qkv,
    w_out,
    w_up,
    w_down,
    gain_attn,
    gain_ffn,
    w_router,
    head_quarters,
    ffn_quarters,
    router_targets,
    cotangent,
):
    rows = tokens.shape[0]
    seq_rank = lax.axis_index("seq")
    seq_count = lax.axis_size("seq")
    head_rank = lax.axis_index("heads")
    head_count = lax.axis_size("heads")
    head_width = w_out.shape[0]
    ffn_width = w_up.shape[1]
    heads = head_width // HD
    members = seq_count // heads
    place, member = seq_rank // members, seq_rank % members
    share = rows // head_count
    short_rows = NSHORT * SHORT_DEV

    def across(values, slot):
        pairs = [
            (h * members + m, (h ^ slot) * members + m)
            for h in range(heads)
            for m in range(members)
        ]
        return lax.ppermute(values, "seq", pairs)

    def exchange(slots):
        sent = [across(slots[slot], slot) for slot in reversed(range(1, heads))]
        return [slots[0]] + sent[::-1]

    def among(values, step):
        pairs = [
            (h * members + (m + step) % members, h * members + m)
            for h in range(heads)
            for m in range(members)
        ]
        return lax.ppermute(values, "seq", pairs)

    def scatter_members(values):
        size = values.shape[0] // members

        def block(number):
            return lax.dynamic_slice_in_dim(values, number * size, size, 0)

        total = block(member).astype(f32)
        for step in range(1, members):
            sent = block((member + members - step) % members)
            total = total + among(sent, step).astype(f32)
        return total.astype(bf16)

    def scatter_places(values):
        size = values.shape[0] // heads
        pieces = [
            lax.dynamic_slice_in_dim(values, (place ^ slot) * size, size, 0) for slot in range(heads)
        ]
        pieces = [v.astype(f32) for v in exchange(pieces)]
        return sum(pieces[1:], pieces[0]).astype(bf16)

    def gather_seq(values):
        values = placed(exchange([values] * heads), place, 0)
        size = values.shape[0]
        full = jnp.zeros((size * members,) + values.shape[1:], values.dtype)
        for step in range(members):
            piece = among(values, step) if step else values
            at = (member + step) % members * size
            full = lax.dynamic_update_slice_in_dim(full, piece, at, 0)
        return full

    def swap(values, slot):
        return flip(values, "heads", head_count, slot)

    def own_rows(values, slot):
        return lax.dynamic_slice_in_dim(values, (head_rank ^ slot) * share, share, 0)

    def scatter_heads(parts):
        return [parts[0]] + [
            swap(parts[slot].astype(bf16), slot) for slot in range(1, head_count)
        ]

    def gather_heads(values):
        return [values] + [swap(values, slot) for slot in range(1, head_count)]

    def gather_doubling(values):
        slots = [values]
        bit = 1
        while bit < head_count:
            slots = slots + [swap(v, bit) for v in slots]
            bit *= 2
        return slots

    def in_order(slots, kind):
        full = jnp.zeros((rows,) + slots[0].shape[1:], kind)
        for slot in range(head_count):
            full = lax.dynamic_update_slice_in_dim(
                full, slots[slot].astype(kind), (head_rank ^ slot) * share, 0
            )
        return full

    def placed(slots, key, axis):
        size = slots[0].shape[axis]
        shape = list(slots[0].shape)
        shape[axis] = size * len(slots)
        full = jnp.zeros(shape, slots[0].dtype)
        for slot, values in enumerate(slots):
            full = lax.dynamic_update_slice_in_dim(full, values, (key ^ slot) * size, axis)
        return full

    out_slots = gather_heads(w_out)

    column = jnp.arange(rows)
    is_short = column < short_rows
    offset = column - short_rows
    seq_id = jnp.where(is_short, column // SHORT_DEV, NSHORT + offset // (2 * SHORT_DEV))
    position = jnp.where(
        is_short,
        seq_rank * SHORT_DEV + column % SHORT_DEV,
        seq_rank * 2 * SHORT_DEV + offset % (2 * SHORT_DEV),
    )
    in_seq = seq_id[:, None] == jnp.arange(SEQS)[None, :]
    seq_length = jnp.where(
        jnp.arange(SEQS) < NSHORT, SHORT_DEV * seq_count, 2 * SHORT_DEV * seq_count
    ).astype(f32)
    ffn_level = jnp.sum(jnp.where(in_seq, ffn_quarters[None, :], 0), axis=1)
    half_dim = HD // 2
    frequency = 10000.0 ** (-jnp.arange(half_dim, dtype=f32) * 2.0 / HD)
    angle = position.astype(f32)[:, None] * frequency[None, :]
    cosine = jnp.cos(angle)
    sine = jnp.sin(angle)
    cosine = jnp.concatenate([cosine, cosine], axis=1)
    sine = jnp.concatenate([-sine, sine], axis=1)
    my_head = head_rank * heads + place
    head_live = (my_head < head_quarters * (H // LEVELS)).astype(jnp.int32)
    scal = jnp.concatenate([jnp.stack([place, member]).astype(jnp.int32), head_live])

    slots, normed_low, pooled = project(
        scal, tokens, gain_attn[None, :], cosine, sine, w_qkv.transpose(1, 0, 2)
    )
    slots = exchange(slots)
    other_slots = [among(v, step) for step in range(1, members) for v in slots]
    slots, out_slots[:-1], own_up, own_down = lax.optimization_barrier(
        (slots, out_slots[:-1], w_up, w_down)
    )
    full_up = lax.all_gather(own_up, "seq", axis=0, tiled=True)
    full_down = lax.all_gather(own_down, "seq", axis=1, tiled=True)
    tokens_own = own_rows(tokens, 0).astype(f32)
    hat_own, inverse_own = normalize_parts(tokens_own)
    hops = []
    bit = 1
    while bit < seq_count:
        hops.append(bit)
        bit *= 2

    def hop(values, bits):
        for bit in bits:
            values = values + flip(values, "seq", seq_count, bit)
        return values

    pooled = hop(pooled[:SEQS], hops[:-2])
    slots, other_slots, hat_own, inverse_own, pooled = lax.optimization_barrier(
        (slots, other_slots, hat_own, inverse_own, pooled)
    )
    full_out = jnp.concatenate(out_slots, axis=0)
    pooled = hop(pooled, hops[-2:-1])
    mixed_slots, logs = attend_forward(scal, slots, other_slots, heads, members)
    mixed_slots = [across(v, slot) if slot else v for slot, v in enumerate(mixed_slots)]
    mixed_slots, pooled = lax.optimization_barrier((mixed_slots, pooled))
    pooled = hop(pooled, hops[-1:])
    mixed_slots = [v.reshape(rows, HD) for v in mixed_slots]
    heads_out = placed(mixed_slots, place, 1)

    heads_rel = [own_rows(heads_out, slot) for slot in range(head_count)]
    heads_own = jnp.concatenate(
        [heads_rel[0]] + [swap(heads_rel[slot], slot) for slot in range(1, head_count)], axis=1
    )
    hidden = tokens_own + dot(heads_own, full_out)
    hat_two, inverse_two = normalize_parts(hidden)
    normed_two = gather_heads((hat_two * gain_ffn).astype(bf16))

    cotangent_rel = jnp.concatenate(
        [own_rows(cotangent, slot) for slot in range(head_count)], axis=0
    )
    level_rel = jnp.concatenate([own_rows(ffn_level, slot) for slot in range(head_count)])
    unit_index = head_rank * ffn_width + jnp.arange(ffn_width)
    ffn_live = (unit_index[None, :] < (level_rel * (FF // LEVELS))[:, None]).astype(f32)
    normed_two, pooled = lax.optimization_barrier((normed_two, pooled))
    normed_two = jnp.concatenate(normed_two, axis=0)
    upward = dot(normed_two, full_up)
    kept = jnp.maximum(upward, 0.0)
    active = (jnp.square(kept) * ffn_live).astype(bf16)
    grad_down_part = contract(active, cotangent_rel, 0, 0).astype(bf16)
    cotangent_rel, kept, grad_down_part = lax.optimization_barrier(
        (cotangent_rel, kept, grad_down_part)
    )
    grad_active = contract(cotangent_rel, full_down, 1, 1).astype(bf16)
    grad_upward = (grad_active.astype(f32) * ffn_live * 2.0 * kept).astype(bf16)
    grad_down = lax.psum_scatter(grad_down_part, "seq", scatter_dimension=1, tiled=True)
    two_parts = [
        contract(grad_upward[slot * share : (slot + 1) * share], full_up, 1, 1)
        for slot in range(head_count)
    ]
    two_parts = scatter_heads(two_parts)
    grad_up_part = contract(normed_two, grad_upward, 0, 0).astype(bf16)

    pooled = pooled * lax.rsqrt(seq_length)[:, None]
    logits = jnp.dot(pooled, w_router, precision=highest, preferred_element_type=f32)
    logit_grads = []
    for group in range(2):
        group_logits = logits[:, LEVELS * group : LEVELS * (group + 1)]
        raised = jnp.exp(group_logits - jnp.max(group_logits, axis=1, keepdims=True))
        chosen = (jnp.arange(LEVELS)[None, :] == router_targets[:, group][:, None]).astype(f32)
        logit_grads.append(raised / jnp.sum(raised, axis=1, keepdims=True) - chosen)
    grad_logits = jnp.concatenate(logit_grads, axis=1)
    grad_router = jnp.dot(pooled.T, grad_logits, precision=highest, preferred_element_type=f32)
    grad_pooled = (
        jnp.dot(grad_logits, w_router.T, precision=highest, preferred_element_type=f32)
        * lax.rsqrt(seq_length)[:, None]
    )
    member_own = own_rows(in_seq.astype(f32), 0)
    grad_pooled_own = jnp.dot(
        member_own, grad_pooled, precision=highest, preferred_element_type=f32
    )
    two_parts, grad_up_part, grad_router, grad_pooled_own = lax.optimization_barrier(
        (two_parts, grad_up_part, grad_router, grad_pooled_own)
    )
    grad_up = lax.psum_scatter(grad_up_part, "seq", scatter_dimension=0, tiled=True)

    grad_two = sum([v.astype(f32) for v in two_parts[1:]], two_parts[0])
    back_two, gain_two = normalize_back(grad_two, hat_two, inverse_two, gain_ffn)
    grad_hidden = own_rows(cotangent, 0).astype(f32) + back_two
    grad_attn_own = grad_hidden.astype(bf16)
    grad_mixed = contract(grad_attn_own, full_out, 1, 1).astype(bf16)
    grad_mixed = [
        grad_mixed[:, slot * head_width : (slot + 1) * head_width] for slot in range(head_count)
    ]
    active, grad_mixed = lax.optimization_barrier((active, grad_mixed))
    grad_mixed = [grad_mixed[0]] + [
        swap(grad_mixed[slot], slot) for slot in range(1, head_count)
    ]
    grad_heads = placed(grad_mixed, head_rank, 0)
    grad_heads, grad_attn_own = lax.optimization_barrier((grad_heads, grad_attn_own))
    grad_attn = gather_heads(grad_attn_own)
    grad_slots = []
    for slot in range(heads):
        piece = lax.dynamic_slice_in_dim(grad_heads, (place ^ slot) * HD, HD, 1)
        piece = piece.reshape(CHUNKS, SHORT_DEV, HD)
        grad_slots.append(across(piece, slot) if slot else piece)
    ffn_parts = [
        dot(active[slot * share : (slot + 1) * share], full_down) for slot in range(head_count)
    ]
    ffn_parts[1:] = [v.astype(bf16) for v in ffn_parts[1:]]
    grad_slots, ffn_parts = lax.optimization_barrier((grad_slots, ffn_parts))

    own_grads, other_grads = attend_backward(
        scal, slots, other_slots, grad_slots, logs, heads, members
    )
    own_grads, other_grads, grad_attn[:-1] = lax.optimization_barrier(
        (own_grads, other_grads, grad_attn[:-1])
    )
    other_grads = [
        among(v, members - step) for step, v in zip(range(1, members), other_grads)
    ]
    sums = []
    for slot in range(heads):
        total = own_grads[slot].astype(f32)
        sums.append(sum([v[slot].astype(f32) for v in other_grads], total).astype(bf16))
    sums, ffn_parts = lax.optimization_barrier((sums, ffn_parts))
    sums = exchange(sums)
    ffn_parts = scatter_heads(ffn_parts)
    grad_attn = jnp.concatenate(grad_attn, axis=0)
    grad_out_part = contract(jnp.concatenate(heads_rel, axis=0), grad_attn, 0, 0).astype(bf16)
    grad_out_part, sums, ffn_parts[:-1] = lax.optimization_barrier(
        (grad_out_part, sums, ffn_parts[:-1])
    )
    total_out = scatter_members(grad_out_part)
    grad_projected = gather_grads(scal, cosine, -sine, sums)
    grad_qkv_part = contract(normed_low, grad_projected, 0, 0).astype(bf16)
    grad_projected, grad_qkv_part, ffn_parts, grad_down, grad_up = lax.optimization_barrier(
        (grad_projected, grad_qkv_part, ffn_parts, grad_down, grad_up)
    )
    total_qkv = lax.psum_scatter(grad_qkv_part, "seq", scatter_dimension=0, tiled=True)
    grad_down, grad_up = grad_down.astype(f32), grad_up.astype(f32)
    output_own = (
        hidden + sum([v.astype(f32) for v in ffn_parts[1:]], ffn_parts[0])
    ).astype(bf16)
    output_slots = gather_heads(output_own)
    one_parts = [
        sum(
            contract(
                own_rows(grad_projected, slot)[:, part * head_width : (part + 1) * head_width],
                w_qkv[:, part],
                1,
                1,
            )
            for part in range(3)
        )
        for slot in range(head_count)
    ]
    one_parts[1:] = [v.astype(bf16) for v in one_parts[1:]]
    one_parts, total_out, output_slots[1:-1] = lax.optimization_barrier(
        (one_parts, total_out, output_slots[1:-1])
    )
    one_parts = scatter_heads(one_parts)
    total_out = scatter_places(total_out)

    grad_one = sum([v.astype(f32) for v in one_parts[1:]], one_parts[0]) + grad_pooled_own
    back_one, gain_one = normalize_back(grad_one, hat_own, inverse_own, gain_attn)
    tokens_back = (grad_hidden + back_one).astype(bf16)
    tokens_back, total_qkv, total_out = lax.optimization_barrier(
        (tokens_back, total_qkv, total_out)
    )
    total_qkv = lax.all_gather(total_qkv, "seq", axis=0, tiled=True)
    token_slots = gather_heads(tokens_back)
    grad_out = gather_seq(total_out).astype(f32)
    grad_qkv = jnp.stack(
        [
            total_qkv[:, part * head_width : (part + 1) * head_width].astype(f32)
            for part in range(3)
        ],
        axis=1,
    )
    output = in_order(output_slots, bf16)
    token_slots, gains = lax.optimization_barrier(
        (token_slots, jnp.stack([gain_one, gain_two]))
    )
    grad_tokens = in_order(token_slots, f32)
    gains = butterfly(butterfly(gains, "heads", head_count), "seq", seq_count)
    return (
        output,
        grad_tokens,
        grad_qkv,
        grad_out,
        grad_up,
        grad_down,
        gains[0],
        gains[1],
        grad_router,
    )


def solution(mesh):
    return jax.shard_map(
        local,
        mesh=mesh,
        in_specs=(
            P("seq", None),
            P(None, None, "heads"),
            P("heads", None),
            P("seq", "heads"),
            P("heads", "seq"),
            P(),
            P(),
            P(),
            P(),
            P(),
            P(),
            P("seq", None),
        ),
        out_specs=(
            P("seq", None),
            P("seq", None),
            P(None, None, "heads"),
            P("heads", None),
            P("seq", "heads"),
            P("heads", "seq"),
            P(),
            P(),
            P(),
        ),
        check_vma=False,
    )
```

```python
import functools

import jax
import jax.numpy as jnp
from jax import lax
from jax.experimental import pallas as pl
from jax.experimental.pallas import tpu as pltpu
from jax.sharding import PartitionSpec as P

D = 2048
H = 16
HD = 128
FF = 8192
SHORT_DEV = 128
NSHORT = 3
NLONG = 2
LEVELS = 4
SEQS = 5
CHUNKS = NSHORT + 2 * NLONG

epsilon = 1e-05
highest = lax.Precision.HIGHEST
f32 = jnp.float32
bf16 = jnp.bfloat16
SCALE = HD ** (-0.5)


def dot(left, right):
    return jnp.dot(left, right, preferred_element_type=f32)


def contract(left, right, left_dim, right_dim):
    return lax.dot_general(
        left, right, (((left_dim,), (right_dim,)), ((), ())), preferred_element_type=f32
    )


def normalize_parts(values):
    centered = values - jnp.mean(values, axis=-1, keepdims=True)
    inverse = lax.rsqrt(jnp.mean(centered * centered, axis=-1, keepdims=True) + epsilon)
    return (centered * inverse, inverse)


def normalize_back(grad_normed, normed_hat, inverse, gain):
    grad_hat = grad_normed * gain
    middle = (
        grad_hat
        - jnp.mean(grad_hat, axis=-1, keepdims=True)
        - normed_hat * jnp.mean(grad_hat * normed_hat, axis=-1, keepdims=True)
    )
    return (inverse * middle, jnp.sum(grad_normed * normed_hat, axis=0))


def flip(values, axis, size, bit):
    return lax.ppermute(values, axis, [(i, i ^ bit) for i in range(size)])


def butterfly(values, axis, size):
    bit = 1
    while bit < size:
        values = values + flip(values, axis, size, bit)
        bit *= 2
    return values


def key_copies(scal, own, others, keys_short, keys_long, sems, members, heads):
    head, member = scal[0], scal[1]
    copies = []
    for part in range(members):
        source = own if part == 0 else others[(part - 1) * heads : part * heads]
        whose = lax.rem(member + part, members)
        for slot in range(heads):
            block = (head ^ slot) * members + whose
            number = len(copies)
            copies.append(
                pltpu.make_async_copy(
                    source[slot].at[0:NSHORT, :, HD:], keys_short.at[:, block], sems.at[number]
                )
            )
            for index in range(NLONG):
                first = NSHORT + 2 * index
                number = len(copies)
                copies.append(
                    pltpu.make_async_copy(
                        source[slot].at[first : first + 2, :, HD:],
                        keys_long.at[index, block],
                        sems.at[number],
                    )
                )
    return copies


def row_copies(scal, slots, held, sems, heads, outward):
    head = scal[0]
    copies = []
    for slot in range(heads):
        ends = (slots[slot].at[:, :, 0:HD], held.at[head ^ slot])
        if outward:
            ends = ends[::-1]
        copies.append(pltpu.make_async_copy(ends[0], ends[1], sems.at[slot]))
    return copies


def sequence_loop(work):
    def short(index, carry):
        work(0, index, index, 1, index)
        return carry

    def long(index, carry):
        work(1, index, NSHORT + 2 * index, 2, NSHORT + index)
        return carry

    lax.fori_loop(0, NSHORT, short, 0)
    lax.fori_loop(0, NLONG, long, 0)


def allowed_mask(member, members, size):
    key_at = lax.broadcasted_iota(jnp.int32, (members * size, size), 0)
    query_at = lax.broadcasted_iota(jnp.int32, (members * size, size), 1) + member * size
    return key_at <= query_at


def attend_kernel(heads, members, scal, *refs):
    count = heads
    own = refs[:count]
    others = refs[count : members * count]
    rest = refs[members * count :]
    out_slots = rest[:count]
    log_ref = rest[count]
    queries, keys_short, keys_long, mixed, row_sems, key_sems = rest[count + 1 :]
    copies = row_copies(scal, own, queries, row_sems, heads, False)
    copies += key_copies(scal, own, others, keys_short, keys_long, key_sems, members, heads)
    for copy in copies:
        copy.start()
    for copy in copies:
        copy.wait()

    def work(kind, index, first, chunks, live_at):
        size = chunks * SHORT_DEV
        live = scal[2 + live_at].astype(f32)
        mask = allowed_mask(scal[1], members, size)
        for place in range(heads):
            span = (place + 1) * members
            if kind == 0:
                block = keys_short[index, 0:span]
            else:
                block = keys_long[index, 0:span]
            block = block.reshape(span * size, 2 * HD)
            keys, values = block[:, :HD], block[:, HD:]
            query = queries[place, pl.ds(first, chunks)].reshape(size, HD)
            scores = contract(keys, query, 1, 1) * SCALE
            edge = place * members * size
            last = jnp.where(mask, scores[edge:], -1e30)
            largest = jnp.max(last, axis=0, keepdims=True)
            if place:
                early = scores[:edge]
                largest = jnp.maximum(largest, jnp.max(early, axis=0, keepdims=True))
            raised = jnp.exp(last - largest)
            total = jnp.sum(raised, axis=0, keepdims=True)
            low = raised.astype(bf16)
            turned = contract(values[edge:], low, 0, 0)
            if place:
                raised = jnp.exp(early - largest)
                total = total + jnp.sum(raised, axis=0, keepdims=True)
                turned = turned + contract(values[:edge], raised.astype(bf16), 0, 0)
            turned = turned * (live / total)
            mixed[place, pl.ds(first, chunks)] = (
                turned.T.astype(bf16).reshape(chunks, SHORT_DEV, HD)
            )
            logs = largest + jnp.log(total)
            for chunk in range(chunks):
                log_ref[place, first + chunk] = logs[:, chunk * SHORT_DEV : (chunk + 1) * SHORT_DEV]

    sequence_loop(work)
    copies = row_copies(scal, out_slots, mixed, row_sems, heads, True)
    for copy in copies:
        copy.start()
    for copy in copies:
        copy.wait()


def attend_forward(scal, own, others, heads, members):
    blocks = heads * members
    anywhere = pl.BlockSpec(memory_space=pl.ANY)
    result = pl.pallas_call(
        functools.partial(attend_kernel, heads, members),
        out_shape=[jax.ShapeDtypeStruct((CHUNKS, SHORT_DEV, HD), bf16)] * heads
        + [jax.ShapeDtypeStruct((heads, CHUNKS, 1, SHORT_DEV), f32)],
        in_specs=[pl.BlockSpec(memory_space=pltpu.SMEM)]
        + [anywhere] * (len(own) + len(others)),
        out_specs=[anywhere] * heads + [pl.BlockSpec(memory_space=pltpu.VMEM)],
        scratch_shapes=[
            pltpu.VMEM((heads, CHUNKS, SHORT_DEV, HD), bf16),
            pltpu.VMEM((NSHORT, blocks, SHORT_DEV, 2 * HD), bf16),
            pltpu.VMEM((NLONG, blocks, 2, SHORT_DEV, 2 * HD), bf16),
            pltpu.VMEM((heads, CHUNKS, SHORT_DEV, HD), bf16),
            pltpu.SemaphoreType.DMA((heads,)),
            pltpu.SemaphoreType.DMA((3 * blocks,)),
        ],
        compiler_params=pltpu.CompilerParams(vmem_limit_bytes=56 << 20),
        cost_estimate=pl.CostEstimate(
            flops=4 * 10**9, bytes_accessed=7 << 20, transcendentals=4 * 10**6
        ),
        name="attend_forward",
    )(scal, *own, *others)
    return (result[:heads], result[heads])


def back_kernel(heads, members, scal, *refs):
    count = heads
    own = refs[:count]
    others = refs[count : members * count]
    rest = refs[members * count :]
    grad_slots = rest[:count]
    log_ref = rest[count]
    rest = rest[count + 1 :]
    own_out = rest[:count]
    other_out = rest[count : count + members - 1]
    scratch = rest[count + members - 1 :]
    queries, keys_short, keys_long, grads, sum_short, sum_long = scratch[:6]
    low_short, low_long, zeros, row_sems, grad_sems, key_sems, zero_sems = scratch[6:]
    copies = row_copies(scal, own, queries, row_sems, heads, False)
    copies += row_copies(scal, grad_slots, grads, grad_sems, heads, False)
    copies += key_copies(scal, own, others, keys_short, keys_long, key_sems, members, heads)
    for copy in copies:
        copy.start()
    zeros[...] = jnp.zeros(zeros.shape, bf16)
    blanks = [
        pltpu.make_async_copy(
            zeros, other_out[part].at[slot, :, :, 0:HD], zero_sems.at[part * heads + slot]
        )
        for part in range(members - 1)
        for slot in range(heads)
    ]
    for copy in blanks:
        copy.start()
    for copy in copies:
        copy.wait()

    def work(kind, index, first, chunks, live_at):
        size = chunks * SHORT_DEV
        live = scal[2 + live_at].astype(bf16)
        mask = allowed_mask(scal[1], members, size)
        if kind == 0:
            keys_ref, sum_ref, low_ref = keys_short, sum_short, low_short
        else:
            keys_ref, sum_ref, low_ref = keys_long, sum_long, low_long
        for place in reversed(range(heads)):
            span = (place + 1) * members
            block = keys_ref[index, 0:span].reshape(span * size, 2 * HD)
            keys, values = block[:, :HD], block[:, HD:]
            query = queries[place, pl.ds(first, chunks)].reshape(size, HD)
            grad = grads[place, pl.ds(first, chunks)].reshape(size, HD) * live
            logs = jnp.concatenate(
                [log_ref[place, first + chunk] for chunk in range(chunks)], axis=1
            )
            probs = jnp.exp(contract(keys, query, 1, 1) * SCALE - logs)
            edge = place * members * size
            last = jnp.where(mask, probs[edge:], 0.0)
            probs = jnp.concatenate([probs[:edge], last], axis=0) if place else last
            grad_probs = contract(values, grad, 1, 1)
            delta = jnp.sum(probs * grad_probs, axis=0, keepdims=True)
            grad_scores = (probs * (grad_probs - delta)).astype(bf16)
            grad_value = dot(probs.astype(bf16), grad)
            grad_key = dot(grad_scores, query) * SCALE
            turned = contract(keys, grad_scores, 0, 0) * SCALE
            queries[place, pl.ds(first, chunks)] = (
                turned.T.astype(bf16).reshape(chunks, SHORT_DEV, HD)
            )
            pair = jnp.concatenate([grad_key, grad_value], axis=1)
            if place == heads - 1:
                sum_ref[...] = pair
            else:
                sum_ref[0 : span * size] += pair
        low_ref[index] = sum_ref[...].astype(bf16).reshape(low_ref.shape[1:])

    sequence_loop(work)
    copies = row_copies(scal, own_out, queries, row_sems, heads, True)
    head, member = scal[0], scal[1]
    number = 0
    for part in range(members):
        whose = lax.rem(member + part, members)
        for slot in range(heads):
            block = (head ^ slot) * members + whose
            target = own_out[slot] if part == 0 else other_out[part - 1].at[slot]
            copies.append(
                pltpu.make_async_copy(
                    low_short.at[:, block], target.at[0:NSHORT, :, HD:], key_sems.at[number]
                )
            )
            number += 1
            for index in range(NLONG):
                first = NSHORT + 2 * index
                copies.append(
                    pltpu.make_async_copy(
                        low_long.at[index, block],
                        target.at[first : first + 2, :, HD:],
                        key_sems.at[number],
                    )
                )
                number += 1
    for copy in copies:
        copy.start()
    for copy in blanks + copies:
        copy.wait()


def attend_backward(scal, own, others, grad_slots, logs, heads, members):
    blocks = heads * members
    anywhere = pl.BlockSpec(memory_space=pl.ANY)
    result = pl.pallas_call(
        functools.partial(back_kernel, heads, members),
        out_shape=[jax.ShapeDtypeStruct((CHUNKS, SHORT_DEV, 3 * HD), bf16)] * heads
        + [jax.ShapeDtypeStruct((heads, CHUNKS, SHORT_DEV, 3 * HD), bf16)] * (members - 1),
        in_specs=[pl.BlockSpec(memory_space=pltpu.SMEM)]
        + [anywhere] * (heads + blocks)
        + [pl.BlockSpec(memory_space=pltpu.VMEM)],
        out_specs=[anywhere] * (heads + members - 1),
        scratch_shapes=[
            pltpu.VMEM((heads, CHUNKS, SHORT_DEV, HD), bf16),
            pltpu.VMEM((NSHORT, blocks, SHORT_DEV, 2 * HD), bf16),
            pltpu.VMEM((NLONG, blocks, 2, SHORT_DEV, 2 * HD), bf16),
            pltpu.VMEM((heads, CHUNKS, SHORT_DEV, HD), bf16),
            pltpu.VMEM((blocks * SHORT_DEV, 2 * HD), f32),
            pltpu.VMEM((2 * blocks * SHORT_DEV, 2 * HD), f32),
            pltpu.VMEM((NSHORT, blocks, SHORT_DEV, 2 * HD), bf16),
            pltpu.VMEM((NLONG, blocks, 2, SHORT_DEV, 2 * HD), bf16),
            pltpu.VMEM((CHUNKS, SHORT_DEV, HD), bf16),
            pltpu.SemaphoreType.DMA((heads,)),
            pltpu.SemaphoreType.DMA((heads,)),
            pltpu.SemaphoreType.DMA((3 * blocks,)),
            pltpu.SemaphoreType.DMA(((members - 1) * heads,)),
        ],
        compiler_params=pltpu.CompilerParams(vmem_limit_bytes=60 << 20),
        cost_estimate=pl.CostEstimate(
            flops=10**10, bytes_accessed=12 << 20, transcendentals=4 * 10**6
        ),
        name="attend_backward",
    )(scal, *own, *others, *grad_slots, logs)
    return (result[:heads], result[heads:])


def rotate_rows(values, cosine, sine):
    return values * cosine + pltpu.roll(values, HD // 2, 1) * sine


def project_kernel(heads, scal, tokens, gain, cosine, sine, weights, *refs):
    slots = refs[:heads]
    normed, pooled = refs[heads : heads + 2]
    held_weights, acc, held, in_sems, out_sems = refs[heads + 2 :]
    head = scal[0]
    loads = [
        pltpu.make_async_copy(weights.at[part], held_weights.at[part], in_sems.at[part])
        for part in range(3)
    ]
    for load in loads:
        load.start()
    pooled[...] = jnp.zeros(pooled.shape, f32)

    def norm(chunk, carry):
        here = pl.ds(pl.multiple_of(chunk * SHORT_DEV, SHORT_DEV), SHORT_DEV)
        hat, _ = normalize_parts(tokens[here, :].astype(f32))
        values = hat * gain[...]
        normed[here, :] = values.astype(bf16)
        at = jnp.where(chunk < NSHORT, chunk, NSHORT + (chunk - NSHORT) // 2)
        rows = lax.broadcasted_iota(jnp.int32, pooled.shape, 0)
        added = jnp.sum(values, axis=0, keepdims=True)
        pooled[...] += jnp.where(rows == at, added, 0.0)
        return carry

    lax.fori_loop(0, CHUNKS, norm, 0)
    for part in range(3):
        loads[part].wait()
        acc[...] = dot(normed[...], held_weights[part])

        def spread(chunk, carry):
            here = pl.ds(pl.multiple_of(chunk * SHORT_DEV, SHORT_DEV), SHORT_DEV)
            for index in range(heads):
                values = acc[here, index * HD : (index + 1) * HD]
                if part < 2:
                    values = rotate_rows(values, cosine[here, :], sine[here, :])
                held[index, chunk, :, part * HD : (part + 1) * HD] = values.astype(bf16)
            return carry

        lax.fori_loop(0, CHUNKS, spread, 0)
    stores = [
        pltpu.make_async_copy(held.at[head ^ slot], slots[slot], out_sems.at[slot])
        for slot in range(heads)
    ]
    for store in stores:
        store.start()
    for store in stores:
        store.wait()


def project(scal, tokens, gain, cosine, sine, weights):
    rows = tokens.shape[0]
    width = weights.shape[2]
    heads = width // HD
    anywhere = pl.BlockSpec(memory_space=pl.ANY)
    inside = pl.BlockSpec(memory_space=pltpu.VMEM)
    result = pl.pallas_call(
        functools.partial(project_kernel, heads),
        out_shape=[jax.ShapeDtypeStruct((CHUNKS, SHORT_DEV, 3 * HD), bf16)] * heads
        + [jax.ShapeDtypeStruct((rows, D), bf16), jax.ShapeDtypeStruct((8, D), f32)],
        in_specs=[pl.BlockSpec(memory_space=pltpu.SMEM)] + [inside] * 4 + [anywhere],
        out_specs=[anywhere] * heads + [inside] * 2,
        scratch_shapes=[
            pltpu.VMEM((3, D, width), bf16),
            pltpu.VMEM((rows, width), f32),
            pltpu.VMEM((heads, CHUNKS, SHORT_DEV, 3 * HD), bf16),
            pltpu.SemaphoreType.DMA((3,)),
            pltpu.SemaphoreType.DMA((heads,)),
        ],
        compiler_params=pltpu.CompilerParams(vmem_limit_bytes=50 << 20),
        cost_estimate=pl.CostEstimate(
            flops=6 * rows * D * width, bytes_accessed=16 << 20, transcendentals=rows
        ),
        name="project",
    )(scal, tokens, gain, cosine, sine, weights)
    return (result[:heads], result[heads], result[heads + 1])


def gather_kernel(heads, scal, cosine, sine, *refs):
    slots = refs[:heads]
    out, held, sems = refs[heads:]
    copies = [
        pltpu.make_async_copy(slots[slot], held.at[scal[0] ^ slot], sems.at[slot])
        for slot in range(heads)
    ]
    for copy in copies:
        copy.start()
    for copy in copies:
        copy.wait()

    def spread(chunk, carry):
        here = pl.ds(pl.multiple_of(chunk * SHORT_DEV, SHORT_DEV), SHORT_DEV)
        for index in range(heads):
            for part in range(3):
                values = held[index, chunk, :, part * HD : (part + 1) * HD]
                if part < 2:
                    values = rotate_rows(values.astype(f32), cosine[here, :], sine[here, :])
                at = (part * heads + index) * HD
                out[here, at : at + HD] = values.astype(bf16)
        return carry

    lax.fori_loop(0, CHUNKS, spread, 0)


def gather_grads(scal, cosine, sine, slots):
    heads = len(slots)
    rows = CHUNKS * SHORT_DEV
    inside = pl.BlockSpec(memory_space=pltpu.VMEM)
    return pl.pallas_call(
        functools.partial(gather_kernel, heads),
        out_shape=jax.ShapeDtypeStruct((rows, 3 * heads * HD), bf16),
        in_specs=[pl.BlockSpec(memory_space=pltpu.SMEM)]
        + [inside] * 2
        + [pl.BlockSpec(memory_space=pl.ANY)] * heads,
        out_specs=inside,
        scratch_shapes=[
            pltpu.VMEM((heads, CHUNKS, SHORT_DEV, 3 * HD), bf16),
            pltpu.SemaphoreType.DMA((heads,)),
        ],
        compiler_params=pltpu.CompilerParams(vmem_limit_bytes=24 << 20),
        cost_estimate=pl.CostEstimate(
            flops=10 * rows * heads * HD, bytes_accessed=6 << 20, transcendentals=0
        ),
        name="gather_grads",
    )(scal, cosine, sine, *slots)


def local(
    tokens,
    w_qkv,
    w_out,
    w_up,
    w_down,
    gain_attn,
    gain_ffn,
    w_router,
    head_quarters,
    ffn_quarters,
    router_targets,
    cotangent,
):
    rows = tokens.shape[0]
    seq_rank = lax.axis_index("seq")
    seq_count = lax.axis_size("seq")
    head_rank = lax.axis_index("heads")
    head_count = lax.axis_size("heads")
    head_width = w_out.shape[0]
    ffn_width = w_up.shape[1]
    heads = head_width // HD
    members = seq_count // heads
    place, member = seq_rank // members, seq_rank % members
    share = rows // head_count
    short_rows = NSHORT * SHORT_DEV

    def across(values, slot):
        pairs = [
            (h * members + m, (h ^ slot) * members + m)
            for h in range(heads)
            for m in range(members)
        ]
        return lax.ppermute(values, "seq", pairs)

    def exchange(slots):
        sent = [across(slots[slot], slot) for slot in reversed(range(1, heads))]
        return [slots[0]] + sent[::-1]

    def among(values, step):
        pairs = [
            (h * members + (m + step) % members, h * members + m)
            for h in range(heads)
            for m in range(members)
        ]
        return lax.ppermute(values, "seq", pairs)

    def scatter_members(values):
        size = values.shape[0] // members

        def block(number):
            return lax.dynamic_slice_in_dim(values, number * size, size, 0)

        total = block(member).astype(f32)
        for step in range(1, members):
            sent = block((member + members - step) % members)
            total = total + among(sent, step).astype(f32)
        return total.astype(bf16)

    def scatter_places(values):
        size = values.shape[0] // heads
        pieces = [
            lax.dynamic_slice_in_dim(values, (place ^ slot) * size, size, 0) for slot in range(heads)
        ]
        pieces = [v.astype(f32) for v in exchange(pieces)]
        return sum(pieces[1:], pieces[0]).astype(bf16)

    def gather_seq(values):
        values = placed(exchange([values] * heads), place, 0)
        size = values.shape[0]
        full = jnp.zeros((size * members,) + values.shape[1:], values.dtype)
        for step in range(members):
            piece = among(values, step) if step else values
            at = (member + step) % members * size
            full = lax.dynamic_update_slice_in_dim(full, piece, at, 0)
        return full

    def swap(values, slot):
        return flip(values, "heads", head_count, slot)

    def own_rows(values, slot):
        return lax.dynamic_slice_in_dim(values, (head_rank ^ slot) * share, share, 0)

    def scatter_heads(parts):
        return [parts[0]] + [
            swap(parts[slot].astype(bf16), slot) for slot in range(1, head_count)
        ]

    def gather_heads(values):
        return [values] + [swap(values, slot) for slot in range(1, head_count)]

    def gather_doubling(values):
        slots = [values]
        bit = 1
        while bit < head_count:
            slots = slots + [swap(v, bit) for v in slots]
            bit *= 2
        return slots

    def in_order(slots, kind):
        full = jnp.zeros((rows,) + slots[0].shape[1:], kind)
        for slot in range(head_count):
            full = lax.dynamic_update_slice_in_dim(
                full, slots[slot].astype(kind), (head_rank ^ slot) * share, 0
            )
        return full

    def placed(slots, key, axis):
        size = slots[0].shape[axis]
        shape = list(slots[0].shape)
        shape[axis] = size * len(slots)
        full = jnp.zeros(shape, slots[0].dtype)
        for slot, values in enumerate(slots):
            full = lax.dynamic_update_slice_in_dim(full, values, (key ^ slot) * size, axis)
        return full

    half = ffn_width // 2
    first_up = lax.all_gather(w_up[:, :half], "seq", axis=0, tiled=True)
    out_slots = gather_heads(w_out)

    column = jnp.arange(rows)
    is_short = column < short_rows
    offset = column - short_rows
    seq_id = jnp.where(is_short, column // SHORT_DEV, NSHORT + offset // (2 * SHORT_DEV))
    position = jnp.where(
        is_short,
        seq_rank * SHORT_DEV + column % SHORT_DEV,
        seq_rank * 2 * SHORT_DEV + offset % (2 * SHORT_DEV),
    )
    in_seq = seq_id[:, None] == jnp.arange(SEQS)[None, :]
    seq_length = jnp.where(
        jnp.arange(SEQS) < NSHORT, SHORT_DEV * seq_count, 2 * SHORT_DEV * seq_count
    ).astype(f32)
    ffn_level = jnp.sum(jnp.where(in_seq, ffn_quarters[None, :], 0), axis=1)
    half_dim = HD // 2
    frequency = 10000.0 ** (-jnp.arange(half_dim, dtype=f32) * 2.0 / HD)
    angle = position.astype(f32)[:, None] * frequency[None, :]
    cosine = jnp.cos(angle)
    sine = jnp.sin(angle)
    cosine = jnp.concatenate([cosine, cosine], axis=1)
    sine = jnp.concatenate([-sine, sine], axis=1)
    my_head = head_rank * heads + place
    head_live = (my_head < head_quarters * (H // LEVELS)).astype(jnp.int32)
    scal = jnp.concatenate([jnp.stack([place, member]).astype(jnp.int32), head_live])

    slots, normed_low, pooled = project(
        scal, tokens, gain_attn[None, :], cosine, sine, w_qkv.transpose(1, 0, 2)
    )
    slots = exchange(slots)
    other_slots = [among(v, step) for step in range(1, members) for v in slots]
    tokens_own = own_rows(tokens, 0).astype(f32)
    hat_own, inverse_own = normalize_parts(tokens_own)
    cotangent_rel = jnp.concatenate(
        [own_rows(cotangent, slot) for slot in range(head_count)], axis=0
    )
    hops = []
    bit = 1
    while bit < seq_count:
        hops.append(bit)
        bit *= 2

    def hop(values, bits):
        for bit in bits:
            values = values + flip(values, "seq", seq_count, bit)
        return values

    pooled = hop(pooled[:SEQS], hops[:-2])
    early = (slots, other_slots, out_slots[:-1], w_up[:, half:], w_down)
    early = early + (hat_own, inverse_own, cotangent_rel, pooled)
    early = lax.optimization_barrier(early)
    slots, other_slots, out_slots[:-1], own_up, own_down = early[:5]
    hat_own, inverse_own, cotangent_rel, pooled = early[5:]
    second_up = lax.all_gather(own_up, "seq", axis=0, tiled=True)
    full_down = lax.all_gather(own_down, "seq", axis=1, tiled=True)
    pooled = hop(pooled, hops[-2:-1])
    full_out = jnp.concatenate(out_slots, axis=0)
    mixed_slots, logs = attend_forward(scal, slots, other_slots, heads, members)
    mixed_slots = [across(v, slot) if slot else v for slot, v in enumerate(mixed_slots)]
    mixed_slots, pooled = lax.optimization_barrier((mixed_slots, pooled))
    pooled = hop(pooled, hops[-1:])
    mixed_slots = [v.reshape(rows, HD) for v in mixed_slots]
    heads_out = placed(mixed_slots, place, 1)

    heads_rel = [own_rows(heads_out, slot) for slot in range(head_count)]
    heads_own = jnp.concatenate(
        [heads_rel[0]] + [swap(heads_rel[slot], slot) for slot in range(1, head_count)], axis=1
    )
    hidden = tokens_own + dot(heads_own, full_out)
    hat_two, inverse_two = normalize_parts(hidden)
    normed_two = gather_heads((hat_two * gain_ffn).astype(bf16))

    level_rel = jnp.concatenate([own_rows(ffn_level, slot) for slot in range(head_count)])
    unit_index = head_rank * ffn_width + jnp.arange(ffn_width)
    ffn_live = (unit_index[None, :] < (level_rel * (FF // LEVELS))[:, None]).astype(f32)
    full_up = jnp.concatenate([first_up, second_up], axis=1)
    normed_two, pooled, full_up = lax.optimization_barrier((normed_two, pooled, full_up))
    normed_two = jnp.concatenate(normed_two, axis=0)
    upward = dot(normed_two, full_up)
    kept = jnp.maximum(upward, 0.0)
    active = (jnp.square(kept) * ffn_live).astype(bf16)
    grad_down_part = contract(active, cotangent_rel, 0, 0).astype(bf16)
    cotangent_rel, kept, grad_down_part = lax.optimization_barrier(
        (cotangent_rel, kept, grad_down_part)
    )
    grad_active = contract(cotangent_rel, full_down, 1, 1).astype(bf16)
    grad_upward = (grad_active.astype(f32) * ffn_live * 2.0 * kept).astype(bf16)
    grad_down = lax.psum_scatter(grad_down_part, "seq", scatter_dimension=1, tiled=True)
    two_parts = [
        contract(grad_upward[slot * share : (slot + 1) * share], full_up, 1, 1)
        for slot in range(head_count)
    ]
    two_parts = scatter_heads(two_parts)
    grad_up_part = contract(normed_two, grad_upward, 0, 0).astype(bf16)

    pooled = pooled * lax.rsqrt(seq_length)[:, None]
    logits = jnp.dot(pooled, w_router, precision=highest, preferred_element_type=f32)
    logit_grads = []
    for group in range(2):
        group_logits = logits[:, LEVELS * group : LEVELS * (group + 1)]
        raised = jnp.exp(group_logits - jnp.max(group_logits, axis=1, keepdims=True))
        chosen = (jnp.arange(LEVELS)[None, :] == router_targets[:, group][:, None]).astype(f32)
        logit_grads.append(raised / jnp.sum(raised, axis=1, keepdims=True) - chosen)
    grad_logits = jnp.concatenate(logit_grads, axis=1)
    grad_router = jnp.dot(pooled.T, grad_logits, precision=highest, preferred_element_type=f32)
    grad_pooled = (
        jnp.dot(grad_logits, w_router.T, precision=highest, preferred_element_type=f32)
        * lax.rsqrt(seq_length)[:, None]
    )
    member_own = own_rows(in_seq.astype(f32), 0)
    grad_pooled_own = jnp.dot(
        member_own, grad_pooled, precision=highest, preferred_element_type=f32
    )
    two_parts, grad_up_part, grad_router, grad_pooled_own = lax.optimization_barrier(
        (two_parts, grad_up_part, grad_router, grad_pooled_own)
    )
    grad_up = lax.psum_scatter(grad_up_part, "seq", scatter_dimension=0, tiled=True)

    grad_two = sum([v.astype(f32) for v in two_parts[1:]], two_parts[0])
    back_two, gain_two = normalize_back(grad_two, hat_two, inverse_two, gain_ffn)
    grad_hidden = own_rows(cotangent, 0).astype(f32) + back_two
    grad_attn_own = grad_hidden.astype(bf16)
    grad_mixed = contract(grad_attn_own, full_out, 1, 1).astype(bf16)
    grad_mixed = [
        grad_mixed[:, slot * head_width : (slot + 1) * head_width] for slot in range(head_count)
    ]
    active, grad_mixed = lax.optimization_barrier((active, grad_mixed))
    grad_mixed = [grad_mixed[0]] + [
        swap(grad_mixed[slot], slot) for slot in range(1, head_count)
    ]
    grad_heads = placed(grad_mixed, head_rank, 0)
    grad_heads, grad_attn_own = lax.optimization_barrier((grad_heads, grad_attn_own))
    grad_attn = gather_heads(grad_attn_own)
    grad_slots = []
    for slot in range(heads):
        piece = lax.dynamic_slice_in_dim(grad_heads, (place ^ slot) * HD, HD, 1)
        piece = piece.reshape(CHUNKS, SHORT_DEV, HD)
        grad_slots.append(across(piece, slot) if slot else piece)
    ffn_parts = [
        dot(active[slot * share : (slot + 1) * share], full_down) for slot in range(head_count)
    ]
    ffn_parts[1:] = [v.astype(bf16) for v in ffn_parts[1:]]
    grad_slots, ffn_parts = lax.optimization_barrier((grad_slots, ffn_parts))

    own_grads, other_grads = attend_backward(
        scal, slots, other_slots, grad_slots, logs, heads, members
    )
    own_grads, other_grads, grad_attn[:-1] = lax.optimization_barrier(
        (own_grads, other_grads, grad_attn[:-1])
    )
    other_grads = [
        among(v, members - step) for step, v in zip(range(1, members), other_grads)
    ]
    sums = []
    for slot in range(heads):
        total = own_grads[slot].astype(f32)
        sums.append(sum([v[slot].astype(f32) for v in other_grads], total).astype(bf16))
    sums, ffn_parts = lax.optimization_barrier((sums, ffn_parts))
    sums = exchange(sums)
    ffn_parts = scatter_heads(ffn_parts)
    grad_attn = jnp.concatenate(grad_attn, axis=0)
    grad_out_part = contract(jnp.concatenate(heads_rel, axis=0), grad_attn, 0, 0).astype(bf16)
    grad_out_part, sums, ffn_parts[:-1] = lax.optimization_barrier(
        (grad_out_part, sums, ffn_parts[:-1])
    )
    total_out = scatter_members(grad_out_part)
    grad_projected = gather_grads(scal, cosine, -sine, sums)
    grad_qkv_part = contract(normed_low, grad_projected, 0, 0).astype(bf16)
    grad_projected, grad_qkv_part, ffn_parts, grad_down, grad_up = lax.optimization_barrier(
        (grad_projected, grad_qkv_part, ffn_parts, grad_down, grad_up)
    )
    total_qkv = lax.psum_scatter(grad_qkv_part, "seq", scatter_dimension=0, tiled=True)
    grad_down, grad_up = grad_down.astype(f32), grad_up.astype(f32)
    output_own = (
        hidden + sum([v.astype(f32) for v in ffn_parts[1:]], ffn_parts[0])
    ).astype(bf16)
    output_slots = [output_own] + [
        swap(output_own, slot) for slot in range(1, head_count - 1)
    ]
    one_parts = [
        sum(
            contract(
                own_rows(grad_projected, slot)[:, part * head_width : (part + 1) * head_width],
                w_qkv[:, part],
                1,
                1,
            )
            for part in range(3)
        )
        for slot in range(head_count)
    ]
    one_parts[1:] = [v.astype(bf16) for v in one_parts[1:]]
    one_parts, total_out, output_slots = lax.optimization_barrier(
        (one_parts, total_out, output_slots)
    )
    one_parts = scatter_heads(one_parts)
    total_out = scatter_places(total_out)

    grad_one = sum([v.astype(f32) for v in one_parts[1:]], one_parts[0]) + grad_pooled_own
    back_one, gain_one = normalize_back(grad_one, hat_own, inverse_own, gain_attn)
    tokens_back = (grad_hidden + back_one).astype(bf16)
    gains = butterfly(jnp.stack([gain_one, gain_two]), "heads", head_count)
    tokens_back, total_qkv, total_out, gains = lax.optimization_barrier(
        (tokens_back, total_qkv, total_out, gains)
    )
    total_qkv = lax.all_gather(total_qkv, "seq", axis=0, tiled=True)
    token_slots = gather_heads(tokens_back)
    grad_out = gather_seq(total_out).astype(f32)
    grad_qkv = jnp.stack(
        [
            total_qkv[:, part * head_width : (part + 1) * head_width].astype(f32)
            for part in range(3)
        ],
        axis=1,
    )
    token_slots, gains, output_slots = lax.optimization_barrier(
        (token_slots, gains, output_slots)
    )
    output_slots.append(swap(output_slots[0], head_count - 1))
    output = in_order(output_slots, bf16)
    gains = butterfly(gains, "seq", seq_count)
    grad_tokens = in_order(token_slots, f32)
    return (
        output,
        grad_tokens,
        grad_qkv,
        grad_out,
        grad_up,
        grad_down,
        gains[0],
        gains[1],
        grad_router,
    )


def solution(mesh):
    return jax.shard_map(
        local,
        mesh=mesh,
        in_specs=(
            P("seq", None),
            P(None, None, "heads"),
            P("heads", None),
            P("seq", "heads"),
            P("heads", "seq"),
            P(),
            P(),
            P(),
            P(),
            P(),
            P(),
            P("seq", None),
        ),
        out_specs=(
            P("seq", None),
            P("seq", None),
            P(None, None, "heads"),
            P("heads", None),
            P("seq", "heads"),
            P("heads", "seq"),
            P(),
            P(),
            P(),
        ),
        check_vma=False,
    )
```

```python
import functools

import jax
import jax.numpy as jnp
from jax import lax
from jax.experimental import pallas as pl
from jax.experimental.pallas import tpu as pltpu
from jax.sharding import PartitionSpec as P

D = 2048
H = 16
HD = 128
FF = 8192
SHORT_DEV = 128
NSHORT = 3
NLONG = 2
LEVELS = 4
SEQS = 5
CHUNKS = NSHORT + 2 * NLONG

epsilon = 1e-05
highest = lax.Precision.HIGHEST
f32 = jnp.float32
bf16 = jnp.bfloat16
SCALE = HD ** (-0.5)


def dot(left, right):
    return jnp.dot(left, right, preferred_element_type=f32)


def contract(left, right, left_dim, right_dim):
    return lax.dot_general(
        left, right, (((left_dim,), (right_dim,)), ((), ())), preferred_element_type=f32
    )


def normalize_parts(values):
    centered = values - jnp.mean(values, axis=-1, keepdims=True)
    inverse = lax.rsqrt(jnp.mean(centered * centered, axis=-1, keepdims=True) + epsilon)
    return (centered * inverse, inverse)


def normalize_back(grad_normed, normed_hat, inverse, gain):
    grad_hat = grad_normed * gain
    middle = (
        grad_hat
        - jnp.mean(grad_hat, axis=-1, keepdims=True)
        - normed_hat * jnp.mean(grad_hat * normed_hat, axis=-1, keepdims=True)
    )
    return (inverse * middle, jnp.sum(grad_normed * normed_hat, axis=0))


def flip(values, axis, size, bit):
    return lax.ppermute(values, axis, [(i, i ^ bit) for i in range(size)])


def butterfly(values, axis, size):
    bit = 1
    while bit < size:
        values = values + flip(values, axis, size, bit)
        bit *= 2
    return values


def key_copies(scal, own, others, keys_short, keys_long, sems, members, heads):
    head, member = scal[0], scal[1]
    copies = []
    for part in range(members):
        source = own if part == 0 else others[(part - 1) * heads : part * heads]
        whose = lax.rem(member + part, members)
        for slot in range(heads):
            block = (head ^ slot) * members + whose
            number = len(copies)
            copies.append(
                pltpu.make_async_copy(
                    source[slot].at[0:NSHORT, :, HD:], keys_short.at[:, block], sems.at[number]
                )
            )
            for index in range(NLONG):
                first = NSHORT + 2 * index
                number = len(copies)
                copies.append(
                    pltpu.make_async_copy(
                        source[slot].at[first : first + 2, :, HD:],
                        keys_long.at[index, block],
                        sems.at[number],
                    )
                )
    return copies


def row_copies(scal, slots, held, sems, heads, outward):
    head = scal[0]
    copies = []
    for slot in range(heads):
        ends = (slots[slot].at[:, :, 0:HD], held.at[head ^ slot])
        if outward:
            ends = ends[::-1]
        copies.append(pltpu.make_async_copy(ends[0], ends[1], sems.at[slot]))
    return copies


def sequence_loop(work):
    def short(index, carry):
        work(0, index, index, 1, index)
        return carry

    def long(index, carry):
        work(1, index, NSHORT + 2 * index, 2, NSHORT + index)
        return carry

    lax.fori_loop(0, NSHORT, short, 0)
    lax.fori_loop(0, NLONG, long, 0)


def allowed_mask(member, members, size):
    key_at = lax.broadcasted_iota(jnp.int32, (members * size, size), 0)
    query_at = lax.broadcasted_iota(jnp.int32, (members * size, size), 1) + member * size
    return key_at <= query_at


def attend_kernel(heads, members, scal, *refs):
    count = heads
    own = refs[:count]
    others = refs[count : members * count]
    rest = refs[members * count :]
    out_slots = rest[:count]
    log_ref = rest[count]
    queries, keys_short, keys_long, mixed, row_sems, key_sems = rest[count + 1 :]
    copies = row_copies(scal, own, queries, row_sems, heads, False)
    copies += key_copies(scal, own, others, keys_short, keys_long, key_sems, members, heads)
    for copy in copies:
        copy.start()
    for copy in copies:
        copy.wait()

    def work(kind, index, first, chunks, live_at):
        size = chunks * SHORT_DEV
        live = scal[2 + live_at].astype(f32)
        mask = allowed_mask(scal[1], members, size)
        for place in range(heads):
            span = (place + 1) * members
            if kind == 0:
                block = keys_short[index, 0:span]
            else:
                block = keys_long[index, 0:span]
            block = block.reshape(span * size, 2 * HD)
            keys, values = block[:, :HD], block[:, HD:]
            query = queries[place, pl.ds(first, chunks)].reshape(size, HD)
            scores = contract(keys, query, 1, 1) * SCALE
            edge = place * members * size
            last = jnp.where(mask, scores[edge:], -1e30)
            largest = jnp.max(last, axis=0, keepdims=True)
            if place:
                early = scores[:edge]
                largest = jnp.maximum(largest, jnp.max(early, axis=0, keepdims=True))
            raised = jnp.exp(last - largest)
            total = jnp.sum(raised, axis=0, keepdims=True)
            low = raised.astype(bf16)
            turned = contract(values[edge:], low, 0, 0)
            if place:
                raised = jnp.exp(early - largest)
                total = total + jnp.sum(raised, axis=0, keepdims=True)
                turned = turned + contract(values[:edge], raised.astype(bf16), 0, 0)
            turned = turned * (live / total)
            mixed[place, pl.ds(first, chunks)] = (
                turned.T.astype(bf16).reshape(chunks, SHORT_DEV, HD)
            )
            logs = largest + jnp.log(total)
            for chunk in range(chunks):
                log_ref[place, first + chunk] = logs[:, chunk * SHORT_DEV : (chunk + 1) * SHORT_DEV]

    sequence_loop(work)
    copies = row_copies(scal, out_slots, mixed, row_sems, heads, True)
    for copy in copies:
        copy.start()
    for copy in copies:
        copy.wait()


def attend_forward(scal, own, others, heads, members):
    blocks = heads * members
    anywhere = pl.BlockSpec(memory_space=pl.ANY)
    result = pl.pallas_call(
        functools.partial(attend_kernel, heads, members),
        out_shape=[jax.ShapeDtypeStruct((CHUNKS, SHORT_DEV, HD), bf16)] * heads
        + [jax.ShapeDtypeStruct((heads, CHUNKS, 1, SHORT_DEV), f32)],
        in_specs=[pl.BlockSpec(memory_space=pltpu.SMEM)]
        + [anywhere] * (len(own) + len(others)),
        out_specs=[anywhere] * heads + [pl.BlockSpec(memory_space=pltpu.VMEM)],
        scratch_shapes=[
            pltpu.VMEM((heads, CHUNKS, SHORT_DEV, HD), bf16),
            pltpu.VMEM((NSHORT, blocks, SHORT_DEV, 2 * HD), bf16),
            pltpu.VMEM((NLONG, blocks, 2, SHORT_DEV, 2 * HD), bf16),
            pltpu.VMEM((heads, CHUNKS, SHORT_DEV, HD), bf16),
            pltpu.SemaphoreType.DMA((heads,)),
            pltpu.SemaphoreType.DMA((3 * blocks,)),
        ],
        compiler_params=pltpu.CompilerParams(vmem_limit_bytes=56 << 20),
        cost_estimate=pl.CostEstimate(
            flops=4 * 10**9, bytes_accessed=7 << 20, transcendentals=4 * 10**6
        ),
        name="attend_forward",
    )(scal, *own, *others)
    return (result[:heads], result[heads])


def back_kernel(heads, members, scal, *refs):
    count = heads
    own = refs[:count]
    others = refs[count : members * count]
    rest = refs[members * count :]
    grad_slots = rest[:count]
    log_ref = rest[count]
    rest = rest[count + 1 :]
    own_out = rest[:count]
    other_out = rest[count : count + members - 1]
    scratch = rest[count + members - 1 :]
    queries, keys_short, keys_long, grads, sum_short, sum_long = scratch[:6]
    low_short, low_long, zeros, row_sems, grad_sems, key_sems, zero_sems = scratch[6:]
    copies = row_copies(scal, own, queries, row_sems, heads, False)
    copies += row_copies(scal, grad_slots, grads, grad_sems, heads, False)
    copies += key_copies(scal, own, others, keys_short, keys_long, key_sems, members, heads)
    for copy in copies:
        copy.start()
    zeros[...] = jnp.zeros(zeros.shape, bf16)
    blanks = [
        pltpu.make_async_copy(
            zeros, other_out[part].at[slot, :, :, 0:HD], zero_sems.at[part * heads + slot]
        )
        for part in range(members - 1)
        for slot in range(heads)
    ]
    for copy in blanks:
        copy.start()
    for copy in copies:
        copy.wait()

    def work(kind, index, first, chunks, live_at):
        size = chunks * SHORT_DEV
        live = scal[2 + live_at].astype(bf16)
        mask = allowed_mask(scal[1], members, size)
        if kind == 0:
            keys_ref, sum_ref, low_ref = keys_short, sum_short, low_short
        else:
            keys_ref, sum_ref, low_ref = keys_long, sum_long, low_long
        for place in reversed(range(heads)):
            span = (place + 1) * members
            block = keys_ref[index, 0:span].reshape(span * size, 2 * HD)
            keys, values = block[:, :HD], block[:, HD:]
            query = queries[place, pl.ds(first, chunks)].reshape(size, HD)
            grad = grads[place, pl.ds(first, chunks)].reshape(size, HD) * live
            logs = jnp.concatenate(
                [log_ref[place, first + chunk] for chunk in range(chunks)], axis=1
            )
            probs = jnp.exp(contract(keys, query, 1, 1) * SCALE - logs)
            edge = place * members * size
            last = jnp.where(mask, probs[edge:], 0.0)
            probs = jnp.concatenate([probs[:edge], last], axis=0) if place else last
            grad_probs = contract(values, grad, 1, 1)
            delta = jnp.sum(probs * grad_probs, axis=0, keepdims=True)
            grad_scores = (probs * (grad_probs - delta)).astype(bf16)
            grad_value = dot(probs.astype(bf16), grad)
            grad_key = dot(grad_scores, query) * SCALE
            turned = contract(keys, grad_scores, 0, 0) * SCALE
            queries[place, pl.ds(first, chunks)] = (
                turned.T.astype(bf16).reshape(chunks, SHORT_DEV, HD)
            )
            pair = jnp.concatenate([grad_key, grad_value], axis=1)
            if place == heads - 1:
                sum_ref[...] = pair
            else:
                sum_ref[0 : span * size] += pair
        low_ref[index] = sum_ref[...].astype(bf16).reshape(low_ref.shape[1:])

    sequence_loop(work)
    copies = row_copies(scal, own_out, queries, row_sems, heads, True)
    head, member = scal[0], scal[1]
    number = 0
    for part in range(members):
        whose = lax.rem(member + part, members)
        for slot in range(heads):
            block = (head ^ slot) * members + whose
            target = own_out[slot] if part == 0 else other_out[part - 1].at[slot]
            copies.append(
                pltpu.make_async_copy(
                    low_short.at[:, block], target.at[0:NSHORT, :, HD:], key_sems.at[number]
                )
            )
            number += 1
            for index in range(NLONG):
                first = NSHORT + 2 * index
                copies.append(
                    pltpu.make_async_copy(
                        low_long.at[index, block],
                        target.at[first : first + 2, :, HD:],
                        key_sems.at[number],
                    )
                )
                number += 1
    for copy in copies:
        copy.start()
    for copy in blanks + copies:
        copy.wait()


def attend_backward(scal, own, others, grad_slots, logs, heads, members):
    blocks = heads * members
    anywhere = pl.BlockSpec(memory_space=pl.ANY)
    result = pl.pallas_call(
        functools.partial(back_kernel, heads, members),
        out_shape=[jax.ShapeDtypeStruct((CHUNKS, SHORT_DEV, 3 * HD), bf16)] * heads
        + [jax.ShapeDtypeStruct((heads, CHUNKS, SHORT_DEV, 3 * HD), bf16)] * (members - 1),
        in_specs=[pl.BlockSpec(memory_space=pltpu.SMEM)]
        + [anywhere] * (heads + blocks)
        + [pl.BlockSpec(memory_space=pltpu.VMEM)],
        out_specs=[anywhere] * (heads + members - 1),
        scratch_shapes=[
            pltpu.VMEM((heads, CHUNKS, SHORT_DEV, HD), bf16),
            pltpu.VMEM((NSHORT, blocks, SHORT_DEV, 2 * HD), bf16),
            pltpu.VMEM((NLONG, blocks, 2, SHORT_DEV, 2 * HD), bf16),
            pltpu.VMEM((heads, CHUNKS, SHORT_DEV, HD), bf16),
            pltpu.VMEM((blocks * SHORT_DEV, 2 * HD), f32),
            pltpu.VMEM((2 * blocks * SHORT_DEV, 2 * HD), f32),
            pltpu.VMEM((NSHORT, blocks, SHORT_DEV, 2 * HD), bf16),
            pltpu.VMEM((NLONG, blocks, 2, SHORT_DEV, 2 * HD), bf16),
            pltpu.VMEM((CHUNKS, SHORT_DEV, HD), bf16),
            pltpu.SemaphoreType.DMA((heads,)),
            pltpu.SemaphoreType.DMA((heads,)),
            pltpu.SemaphoreType.DMA((3 * blocks,)),
            pltpu.SemaphoreType.DMA(((members - 1) * heads,)),
        ],
        compiler_params=pltpu.CompilerParams(vmem_limit_bytes=60 << 20),
        cost_estimate=pl.CostEstimate(
            flops=10**10, bytes_accessed=12 << 20, transcendentals=4 * 10**6
        ),
        name="attend_backward",
    )(scal, *own, *others, *grad_slots, logs)
    return (result[:heads], result[heads:])


def rotate_rows(values, cosine, sine):
    return values * cosine + pltpu.roll(values, HD // 2, 1) * sine


def project_kernel(heads, scal, tokens, gain, cosine, sine, weights, *refs):
    slots = refs[:heads]
    normed, pooled = refs[heads : heads + 2]
    held_weights, acc, held, in_sems, out_sems = refs[heads + 2 :]
    head = scal[0]
    loads = [
        pltpu.make_async_copy(weights.at[part], held_weights.at[part], in_sems.at[part])
        for part in range(3)
    ]
    for load in loads:
        load.start()
    pooled[...] = jnp.zeros(pooled.shape, f32)

    def norm(chunk, carry):
        here = pl.ds(pl.multiple_of(chunk * SHORT_DEV, SHORT_DEV), SHORT_DEV)
        hat, _ = normalize_parts(tokens[here, :].astype(f32))
        values = hat * gain[...]
        normed[here, :] = values.astype(bf16)
        at = jnp.where(chunk < NSHORT, chunk, NSHORT + (chunk - NSHORT) // 2)
        rows = lax.broadcasted_iota(jnp.int32, pooled.shape, 0)
        added = jnp.sum(values, axis=0, keepdims=True)
        pooled[...] += jnp.where(rows == at, added, 0.0)
        return carry

    lax.fori_loop(0, CHUNKS, norm, 0)
    for part in range(3):
        loads[part].wait()
        acc[...] = dot(normed[...], held_weights[part])

        def spread(chunk, carry):
            here = pl.ds(pl.multiple_of(chunk * SHORT_DEV, SHORT_DEV), SHORT_DEV)
            for index in range(heads):
                values = acc[here, index * HD : (index + 1) * HD]
                if part < 2:
                    values = rotate_rows(values, cosine[here, :], sine[here, :])
                held[index, chunk, :, part * HD : (part + 1) * HD] = values.astype(bf16)
            return carry

        lax.fori_loop(0, CHUNKS, spread, 0)
    stores = [
        pltpu.make_async_copy(held.at[head ^ slot], slots[slot], out_sems.at[slot])
        for slot in range(heads)
    ]
    for store in stores:
        store.start()
    for store in stores:
        store.wait()


def project(scal, tokens, gain, cosine, sine, weights):
    rows = tokens.shape[0]
    width = weights.shape[2]
    heads = width // HD
    anywhere = pl.BlockSpec(memory_space=pl.ANY)
    inside = pl.BlockSpec(memory_space=pltpu.VMEM)
    result = pl.pallas_call(
        functools.partial(project_kernel, heads),
        out_shape=[jax.ShapeDtypeStruct((CHUNKS, SHORT_DEV, 3 * HD), bf16)] * heads
        + [jax.ShapeDtypeStruct((rows, D), bf16), jax.ShapeDtypeStruct((8, D), f32)],
        in_specs=[pl.BlockSpec(memory_space=pltpu.SMEM)] + [inside] * 4 + [anywhere],
        out_specs=[anywhere] * heads + [inside] * 2,
        scratch_shapes=[
            pltpu.VMEM((3, D, width), bf16),
            pltpu.VMEM((rows, width), f32),
            pltpu.VMEM((heads, CHUNKS, SHORT_DEV, 3 * HD), bf16),
            pltpu.SemaphoreType.DMA((3,)),
            pltpu.SemaphoreType.DMA((heads,)),
        ],
        compiler_params=pltpu.CompilerParams(vmem_limit_bytes=50 << 20),
        cost_estimate=pl.CostEstimate(
            flops=6 * rows * D * width, bytes_accessed=16 << 20, transcendentals=rows
        ),
        name="project",
    )(scal, tokens, gain, cosine, sine, weights)
    return (result[:heads], result[heads], result[heads + 1])


def gather_kernel(heads, scal, cosine, sine, *refs):
    slots = refs[:heads]
    out, held, sems = refs[heads:]
    copies = [
        pltpu.make_async_copy(slots[slot], held.at[scal[0] ^ slot], sems.at[slot])
        for slot in range(heads)
    ]
    for copy in copies:
        copy.start()
    for copy in copies:
        copy.wait()

    def spread(chunk, carry):
        here = pl.ds(pl.multiple_of(chunk * SHORT_DEV, SHORT_DEV), SHORT_DEV)
        for index in range(heads):
            for part in range(3):
                values = held[index, chunk, :, part * HD : (part + 1) * HD]
                if part < 2:
                    values = rotate_rows(values.astype(f32), cosine[here, :], sine[here, :])
                at = (part * heads + index) * HD
                out[here, at : at + HD] = values.astype(bf16)
        return carry

    lax.fori_loop(0, CHUNKS, spread, 0)


def gather_grads(scal, cosine, sine, slots):
    heads = len(slots)
    rows = CHUNKS * SHORT_DEV
    inside = pl.BlockSpec(memory_space=pltpu.VMEM)
    return pl.pallas_call(
        functools.partial(gather_kernel, heads),
        out_shape=jax.ShapeDtypeStruct((rows, 3 * heads * HD), bf16),
        in_specs=[pl.BlockSpec(memory_space=pltpu.SMEM)]
        + [inside] * 2
        + [pl.BlockSpec(memory_space=pl.ANY)] * heads,
        out_specs=inside,
        scratch_shapes=[
            pltpu.VMEM((heads, CHUNKS, SHORT_DEV, 3 * HD), bf16),
            pltpu.SemaphoreType.DMA((heads,)),
        ],
        compiler_params=pltpu.CompilerParams(vmem_limit_bytes=24 << 20),
        cost_estimate=pl.CostEstimate(
            flops=10 * rows * heads * HD, bytes_accessed=6 << 20, transcendentals=0
        ),
        name="gather_grads",
    )(scal, cosine, sine, *slots)


def local(
    tokens,
    w_qkv,
    w_out,
    w_up,
    w_down,
    gain_attn,
    gain_ffn,
    w_router,
    head_quarters,
    ffn_quarters,
    router_targets,
    cotangent,
):
    rows = tokens.shape[0]
    seq_rank = lax.axis_index("seq")
    seq_count = lax.axis_size("seq")
    head_rank = lax.axis_index("heads")
    head_count = lax.axis_size("heads")
    head_width = w_out.shape[0]
    ffn_width = w_up.shape[1]
    heads = head_width // HD
    members = seq_count // heads
    place, member = seq_rank // members, seq_rank % members
    share = rows // head_count
    short_rows = NSHORT * SHORT_DEV

    def across(values, slot):
        pairs = [
            (h * members + m, (h ^ slot) * members + m)
            for h in range(heads)
            for m in range(members)
        ]
        return lax.ppermute(values, "seq", pairs)

    def exchange(slots):
        sent = [across(slots[slot], slot) for slot in reversed(range(1, heads))]
        return [slots[0]] + sent[::-1]

    def among(values, step):
        pairs = [
            (h * members + (m + step) % members, h * members + m)
            for h in range(heads)
            for m in range(members)
        ]
        return lax.ppermute(values, "seq", pairs)

    block = D // seq_count
    z_groups = [[h * members + m for h in range(heads)] for m in range(members)]

    def member_columns(values):
        parts = []
        for step in range(members):
            whose = (member + members - step) % members
            columns = [
                lax.dynamic_slice_in_dim(values, (h * members + whose) * block, block, 1)
                for h in range(heads)
            ]
            parts.append(jnp.concatenate(columns, axis=1))
        return parts

    def member_sum(parts, product):
        sent = [among(product(parts[step]).astype(bf16), step) for step in range(1, members)]
        return sum([v.astype(f32) for v in sent], product(parts[0]).astype(f32)).astype(bf16)

    def scatter_z(values, axis):
        return lax.psum_scatter(
            values, "seq", scatter_dimension=axis, tiled=True, axis_index_groups=z_groups
        )

    def scatter_members(values):
        size = values.shape[0] // members

        def piece(number):
            return lax.dynamic_slice_in_dim(values, number * size, size, 0)

        total = piece(member).astype(f32)
        for step in range(1, members):
            sent = piece((member + members - step) % members)
            total = total + among(sent, step).astype(f32)
        return total.astype(bf16)

    def scatter_places(values):
        size = values.shape[0] // heads
        pieces = [
            lax.dynamic_slice_in_dim(values, (place ^ slot) * size, size, 0) for slot in range(heads)
        ]
        pieces = [v.astype(f32) for v in exchange(pieces)]
        return sum(pieces[1:], pieces[0]).astype(bf16)

    def gather_seq(values):
        values = placed(exchange([values] * heads), place, 0)
        size = values.shape[0]
        full = jnp.zeros((size * members,) + values.shape[1:], values.dtype)
        for step in range(members):
            piece = among(values, step) if step else values
            at = (member + step) % members * size
            full = lax.dynamic_update_slice_in_dim(full, piece, at, 0)
        return full

    def swap(values, slot):
        return flip(values, "heads", head_count, slot)

    def own_rows(values, slot):
        return lax.dynamic_slice_in_dim(values, (head_rank ^ slot) * share, share, 0)

    def scatter_heads(parts):
        return [parts[0]] + [
            swap(parts[slot].astype(bf16), slot) for slot in range(1, head_count)
        ]

    def gather_heads(values):
        return [values] + [swap(values, slot) for slot in range(1, head_count)]

    def gather_doubling(values):
        slots = [values]
        bit = 1
        while bit < head_count:
            slots = slots + [swap(v, bit) for v in slots]
            bit *= 2
        return slots

    def in_order(slots, kind):
        full = jnp.zeros((rows,) + slots[0].shape[1:], kind)
        for slot in range(head_count):
            full = lax.dynamic_update_slice_in_dim(
                full, slots[slot].astype(kind), (head_rank ^ slot) * share, 0
            )
        return full

    def placed(slots, key, axis):
        size = slots[0].shape[axis]
        shape = list(slots[0].shape)
        shape[axis] = size * len(slots)
        full = jnp.zeros(shape, slots[0].dtype)
        for slot, values in enumerate(slots):
            full = lax.dynamic_update_slice_in_dim(full, values, (key ^ slot) * size, axis)
        return full

    half = ffn_width // 2
    first_up = lax.all_gather(w_up[:, :half], "seq", axis=0, tiled=True)
    out_slots = gather_heads(w_out)

    column = jnp.arange(rows)
    is_short = column < short_rows
    offset = column - short_rows
    seq_id = jnp.where(is_short, column // SHORT_DEV, NSHORT + offset // (2 * SHORT_DEV))
    position = jnp.where(
        is_short,
        seq_rank * SHORT_DEV + column % SHORT_DEV,
        seq_rank * 2 * SHORT_DEV + offset % (2 * SHORT_DEV),
    )
    in_seq = seq_id[:, None] == jnp.arange(SEQS)[None, :]
    seq_length = jnp.where(
        jnp.arange(SEQS) < NSHORT, SHORT_DEV * seq_count, 2 * SHORT_DEV * seq_count
    ).astype(f32)
    ffn_level = jnp.sum(jnp.where(in_seq, ffn_quarters[None, :], 0), axis=1)
    half_dim = HD // 2
    frequency = 10000.0 ** (-jnp.arange(half_dim, dtype=f32) * 2.0 / HD)
    angle = position.astype(f32)[:, None] * frequency[None, :]
    cosine = jnp.cos(angle)
    sine = jnp.sin(angle)
    cosine = jnp.concatenate([cosine, cosine], axis=1)
    sine = jnp.concatenate([-sine, sine], axis=1)
    my_head = head_rank * heads + place
    head_live = (my_head < head_quarters * (H // LEVELS)).astype(jnp.int32)
    scal = jnp.concatenate([jnp.stack([place, member]).astype(jnp.int32), head_live])

    slots, normed_low, pooled = project(
        scal, tokens, gain_attn[None, :], cosine, sine, w_qkv.transpose(1, 0, 2)
    )
    slots = exchange(slots)
    other_slots = [among(v, step) for step in range(1, members) for v in slots]
    tokens_own = own_rows(tokens, 0).astype(f32)
    hat_own, inverse_own = normalize_parts(tokens_own)
    cotangent_rel = jnp.concatenate(
        [own_rows(cotangent, slot) for slot in range(head_count)], axis=0
    )
    hops = []
    bit = 1
    while bit < seq_count:
        hops.append(bit)
        bit *= 2

    def hop(values, bits):
        for bit in bits:
            values = values + flip(values, "seq", seq_count, bit)
        return values

    pooled = pooled[:SEQS]
    early = (slots, other_slots, out_slots[:-1], w_up[:, half:], w_down)
    early = early + (hat_own, inverse_own, cotangent_rel, pooled, member_columns(cotangent_rel))
    early = lax.optimization_barrier(early)
    slots, other_slots, out_slots[:-1], own_up, own_down = early[:5]
    hat_own, inverse_own, cotangent_rel, pooled, cotangent_parts = early[5:]
    second_up = lax.all_gather(own_up, "seq", axis=0, tiled=True)
    full_down = lax.all_gather(own_down, "seq", axis=1, tiled=True)
    pooled = hop(pooled, hops[:-1])
    full_out = jnp.concatenate(out_slots, axis=0)
    mixed_slots, logs = attend_forward(scal, slots, other_slots, heads, members)
    mixed_slots = [across(v, slot) if slot else v for slot, v in enumerate(mixed_slots)]
    mixed_slots, pooled = lax.optimization_barrier((mixed_slots, pooled))
    pooled = hop(pooled, hops[-1:])
    mixed_slots = [v.reshape(rows, HD) for v in mixed_slots]
    heads_out = placed(mixed_slots, place, 1)

    heads_rel = [own_rows(heads_out, slot) for slot in range(head_count)]
    heads_own = jnp.concatenate(
        [heads_rel[0]] + [swap(heads_rel[slot], slot) for slot in range(1, head_count)], axis=1
    )
    hidden = tokens_own + dot(heads_own, full_out)
    hat_two, inverse_two = normalize_parts(hidden)
    normed_two = gather_heads((hat_two * gain_ffn).astype(bf16))

    level_rel = jnp.concatenate([own_rows(ffn_level, slot) for slot in range(head_count)])
    unit_index = head_rank * ffn_width + jnp.arange(ffn_width)
    ffn_live = (unit_index[None, :] < (level_rel * (FF // LEVELS))[:, None]).astype(f32)
    full_up = jnp.concatenate([first_up, second_up], axis=1)
    normed_two, pooled, full_up = lax.optimization_barrier((normed_two, pooled, full_up))
    normed_two = jnp.concatenate(normed_two, axis=0)
    upward = dot(normed_two, full_up)
    kept = jnp.maximum(upward, 0.0)
    active = (jnp.square(kept) * ffn_live).astype(bf16)
    grad_down_part = member_sum(cotangent_parts, lambda v: contract(active, v, 0, 0))
    cotangent_rel, kept, grad_down_part = lax.optimization_barrier(
        (cotangent_rel, kept, grad_down_part)
    )
    grad_active = contract(cotangent_rel, full_down, 1, 1).astype(bf16)
    grad_upward = (grad_active.astype(f32) * ffn_live * 2.0 * kept).astype(bf16)
    grad_down = scatter_z(grad_down_part, 1)
    two_parts = [
        contract(grad_upward[slot * share : (slot + 1) * share], full_up, 1, 1)
        for slot in range(head_count)
    ]
    two_parts = scatter_heads(two_parts)
    grad_up_parts = [
        contract(v, grad_upward, 0, 0).astype(bf16) for v in member_columns(normed_two)
    ]

    pooled = pooled * lax.rsqrt(seq_length)[:, None]
    logits = jnp.dot(pooled, w_router, precision=highest, preferred_element_type=f32)
    logit_grads = []
    for group in range(2):
        group_logits = logits[:, LEVELS * group : LEVELS * (group + 1)]
        raised = jnp.exp(group_logits - jnp.max(group_logits, axis=1, keepdims=True))
        chosen = (jnp.arange(LEVELS)[None, :] == router_targets[:, group][:, None]).astype(f32)
        logit_grads.append(raised / jnp.sum(raised, axis=1, keepdims=True) - chosen)
    grad_logits = jnp.concatenate(logit_grads, axis=1)
    grad_router = jnp.dot(pooled.T, grad_logits, precision=highest, preferred_element_type=f32)
    grad_pooled = (
        jnp.dot(grad_logits, w_router.T, precision=highest, preferred_element_type=f32)
        * lax.rsqrt(seq_length)[:, None]
    )
    member_own = own_rows(in_seq.astype(f32), 0)
    grad_pooled_own = jnp.dot(
        member_own, grad_pooled, precision=highest, preferred_element_type=f32
    )
    two_parts, grad_up_parts, grad_router, grad_pooled_own = lax.optimization_barrier(
        (two_parts, grad_up_parts, grad_router, grad_pooled_own)
    )
    grad_up_part = member_sum(grad_up_parts, lambda v: v)
    grad_up = scatter_z(grad_up_part, 0)

    grad_two = sum([v.astype(f32) for v in two_parts[1:]], two_parts[0])
    back_two, gain_two = normalize_back(grad_two, hat_two, inverse_two, gain_ffn)
    grad_hidden = own_rows(cotangent, 0).astype(f32) + back_two
    grad_attn_own = grad_hidden.astype(bf16)
    grad_mixed = contract(grad_attn_own, full_out, 1, 1).astype(bf16)
    grad_mixed = [
        grad_mixed[:, slot * head_width : (slot + 1) * head_width] for slot in range(head_count)
    ]
    active, grad_mixed = lax.optimization_barrier((active, grad_mixed))
    grad_mixed = [grad_mixed[0]] + [
        swap(grad_mixed[slot], slot) for slot in range(1, head_count)
    ]
    grad_heads = placed(grad_mixed, head_rank, 0)
    grad_heads, grad_attn_own = lax.optimization_barrier((grad_heads, grad_attn_own))
    grad_attn = gather_heads(grad_attn_own)
    grad_slots = []
    for slot in range(heads):
        piece = lax.dynamic_slice_in_dim(grad_heads, (place ^ slot) * HD, HD, 1)
        piece = piece.reshape(CHUNKS, SHORT_DEV, HD)
        grad_slots.append(across(piece, slot) if slot else piece)
    ffn_parts = [
        dot(active[slot * share : (slot + 1) * share], full_down) for slot in range(head_count)
    ]
    ffn_parts[1:] = [v.astype(bf16) for v in ffn_parts[1:]]
    grad_slots, ffn_parts = lax.optimization_barrier((grad_slots, ffn_parts))

    own_grads, other_grads = attend_backward(
        scal, slots, other_slots, grad_slots, logs, heads, members
    )
    own_grads, other_grads, grad_attn[:-1] = lax.optimization_barrier(
        (own_grads, other_grads, grad_attn[:-1])
    )
    other_grads = [
        among(v, members - step) for step, v in zip(range(1, members), other_grads)
    ]
    sums = []
    for slot in range(heads):
        total = own_grads[slot].astype(f32)
        sums.append(sum([v[slot].astype(f32) for v in other_grads], total).astype(bf16))
    sums, ffn_parts = lax.optimization_barrier((sums, ffn_parts))
    sums = exchange(sums)
    ffn_parts = scatter_heads(ffn_parts)
    grad_attn = jnp.concatenate(grad_attn, axis=0)
    grad_out_part = contract(jnp.concatenate(heads_rel, axis=0), grad_attn, 0, 0).astype(bf16)
    grad_out_part, sums, ffn_parts[:-1] = lax.optimization_barrier(
        (grad_out_part, sums, ffn_parts[:-1])
    )
    total_out = scatter_members(grad_out_part)
    grad_projected = gather_grads(scal, cosine, -sine, sums)
    grad_qkv_part = contract(normed_low, grad_projected, 0, 0).astype(bf16)
    grad_projected, grad_qkv_part, ffn_parts, grad_down, grad_up = lax.optimization_barrier(
        (grad_projected, grad_qkv_part, ffn_parts, grad_down, grad_up)
    )
    total_qkv = lax.psum_scatter(grad_qkv_part, "seq", scatter_dimension=0, tiled=True)
    grad_down, grad_up = grad_down.astype(f32), grad_up.astype(f32)
    output_own = (
        hidden + sum([v.astype(f32) for v in ffn_parts[1:]], ffn_parts[0])
    ).astype(bf16)
    output_slots = [output_own] + [
        swap(output_own, slot) for slot in range(1, head_count - 1)
    ]
    one_parts = [
        sum(
            contract(
                own_rows(grad_projected, slot)[:, part * head_width : (part + 1) * head_width],
                w_qkv[:, part],
                1,
                1,
            )
            for part in range(3)
        )
        for slot in range(head_count)
    ]
    one_parts[1:] = [v.astype(bf16) for v in one_parts[1:]]
    one_parts, total_out, output_slots = lax.optimization_barrier(
        (one_parts, total_out, output_slots)
    )
    one_parts = scatter_heads(one_parts)
    total_out = scatter_places(total_out)

    grad_one = sum([v.astype(f32) for v in one_parts[1:]], one_parts[0]) + grad_pooled_own
    back_one, gain_one = normalize_back(grad_one, hat_own, inverse_own, gain_attn)
    tokens_back = (grad_hidden + back_one).astype(bf16)
    gains = butterfly(jnp.stack([gain_one, gain_two]), "heads", head_count)
    tokens_back, total_qkv, total_out, gains = lax.optimization_barrier(
        (tokens_back, total_qkv, total_out, gains)
    )
    total_qkv = lax.all_gather(total_qkv, "seq", axis=0, tiled=True)
    token_slots = gather_heads(tokens_back)
    grad_out = gather_seq(total_out).astype(f32)
    grad_qkv = jnp.stack(
        [
            total_qkv[:, part * head_width : (part + 1) * head_width].astype(f32)
            for part in range(3)
        ],
        axis=1,
    )
    token_slots, gains, output_slots = lax.optimization_barrier(
        (token_slots, gains, output_slots)
    )
    output_slots.append(swap(output_slots[0], head_count - 1))
    output = in_order(output_slots, bf16)
    gains = butterfly(gains, "seq", seq_count)
    grad_tokens = in_order(token_slots, f32)
    return (
        output,
        grad_tokens,
        grad_qkv,
        grad_out,
        grad_up,
        grad_down,
        gains[0],
        gains[1],
        grad_router,
    )


def solution(mesh):
    return jax.shard_map(
        local,
        mesh=mesh,
        in_specs=(
            P("seq", None),
            P(None, None, "heads"),
            P("heads", None),
            P("seq", "heads"),
            P("heads", "seq"),
            P(),
            P(),
            P(),
            P(),
            P(),
            P(),
            P("seq", None),
        ),
        out_specs=(
            P("seq", None),
            P("seq", None),
            P(None, None, "heads"),
            P("heads", None),
            P("seq", "heads"),
            P("heads", "seq"),
            P(),
            P(),
            P(),
        ),
        check_vma=False,
    )
```

```python
import functools

import jax
import jax.numpy as jnp
from jax import lax
from jax.experimental import pallas as pl
from jax.experimental.pallas import tpu as pltpu
from jax.sharding import PartitionSpec as P

D = 2048
H = 16
HD = 128
FF = 8192
SHORT_DEV = 128
NSHORT = 3
NLONG = 2
LEVELS = 4
SEQS = 5
CHUNKS = NSHORT + 2 * NLONG

epsilon = 1e-05
highest = lax.Precision.HIGHEST
f32 = jnp.float32
bf16 = jnp.bfloat16
SCALE = HD ** (-0.5)


def dot(left, right):
    return jnp.dot(left, right, preferred_element_type=f32)


def contract(left, right, left_dim, right_dim):
    return lax.dot_general(
        left, right, (((left_dim,), (right_dim,)), ((), ())), preferred_element_type=f32
    )


def normalize_parts(values):
    centered = values - jnp.mean(values, axis=-1, keepdims=True)
    inverse = lax.rsqrt(jnp.mean(centered * centered, axis=-1, keepdims=True) + epsilon)
    return (centered * inverse, inverse)


def normalize_back(grad_normed, normed_hat, inverse, gain):
    grad_hat = grad_normed * gain
    middle = (
        grad_hat
        - jnp.mean(grad_hat, axis=-1, keepdims=True)
        - normed_hat * jnp.mean(grad_hat * normed_hat, axis=-1, keepdims=True)
    )
    return (inverse * middle, jnp.sum(grad_normed * normed_hat, axis=0))


def flip(values, axis, size, bit):
    return lax.ppermute(values, axis, [(i, i ^ bit) for i in range(size)])


def butterfly(values, axis, size):
    bit = 1
    while bit < size:
        values = values + flip(values, axis, size, bit)
        bit *= 2
    return values


def key_copies(scal, own, others, keys_short, keys_long, sems, members, heads):
    head, member = scal[0], scal[1]
    copies = []
    for part in range(members):
        source = own if part == 0 else others[(part - 1) * heads : part * heads]
        whose = lax.rem(member + part, members)
        for slot in range(heads):
            block = (head ^ slot) * members + whose
            number = len(copies)
            copies.append(
                pltpu.make_async_copy(
                    source[slot].at[0:NSHORT, :, HD:], keys_short.at[:, block], sems.at[number]
                )
            )
            for index in range(NLONG):
                first = NSHORT + 2 * index
                number = len(copies)
                copies.append(
                    pltpu.make_async_copy(
                        source[slot].at[first : first + 2, :, HD:],
                        keys_long.at[index, block],
                        sems.at[number],
                    )
                )
    return copies


def row_copies(scal, slots, held, sems, heads, outward):
    head = scal[0]
    copies = []
    for slot in range(heads):
        ends = (slots[slot].at[:, :, 0:HD], held.at[head ^ slot])
        if outward:
            ends = ends[::-1]
        copies.append(pltpu.make_async_copy(ends[0], ends[1], sems.at[slot]))
    return copies


def sequence_loop(work):
    def short(index, carry):
        work(0, index, index, 1, index)
        return carry

    def long(index, carry):
        work(1, index, NSHORT + 2 * index, 2, NSHORT + index)
        return carry

    lax.fori_loop(0, NSHORT, short, 0)
    lax.fori_loop(0, NLONG, long, 0)


def allowed_mask(member, members, size):
    key_at = lax.broadcasted_iota(jnp.int32, (members * size, size), 0)
    query_at = lax.broadcasted_iota(jnp.int32, (members * size, size), 1) + member * size
    return key_at <= query_at


def attend_kernel(heads, members, scal, *refs):
    count = heads
    own = refs[:count]
    others = refs[count : members * count]
    rest = refs[members * count :]
    out_slots = rest[:count]
    log_ref = rest[count]
    queries, keys_short, keys_long, mixed, row_sems, key_sems = rest[count + 1 :]
    copies = row_copies(scal, own, queries, row_sems, heads, False)
    copies += key_copies(scal, own, others, keys_short, keys_long, key_sems, members, heads)
    for copy in copies:
        copy.start()
    for copy in copies:
        copy.wait()

    def work(kind, index, first, chunks, live_at):
        size = chunks * SHORT_DEV
        live = scal[2 + live_at].astype(f32)
        mask = allowed_mask(scal[1], members, size)
        for place in range(heads):
            span = (place + 1) * members
            if kind == 0:
                block = keys_short[index, 0:span]
            else:
                block = keys_long[index, 0:span]
            block = block.reshape(span * size, 2 * HD)
            keys, values = block[:, :HD], block[:, HD:]
            query = queries[place, pl.ds(first, chunks)].reshape(size, HD)
            scores = contract(keys, query, 1, 1) * SCALE
            edge = place * members * size
            last = jnp.where(mask, scores[edge:], -1e30)
            largest = jnp.max(last, axis=0, keepdims=True)
            if place:
                early = scores[:edge]
                largest = jnp.maximum(largest, jnp.max(early, axis=0, keepdims=True))
            raised = jnp.exp(last - largest)
            total = jnp.sum(raised, axis=0, keepdims=True)
            low = raised.astype(bf16)
            turned = contract(values[edge:], low, 0, 0)
            if place:
                raised = jnp.exp(early - largest)
                total = total + jnp.sum(raised, axis=0, keepdims=True)
                turned = turned + contract(values[:edge], raised.astype(bf16), 0, 0)
            turned = turned * (live / total)
            mixed[place, pl.ds(first, chunks)] = (
                turned.T.astype(bf16).reshape(chunks, SHORT_DEV, HD)
            )
            logs = largest + jnp.log(total)
            for chunk in range(chunks):
                log_ref[place, first + chunk] = logs[:, chunk * SHORT_DEV : (chunk + 1) * SHORT_DEV]

    sequence_loop(work)
    copies = row_copies(scal, out_slots, mixed, row_sems, heads, True)
    for copy in copies:
        copy.start()
    for copy in copies:
        copy.wait()


def attend_forward(scal, own, others, heads, members):
    blocks = heads * members
    anywhere = pl.BlockSpec(memory_space=pl.ANY)
    result = pl.pallas_call(
        functools.partial(attend_kernel, heads, members),
        out_shape=[jax.ShapeDtypeStruct((CHUNKS, SHORT_DEV, HD), bf16)] * heads
        + [jax.ShapeDtypeStruct((heads, CHUNKS, 1, SHORT_DEV), f32)],
        in_specs=[pl.BlockSpec(memory_space=pltpu.SMEM)]
        + [anywhere] * (len(own) + len(others)),
        out_specs=[anywhere] * heads + [pl.BlockSpec(memory_space=pltpu.VMEM)],
        scratch_shapes=[
            pltpu.VMEM((heads, CHUNKS, SHORT_DEV, HD), bf16),
            pltpu.VMEM((NSHORT, blocks, SHORT_DEV, 2 * HD), bf16),
            pltpu.VMEM((NLONG, blocks, 2, SHORT_DEV, 2 * HD), bf16),
            pltpu.VMEM((heads, CHUNKS, SHORT_DEV, HD), bf16),
            pltpu.SemaphoreType.DMA((heads,)),
            pltpu.SemaphoreType.DMA((3 * blocks,)),
        ],
        compiler_params=pltpu.CompilerParams(vmem_limit_bytes=56 << 20),
        cost_estimate=pl.CostEstimate(
            flops=4 * 10**9, bytes_accessed=7 << 20, transcendentals=4 * 10**6
        ),
        name="attend_forward",
    )(scal, *own, *others)
    return (result[:heads], result[heads])


def back_kernel(heads, members, scal, *refs):
    count = heads
    own = refs[:count]
    others = refs[count : members * count]
    rest = refs[members * count :]
    grad_slots = rest[:count]
    log_ref = rest[count]
    rest = rest[count + 1 :]
    own_out = rest[:count]
    other_out = rest[count : count + members - 1]
    scratch = rest[count + members - 1 :]
    queries, keys_short, keys_long, grads, sum_short, sum_long = scratch[:6]
    low_short, low_long, zeros, row_sems, grad_sems, key_sems, zero_sems = scratch[6:]
    copies = row_copies(scal, own, queries, row_sems, heads, False)
    copies += row_copies(scal, grad_slots, grads, grad_sems, heads, False)
    copies += key_copies(scal, own, others, keys_short, keys_long, key_sems, members, heads)
    for copy in copies:
        copy.start()
    zeros[...] = jnp.zeros(zeros.shape, bf16)
    blanks = [
        pltpu.make_async_copy(
            zeros, other_out[part].at[slot, :, :, 0:HD], zero_sems.at[part * heads + slot]
        )
        for part in range(members - 1)
        for slot in range(heads)
    ]
    for copy in blanks:
        copy.start()
    for copy in copies:
        copy.wait()

    def work(kind, index, first, chunks, live_at):
        size = chunks * SHORT_DEV
        live = scal[2 + live_at].astype(bf16)
        mask = allowed_mask(scal[1], members, size)
        if kind == 0:
            keys_ref, sum_ref, low_ref = keys_short, sum_short, low_short
        else:
            keys_ref, sum_ref, low_ref = keys_long, sum_long, low_long
        for place in reversed(range(heads)):
            span = (place + 1) * members
            block = keys_ref[index, 0:span].reshape(span * size, 2 * HD)
            keys, values = block[:, :HD], block[:, HD:]
            query = queries[place, pl.ds(first, chunks)].reshape(size, HD)
            grad = grads[place, pl.ds(first, chunks)].reshape(size, HD) * live
            logs = jnp.concatenate(
                [log_ref[place, first + chunk] for chunk in range(chunks)], axis=1
            )
            probs = jnp.exp(contract(keys, query, 1, 1) * SCALE - logs)
            edge = place * members * size
            last = jnp.where(mask, probs[edge:], 0.0)
            probs = jnp.concatenate([probs[:edge], last], axis=0) if place else last
            grad_probs = contract(values, grad, 1, 1)
            delta = jnp.sum(probs * grad_probs, axis=0, keepdims=True)
            grad_scores = (probs * (grad_probs - delta)).astype(bf16)
            grad_value = dot(probs.astype(bf16), grad)
            grad_key = dot(grad_scores, query) * SCALE
            turned = contract(keys, grad_scores, 0, 0) * SCALE
            queries[place, pl.ds(first, chunks)] = (
                turned.T.astype(bf16).reshape(chunks, SHORT_DEV, HD)
            )
            pair = jnp.concatenate([grad_key, grad_value], axis=1)
            if place == heads - 1:
                sum_ref[...] = pair
            else:
                sum_ref[0 : span * size] += pair
        low_ref[index] = sum_ref[...].astype(bf16).reshape(low_ref.shape[1:])

    sequence_loop(work)
    copies = row_copies(scal, own_out, queries, row_sems, heads, True)
    head, member = scal[0], scal[1]
    number = 0
    for part in range(members):
        whose = lax.rem(member + part, members)
        for slot in range(heads):
            block = (head ^ slot) * members + whose
            target = own_out[slot] if part == 0 else other_out[part - 1].at[slot]
            copies.append(
                pltpu.make_async_copy(
                    low_short.at[:, block], target.at[0:NSHORT, :, HD:], key_sems.at[number]
                )
            )
            number += 1
            for index in range(NLONG):
                first = NSHORT + 2 * index
                copies.append(
                    pltpu.make_async_copy(
                        low_long.at[index, block],
                        target.at[first : first + 2, :, HD:],
                        key_sems.at[number],
                    )
                )
                number += 1
    for copy in copies:
        copy.start()
    for copy in blanks + copies:
        copy.wait()


def attend_backward(scal, own, others, grad_slots, logs, heads, members):
    blocks = heads * members
    anywhere = pl.BlockSpec(memory_space=pl.ANY)
    result = pl.pallas_call(
        functools.partial(back_kernel, heads, members),
        out_shape=[jax.ShapeDtypeStruct((CHUNKS, SHORT_DEV, 3 * HD), bf16)] * heads
        + [jax.ShapeDtypeStruct((heads, CHUNKS, SHORT_DEV, 3 * HD), bf16)] * (members - 1),
        in_specs=[pl.BlockSpec(memory_space=pltpu.SMEM)]
        + [anywhere] * (heads + blocks)
        + [pl.BlockSpec(memory_space=pltpu.VMEM)],
        out_specs=[anywhere] * (heads + members - 1),
        scratch_shapes=[
            pltpu.VMEM((heads, CHUNKS, SHORT_DEV, HD), bf16),
            pltpu.VMEM((NSHORT, blocks, SHORT_DEV, 2 * HD), bf16),
            pltpu.VMEM((NLONG, blocks, 2, SHORT_DEV, 2 * HD), bf16),
            pltpu.VMEM((heads, CHUNKS, SHORT_DEV, HD), bf16),
            pltpu.VMEM((blocks * SHORT_DEV, 2 * HD), f32),
            pltpu.VMEM((2 * blocks * SHORT_DEV, 2 * HD), f32),
            pltpu.VMEM((NSHORT, blocks, SHORT_DEV, 2 * HD), bf16),
            pltpu.VMEM((NLONG, blocks, 2, SHORT_DEV, 2 * HD), bf16),
            pltpu.VMEM((CHUNKS, SHORT_DEV, HD), bf16),
            pltpu.SemaphoreType.DMA((heads,)),
            pltpu.SemaphoreType.DMA((heads,)),
            pltpu.SemaphoreType.DMA((3 * blocks,)),
            pltpu.SemaphoreType.DMA(((members - 1) * heads,)),
        ],
        compiler_params=pltpu.CompilerParams(vmem_limit_bytes=60 << 20),
        cost_estimate=pl.CostEstimate(
            flops=10**10, bytes_accessed=12 << 20, transcendentals=4 * 10**6
        ),
        name="attend_backward",
    )(scal, *own, *others, *grad_slots, logs)
    return (result[:heads], result[heads:])


def rotate_rows(values, cosine, sine):
    return values * cosine + pltpu.roll(values, HD // 2, 1) * sine


def project_kernel(heads, scal, tokens, gain, cosine, sine, weights, *refs):
    slots = refs[:heads]
    normed, pooled = refs[heads : heads + 2]
    held_weights, acc, held, in_sems, out_sems = refs[heads + 2 :]
    head = scal[0]
    loads = [
        pltpu.make_async_copy(weights.at[part], held_weights.at[part], in_sems.at[part])
        for part in range(3)
    ]
    for load in loads:
        load.start()
    pooled[...] = jnp.zeros(pooled.shape, f32)

    def norm(chunk, carry):
        here = pl.ds(pl.multiple_of(chunk * SHORT_DEV, SHORT_DEV), SHORT_DEV)
        hat, _ = normalize_parts(tokens[here, :].astype(f32))
        values = hat * gain[...]
        normed[here, :] = values.astype(bf16)
        at = jnp.where(chunk < NSHORT, chunk, NSHORT + (chunk - NSHORT) // 2)
        rows = lax.broadcasted_iota(jnp.int32, pooled.shape, 0)
        added = jnp.sum(values, axis=0, keepdims=True)
        pooled[...] += jnp.where(rows == at, added, 0.0)
        return carry

    lax.fori_loop(0, CHUNKS, norm, 0)
    for part in range(3):
        loads[part].wait()
        acc[...] = dot(normed[...], held_weights[part])

        def spread(chunk, carry):
            here = pl.ds(pl.multiple_of(chunk * SHORT_DEV, SHORT_DEV), SHORT_DEV)
            for index in range(heads):
                values = acc[here, index * HD : (index + 1) * HD]
                if part < 2:
                    values = rotate_rows(values, cosine[here, :], sine[here, :])
                held[index, chunk, :, part * HD : (part + 1) * HD] = values.astype(bf16)
            return carry

        lax.fori_loop(0, CHUNKS, spread, 0)
    stores = [
        pltpu.make_async_copy(held.at[head ^ slot], slots[slot], out_sems.at[slot])
        for slot in range(heads)
    ]
    for store in stores:
        store.start()
    for store in stores:
        store.wait()


def project(scal, tokens, gain, cosine, sine, weights):
    rows = tokens.shape[0]
    width = weights.shape[2]
    heads = width // HD
    anywhere = pl.BlockSpec(memory_space=pl.ANY)
    inside = pl.BlockSpec(memory_space=pltpu.VMEM)
    result = pl.pallas_call(
        functools.partial(project_kernel, heads),
        out_shape=[jax.ShapeDtypeStruct((CHUNKS, SHORT_DEV, 3 * HD), bf16)] * heads
        + [jax.ShapeDtypeStruct((rows, D), bf16), jax.ShapeDtypeStruct((8, D), f32)],
        in_specs=[pl.BlockSpec(memory_space=pltpu.SMEM)] + [inside] * 4 + [anywhere],
        out_specs=[anywhere] * heads + [inside] * 2,
        scratch_shapes=[
            pltpu.VMEM((3, D, width), bf16),
            pltpu.VMEM((rows, width), f32),
            pltpu.VMEM((heads, CHUNKS, SHORT_DEV, 3 * HD), bf16),
            pltpu.SemaphoreType.DMA((3,)),
            pltpu.SemaphoreType.DMA((heads,)),
        ],
        compiler_params=pltpu.CompilerParams(vmem_limit_bytes=50 << 20),
        cost_estimate=pl.CostEstimate(
            flops=6 * rows * D * width, bytes_accessed=16 << 20, transcendentals=rows
        ),
        name="project",
    )(scal, tokens, gain, cosine, sine, weights)
    return (result[:heads], result[heads], result[heads + 1])


def gather_kernel(heads, scal, cosine, sine, *refs):
    slots = refs[:heads]
    out, held, sems = refs[heads:]
    copies = [
        pltpu.make_async_copy(slots[slot], held.at[scal[0] ^ slot], sems.at[slot])
        for slot in range(heads)
    ]
    for copy in copies:
        copy.start()
    for copy in copies:
        copy.wait()

    def spread(chunk, carry):
        here = pl.ds(pl.multiple_of(chunk * SHORT_DEV, SHORT_DEV), SHORT_DEV)
        for index in range(heads):
            for part in range(3):
                values = held[index, chunk, :, part * HD : (part + 1) * HD]
                if part < 2:
                    values = rotate_rows(values.astype(f32), cosine[here, :], sine[here, :])
                at = (part * heads + index) * HD
                out[here, at : at + HD] = values.astype(bf16)
        return carry

    lax.fori_loop(0, CHUNKS, spread, 0)


def gather_grads(scal, cosine, sine, slots):
    heads = len(slots)
    rows = CHUNKS * SHORT_DEV
    inside = pl.BlockSpec(memory_space=pltpu.VMEM)
    return pl.pallas_call(
        functools.partial(gather_kernel, heads),
        out_shape=jax.ShapeDtypeStruct((rows, 3 * heads * HD), bf16),
        in_specs=[pl.BlockSpec(memory_space=pltpu.SMEM)]
        + [inside] * 2
        + [pl.BlockSpec(memory_space=pl.ANY)] * heads,
        out_specs=inside,
        scratch_shapes=[
            pltpu.VMEM((heads, CHUNKS, SHORT_DEV, 3 * HD), bf16),
            pltpu.SemaphoreType.DMA((heads,)),
        ],
        compiler_params=pltpu.CompilerParams(vmem_limit_bytes=24 << 20),
        cost_estimate=pl.CostEstimate(
            flops=10 * rows * heads * HD, bytes_accessed=6 << 20, transcendentals=0
        ),
        name="gather_grads",
    )(scal, cosine, sine, *slots)


def local(
    tokens,
    w_qkv,
    w_out,
    w_up,
    w_down,
    gain_attn,
    gain_ffn,
    w_router,
    head_quarters,
    ffn_quarters,
    router_targets,
    cotangent,
):
    rows = tokens.shape[0]
    seq_rank = lax.axis_index("seq")
    seq_count = lax.axis_size("seq")
    head_rank = lax.axis_index("heads")
    head_count = lax.axis_size("heads")
    head_width = w_out.shape[0]
    ffn_width = w_up.shape[1]
    heads = head_width // HD
    members = seq_count // heads
    place, member = seq_rank // members, seq_rank % members
    share = rows // head_count
    short_rows = NSHORT * SHORT_DEV

    def across(values, slot):
        pairs = [
            (h * members + m, (h ^ slot) * members + m)
            for h in range(heads)
            for m in range(members)
        ]
        return lax.ppermute(values, "seq", pairs)

    def exchange(slots):
        sent = [across(slots[slot], slot) for slot in reversed(range(1, heads))]
        return [slots[0]] + sent[::-1]

    def among(values, step):
        pairs = [
            (h * members + (m + step) % members, h * members + m)
            for h in range(heads)
            for m in range(members)
        ]
        return lax.ppermute(values, "seq", pairs)

    block = D // seq_count
    z_groups = [[h * members + m for h in range(heads)] for m in range(members)]

    def member_columns(values):
        parts = []
        for step in range(members):
            whose = (member + members - step) % members
            columns = [
                lax.dynamic_slice_in_dim(values, (h * members + whose) * block, block, 1)
                for h in range(heads)
            ]
            parts.append(jnp.concatenate(columns, axis=1))
        return parts

    def member_sum(parts, product):
        sent = [among(product(parts[step]).astype(bf16), step) for step in range(1, members)]
        return sum([v.astype(f32) for v in sent], product(parts[0]).astype(f32)).astype(bf16)

    def scatter_z(values, axis):
        return lax.psum_scatter(
            values, "seq", scatter_dimension=axis, tiled=True, axis_index_groups=z_groups
        )

    def scatter_members(values):
        size = values.shape[0] // members

        def piece(number):
            return lax.dynamic_slice_in_dim(values, number * size, size, 0)

        total = piece(member).astype(f32)
        for step in range(1, members):
            sent = piece((member + members - step) % members)
            total = total + among(sent, step).astype(f32)
        return total.astype(bf16)

    def scatter_places(values):
        size = values.shape[0] // heads
        held = {
            slot: lax.dynamic_slice_in_dim(values, (place ^ slot) * size, size, 0)
            for slot in range(heads)
        }
        bit = 1
        while bit < heads:
            slots = [slot for slot in sorted(held) if slot & bit]
            joined = jnp.concatenate([held[slot] for slot in slots], axis=0)
            joined = jnp.split(across(joined, bit), len(slots), axis=0)
            held = {
                slot ^ bit: (held[slot ^ bit].astype(f32) + v.astype(f32)).astype(bf16)
                for slot, v in zip(slots, joined)
            }
            bit *= 2
        return held[0]

    def gather_seq(values):
        held = {0: values}
        bit = heads // 2
        while bit:
            slots = sorted(held)
            joined = jnp.concatenate([held[slot] for slot in slots], axis=0)
            joined = jnp.split(across(joined, bit), len(slots), axis=0)
            held.update({slot ^ bit: v for slot, v in zip(slots, joined)})
            bit //= 2
        values = placed([held[slot] for slot in range(heads)], place, 0)
        size = values.shape[0]
        full = jnp.zeros((size * members,) + values.shape[1:], values.dtype)
        for step in range(members):
            piece = among(values, step) if step else values
            at = (member + step) % members * size
            full = lax.dynamic_update_slice_in_dim(full, piece, at, 0)
        return full

    def swap(values, slot):
        return flip(values, "heads", head_count, slot)

    def own_rows(values, slot):
        return lax.dynamic_slice_in_dim(values, (head_rank ^ slot) * share, share, 0)

    def scatter_heads(parts):
        return [parts[0]] + [
            swap(parts[slot].astype(bf16), slot) for slot in range(1, head_count)
        ]

    def gather_heads(values):
        return [values] + [swap(values, slot) for slot in range(1, head_count)]

    def gather_doubling(values):
        slots = [values]
        bit = 1
        while bit < head_count:
            slots = slots + [swap(v, bit) for v in slots]
            bit *= 2
        return slots

    def in_order(slots, kind):
        full = jnp.zeros((rows,) + slots[0].shape[1:], kind)
        for slot in range(head_count):
            full = lax.dynamic_update_slice_in_dim(
                full, slots[slot].astype(kind), (head_rank ^ slot) * share, 0
            )
        return full

    def placed(slots, key, axis):
        size = slots[0].shape[axis]
        shape = list(slots[0].shape)
        shape[axis] = size * len(slots)
        full = jnp.zeros(shape, slots[0].dtype)
        for slot, values in enumerate(slots):
            full = lax.dynamic_update_slice_in_dim(full, values, (key ^ slot) * size, axis)
        return full

    half = ffn_width // 2
    first_up = lax.all_gather(w_up[:, :half], "seq", axis=0, tiled=True)
    out_slots = gather_heads(w_out)

    column = jnp.arange(rows)
    is_short = column < short_rows
    offset = column - short_rows
    seq_id = jnp.where(is_short, column // SHORT_DEV, NSHORT + offset // (2 * SHORT_DEV))
    position = jnp.where(
        is_short,
        seq_rank * SHORT_DEV + column % SHORT_DEV,
        seq_rank * 2 * SHORT_DEV + offset % (2 * SHORT_DEV),
    )
    in_seq = seq_id[:, None] == jnp.arange(SEQS)[None, :]
    seq_length = jnp.where(
        jnp.arange(SEQS) < NSHORT, SHORT_DEV * seq_count, 2 * SHORT_DEV * seq_count
    ).astype(f32)
    ffn_level = jnp.sum(jnp.where(in_seq, ffn_quarters[None, :], 0), axis=1)
    half_dim = HD // 2
    frequency = 10000.0 ** (-jnp.arange(half_dim, dtype=f32) * 2.0 / HD)
    angle = position.astype(f32)[:, None] * frequency[None, :]
    cosine = jnp.cos(angle)
    sine = jnp.sin(angle)
    cosine = jnp.concatenate([cosine, cosine], axis=1)
    sine = jnp.concatenate([-sine, sine], axis=1)
    my_head = head_rank * heads + place
    head_live = (my_head < head_quarters * (H // LEVELS)).astype(jnp.int32)
    scal = jnp.concatenate([jnp.stack([place, member]).astype(jnp.int32), head_live])

    slots, normed_low, pooled = project(
        scal, tokens, gain_attn[None, :], cosine, sine, w_qkv.transpose(1, 0, 2)
    )
    slots = exchange(slots)
    other_slots = [among(v, step) for step in range(1, members) for v in slots]
    tokens_own = own_rows(tokens, 0).astype(f32)
    hat_own, inverse_own = normalize_parts(tokens_own)
    cotangent_rel = jnp.concatenate(
        [own_rows(cotangent, slot) for slot in range(head_count)], axis=0
    )
    hops = []
    bit = 1
    while bit < seq_count:
        hops.append(bit)
        bit *= 2

    def hop(values, bits):
        for bit in bits:
            values = values + flip(values, "seq", seq_count, bit)
        return values

    pooled = pooled[:SEQS]
    early = (slots, other_slots, out_slots[:-1], w_up[:, half:], w_down)
    early = early + (hat_own, inverse_own, cotangent_rel, pooled, member_columns(cotangent_rel))
    early = lax.optimization_barrier(early)
    slots, other_slots, out_slots[:-1], own_up, own_down = early[:5]
    hat_own, inverse_own, cotangent_rel, pooled, cotangent_parts = early[5:]
    second_up = lax.all_gather(own_up, "seq", axis=0, tiled=True)
    full_down = lax.all_gather(own_down, "seq", axis=1, tiled=True)
    pooled = hop(pooled, hops[:-1])
    full_out = jnp.concatenate(out_slots, axis=0)
    mixed_slots, logs = attend_forward(scal, slots, other_slots, heads, members)
    mixed_slots = [across(v, slot) if slot else v for slot, v in enumerate(mixed_slots)]
    mixed_slots, pooled = lax.optimization_barrier((mixed_slots, pooled))
    pooled = hop(pooled, hops[-1:])
    mixed_slots = [v.reshape(rows, HD) for v in mixed_slots]
    heads_out = placed(mixed_slots, place, 1)

    heads_rel = [own_rows(heads_out, slot) for slot in range(head_count)]
    heads_own = jnp.concatenate(
        [heads_rel[0]] + [swap(heads_rel[slot], slot) for slot in range(1, head_count)], axis=1
    )
    hidden = tokens_own + dot(heads_own, full_out)
    hat_two, inverse_two = normalize_parts(hidden)
    normed_two = gather_heads((hat_two * gain_ffn).astype(bf16))

    level_rel = jnp.concatenate([own_rows(ffn_level, slot) for slot in range(head_count)])
    unit_index = head_rank * ffn_width + jnp.arange(ffn_width)
    ffn_live = (unit_index[None, :] < (level_rel * (FF // LEVELS))[:, None]).astype(f32)
    full_up = jnp.concatenate([first_up, second_up], axis=1)
    normed_two, pooled, full_up = lax.optimization_barrier((normed_two, pooled, full_up))
    normed_two = jnp.concatenate(normed_two, axis=0)
    upward = dot(normed_two, full_up)
    kept = jnp.maximum(upward, 0.0)
    active = (jnp.square(kept) * ffn_live).astype(bf16)
    grad_down_part = member_sum(cotangent_parts, lambda v: contract(active, v, 0, 0))
    cotangent_rel, kept, grad_down_part = lax.optimization_barrier(
        (cotangent_rel, kept, grad_down_part)
    )
    grad_active = contract(cotangent_rel, full_down, 1, 1).astype(bf16)
    grad_upward = (grad_active.astype(f32) * ffn_live * 2.0 * kept).astype(bf16)
    grad_down = scatter_z(grad_down_part, 1)
    two_parts = [
        contract(grad_upward[slot * share : (slot + 1) * share], full_up, 1, 1)
        for slot in range(head_count)
    ]
    two_parts = scatter_heads(two_parts)
    grad_up_parts = [
        contract(v, grad_upward, 0, 0).astype(bf16) for v in member_columns(normed_two)
    ]

    pooled = pooled * lax.rsqrt(seq_length)[:, None]
    logits = jnp.dot(pooled, w_router, precision=highest, preferred_element_type=f32)
    logit_grads = []
    for group in range(2):
        group_logits = logits[:, LEVELS * group : LEVELS * (group + 1)]
        raised = jnp.exp(group_logits - jnp.max(group_logits, axis=1, keepdims=True))
        chosen = (jnp.arange(LEVELS)[None, :] == router_targets[:, group][:, None]).astype(f32)
        logit_grads.append(raised / jnp.sum(raised, axis=1, keepdims=True) - chosen)
    grad_logits = jnp.concatenate(logit_grads, axis=1)
    grad_router = jnp.dot(pooled.T, grad_logits, precision=highest, preferred_element_type=f32)
    grad_pooled = (
        jnp.dot(grad_logits, w_router.T, precision=highest, preferred_element_type=f32)
        * lax.rsqrt(seq_length)[:, None]
    )
    member_own = own_rows(in_seq.astype(f32), 0)
    grad_pooled_own = jnp.dot(
        member_own, grad_pooled, precision=highest, preferred_element_type=f32
    )
    two_parts, grad_up_parts, grad_router, grad_pooled_own = lax.optimization_barrier(
        (two_parts, grad_up_parts, grad_router, grad_pooled_own)
    )
    grad_up_part = member_sum(grad_up_parts, lambda v: v)
    grad_up = scatter_z(grad_up_part, 0)

    grad_two = sum([v.astype(f32) for v in two_parts[1:]], two_parts[0])
    back_two, gain_two = normalize_back(grad_two, hat_two, inverse_two, gain_ffn)
    grad_hidden = own_rows(cotangent, 0).astype(f32) + back_two
    grad_attn_own = grad_hidden.astype(bf16)
    grad_mixed = contract(grad_attn_own, full_out, 1, 1).astype(bf16)
    grad_mixed = [
        grad_mixed[:, slot * head_width : (slot + 1) * head_width] for slot in range(head_count)
    ]
    grad_mixed = [grad_mixed[0]] + [
        swap(grad_mixed[slot], slot) for slot in range(1, head_count)
    ]
    grad_heads = placed(grad_mixed, head_rank, 0)
    grad_heads, grad_attn_own, active = lax.optimization_barrier(
        (grad_heads, grad_attn_own, active)
    )
    grad_attn = gather_heads(grad_attn_own)
    grad_slots = []
    for slot in range(heads):
        piece = lax.dynamic_slice_in_dim(grad_heads, (place ^ slot) * HD, HD, 1)
        piece = piece.reshape(CHUNKS, SHORT_DEV, HD)
        grad_slots.append(across(piece, slot) if slot else piece)
    ffn_parts = [
        dot(active[slot * share : (slot + 1) * share], full_down) for slot in range(head_count)
    ]
    ffn_parts[1:] = [v.astype(bf16) for v in ffn_parts[1:]]
    grad_slots, ffn_parts = lax.optimization_barrier((grad_slots, ffn_parts))

    own_grads, other_grads = attend_backward(
        scal, slots, other_slots, grad_slots, logs, heads, members
    )
    own_grads, other_grads, grad_attn[:-1] = lax.optimization_barrier(
        (own_grads, other_grads, grad_attn[:-1])
    )
    other_grads = [
        among(v, members - step) for step, v in zip(range(1, members), other_grads)
    ]
    sums = []
    for slot in range(heads):
        total = own_grads[slot].astype(f32)
        sums.append(sum([v[slot].astype(f32) for v in other_grads], total).astype(bf16))
    sums, ffn_parts = lax.optimization_barrier((sums, ffn_parts))
    sums = exchange(sums)
    ffn_parts = scatter_heads(ffn_parts)
    grad_attn = jnp.concatenate(grad_attn, axis=0)
    grad_out_part = contract(jnp.concatenate(heads_rel, axis=0), grad_attn, 0, 0).astype(bf16)
    grad_out_part, sums, ffn_parts[:-1] = lax.optimization_barrier(
        (grad_out_part, sums, ffn_parts[:-1])
    )
    total_out = scatter_members(grad_out_part)
    grad_projected = gather_grads(scal, cosine, -sine, sums)
    grad_qkv_part = contract(normed_low, grad_projected, 0, 0).astype(bf16)
    grad_projected, grad_qkv_part, ffn_parts, grad_down, grad_up = lax.optimization_barrier(
        (grad_projected, grad_qkv_part, ffn_parts, grad_down, grad_up)
    )
    total_qkv = lax.psum_scatter(grad_qkv_part, "seq", scatter_dimension=0, tiled=True)
    grad_down, grad_up = grad_down.astype(f32), grad_up.astype(f32)
    output_own = (
        hidden + sum([v.astype(f32) for v in ffn_parts[1:]], ffn_parts[0])
    ).astype(bf16)
    output_slots = [output_own] + [
        swap(output_own, slot) for slot in range(1, head_count - 1)
    ]
    one_parts = [
        sum(
            contract(
                own_rows(grad_projected, slot)[:, part * head_width : (part + 1) * head_width],
                w_qkv[:, part],
                1,
                1,
            )
            for part in range(3)
        )
        for slot in range(head_count)
    ]
    one_parts[1:] = [v.astype(bf16) for v in one_parts[1:]]
    one_parts, total_out, output_slots = lax.optimization_barrier(
        (one_parts, total_out, output_slots)
    )
    one_parts = scatter_heads(one_parts)
    total_out = scatter_places(total_out)

    grad_one = sum([v.astype(f32) for v in one_parts[1:]], one_parts[0]) + grad_pooled_own
    back_one, gain_one = normalize_back(grad_one, hat_own, inverse_own, gain_attn)
    tokens_back = (grad_hidden + back_one).astype(bf16)
    gains = butterfly(jnp.stack([gain_one, gain_two]), "heads", head_count)
    tokens_back, total_qkv, total_out, gains = lax.optimization_barrier(
        (tokens_back, total_qkv, total_out, gains)
    )
    total_qkv = lax.all_gather(total_qkv, "seq", axis=0, tiled=True)
    token_slots = gather_heads(tokens_back)
    grad_out = gather_seq(total_out).astype(f32)
    grad_qkv = jnp.stack(
        [
            total_qkv[:, part * head_width : (part + 1) * head_width].astype(f32)
            for part in range(3)
        ],
        axis=1,
    )
    token_slots, gains, output_slots = lax.optimization_barrier(
        (token_slots, gains, output_slots)
    )
    output_slots.append(swap(output_slots[0], head_count - 1))
    output = in_order(output_slots, bf16)
    gains = butterfly(gains, "seq", seq_count)
    grad_tokens = in_order(token_slots, f32)
    return (
        output,
        grad_tokens,
        grad_qkv,
        grad_out,
        grad_up,
        grad_down,
        gains[0],
        gains[1],
        grad_router,
    )


def solution(mesh):
    return jax.shard_map(
        local,
        mesh=mesh,
        in_specs=(
            P("seq", None),
            P(None, None, "heads"),
            P("heads", None),
            P("seq", "heads"),
            P("heads", "seq"),
            P(),
            P(),
            P(),
            P(),
            P(),
            P(),
            P("seq", None),
        ),
        out_specs=(
            P("seq", None),
            P("seq", None),
            P(None, None, "heads"),
            P("heads", None),
            P("seq", "heads"),
            P("heads", "seq"),
            P(),
            P(),
            P(),
        ),
        check_vma=False,
    )
```

```python
import functools

import jax
import jax.numpy as jnp
from jax import lax
from jax.experimental import pallas as pl
from jax.experimental.pallas import tpu as pltpu
from jax.sharding import PartitionSpec as P

D = 2048
H = 16
HD = 128
FF = 8192
SHORT_DEV = 128
NSHORT = 3
NLONG = 2
LEVELS = 4
SEQS = 5
CHUNKS = NSHORT + 2 * NLONG

epsilon = 1e-05
highest = lax.Precision.HIGHEST
f32 = jnp.float32
bf16 = jnp.bfloat16
SCALE = HD ** (-0.5)


def dot(left, right):
    return jnp.dot(left, right, preferred_element_type=f32)


def contract(left, right, left_dim, right_dim):
    return lax.dot_general(
        left, right, (((left_dim,), (right_dim,)), ((), ())), preferred_element_type=f32
    )


def normalize_parts(values):
    centered = values - jnp.mean(values, axis=-1, keepdims=True)
    inverse = lax.rsqrt(jnp.mean(centered * centered, axis=-1, keepdims=True) + epsilon)
    return (centered * inverse, inverse)


def normalize_back(grad_normed, normed_hat, inverse, gain):
    grad_hat = grad_normed * gain
    middle = (
        grad_hat
        - jnp.mean(grad_hat, axis=-1, keepdims=True)
        - normed_hat * jnp.mean(grad_hat * normed_hat, axis=-1, keepdims=True)
    )
    return (inverse * middle, jnp.sum(grad_normed * normed_hat, axis=0))


def flip(values, axis, size, bit):
    return lax.ppermute(values, axis, [(i, i ^ bit) for i in range(size)])


def butterfly(values, axis, size):
    bit = 1
    while bit < size:
        values = values + flip(values, axis, size, bit)
        bit *= 2
    return values


def key_copies(scal, own, others, keys_short, keys_long, sems, members, heads):
    head, member = scal[0], scal[1]
    copies = []
    for part in range(members):
        source = own if part == 0 else others[(part - 1) * heads : part * heads]
        whose = lax.rem(member + part, members)
        for slot in range(heads):
            block = (head ^ slot) * members + whose
            number = len(copies)
            copies.append(
                pltpu.make_async_copy(
                    source[slot].at[0:NSHORT, :, HD:], keys_short.at[:, block], sems.at[number]
                )
            )
            for index in range(NLONG):
                first = NSHORT + 2 * index
                number = len(copies)
                copies.append(
                    pltpu.make_async_copy(
                        source[slot].at[first : first + 2, :, HD:],
                        keys_long.at[index, block],
                        sems.at[number],
                    )
                )
    return copies


def row_copies(scal, slots, held, sems, heads, outward):
    head = scal[0]
    copies = []
    for slot in range(heads):
        ends = (slots[slot].at[:, :, 0:HD], held.at[head ^ slot])
        if outward:
            ends = ends[::-1]
        copies.append(pltpu.make_async_copy(ends[0], ends[1], sems.at[slot]))
    return copies


def sequence_loop(work):
    def short(index, carry):
        work(0, index, index, 1, index)
        return carry

    def long(index, carry):
        work(1, index, NSHORT + 2 * index, 2, NSHORT + index)
        return carry

    lax.fori_loop(0, NSHORT, short, 0)
    lax.fori_loop(0, NLONG, long, 0)


def allowed_mask(member, members, size):
    key_at = lax.broadcasted_iota(jnp.int32, (members * size, size), 0)
    query_at = lax.broadcasted_iota(jnp.int32, (members * size, size), 1) + member * size
    return key_at <= query_at


def attend_kernel(heads, members, scal, *refs):
    count = heads
    own = refs[:count]
    others = refs[count : members * count]
    rest = refs[members * count :]
    out_slots = rest[:count]
    log_ref = rest[count]
    queries, keys_short, keys_long, mixed, row_sems, key_sems = rest[count + 1 :]
    copies = row_copies(scal, own, queries, row_sems, heads, False)
    copies += key_copies(scal, own, others, keys_short, keys_long, key_sems, members, heads)
    for copy in copies:
        copy.start()
    for copy in copies:
        copy.wait()

    def work(kind, index, first, chunks, live_at):
        size = chunks * SHORT_DEV
        live = scal[2 + live_at].astype(f32)
        mask = allowed_mask(scal[1], members, size)
        for place in range(heads):
            span = (place + 1) * members
            if kind == 0:
                block = keys_short[index, 0:span]
            else:
                block = keys_long[index, 0:span]
            block = block.reshape(span * size, 2 * HD)
            keys, values = block[:, :HD], block[:, HD:]
            query = queries[place, pl.ds(first, chunks)].reshape(size, HD)
            scores = contract(keys, query, 1, 1) * SCALE
            edge = place * members * size
            last = jnp.where(mask, scores[edge:], -1e30)
            largest = jnp.max(last, axis=0, keepdims=True)
            if place:
                early = scores[:edge]
                largest = jnp.maximum(largest, jnp.max(early, axis=0, keepdims=True))
            raised = jnp.exp(last - largest)
            total = jnp.sum(raised, axis=0, keepdims=True)
            low = raised.astype(bf16)
            turned = contract(values[edge:], low, 0, 0)
            if place:
                raised = jnp.exp(early - largest)
                total = total + jnp.sum(raised, axis=0, keepdims=True)
                turned = turned + contract(values[:edge], raised.astype(bf16), 0, 0)
            turned = turned * (live / total)
            mixed[place, pl.ds(first, chunks)] = (
                turned.T.astype(bf16).reshape(chunks, SHORT_DEV, HD)
            )
            logs = largest + jnp.log(total)
            for chunk in range(chunks):
                log_ref[place, first + chunk] = logs[:, chunk * SHORT_DEV : (chunk + 1) * SHORT_DEV]

    sequence_loop(work)
    copies = row_copies(scal, out_slots, mixed, row_sems, heads, True)
    for copy in copies:
        copy.start()
    for copy in copies:
        copy.wait()


def attend_forward(scal, own, others, heads, members):
    blocks = heads * members
    anywhere = pl.BlockSpec(memory_space=pl.ANY)
    result = pl.pallas_call(
        functools.partial(attend_kernel, heads, members),
        out_shape=[jax.ShapeDtypeStruct((CHUNKS, SHORT_DEV, HD), bf16)] * heads
        + [jax.ShapeDtypeStruct((heads, CHUNKS, 1, SHORT_DEV), f32)],
        in_specs=[pl.BlockSpec(memory_space=pltpu.SMEM)]
        + [anywhere] * (len(own) + len(others)),
        out_specs=[anywhere] * heads + [pl.BlockSpec(memory_space=pltpu.VMEM)],
        scratch_shapes=[
            pltpu.VMEM((heads, CHUNKS, SHORT_DEV, HD), bf16),
            pltpu.VMEM((NSHORT, blocks, SHORT_DEV, 2 * HD), bf16),
            pltpu.VMEM((NLONG, blocks, 2, SHORT_DEV, 2 * HD), bf16),
            pltpu.VMEM((heads, CHUNKS, SHORT_DEV, HD), bf16),
            pltpu.SemaphoreType.DMA((heads,)),
            pltpu.SemaphoreType.DMA((3 * blocks,)),
        ],
        compiler_params=pltpu.CompilerParams(vmem_limit_bytes=56 << 20),
        cost_estimate=pl.CostEstimate(
            flops=4 * 10**9, bytes_accessed=7 << 20, transcendentals=4 * 10**6
        ),
        name="attend_forward",
    )(scal, *own, *others)
    return (result[:heads], result[heads])


def back_kernel(heads, members, scal, *refs):
    count = heads
    own = refs[:count]
    others = refs[count : members * count]
    rest = refs[members * count :]
    grad_slots = rest[:count]
    log_ref = rest[count]
    rest = rest[count + 1 :]
    own_out = rest[:count]
    other_out = rest[count : count + members - 1]
    scratch = rest[count + members - 1 :]
    queries, keys_short, keys_long, grads, sum_short, sum_long = scratch[:6]
    low_short, low_long, zeros, row_sems, grad_sems, key_sems, zero_sems = scratch[6:]
    copies = row_copies(scal, own, queries, row_sems, heads, False)
    copies += row_copies(scal, grad_slots, grads, grad_sems, heads, False)
    copies += key_copies(scal, own, others, keys_short, keys_long, key_sems, members, heads)
    for copy in copies:
        copy.start()
    zeros[...] = jnp.zeros(zeros.shape, bf16)
    blanks = [
        pltpu.make_async_copy(
            zeros, other_out[part].at[slot, :, :, 0:HD], zero_sems.at[part * heads + slot]
        )
        for part in range(members - 1)
        for slot in range(heads)
    ]
    for copy in blanks:
        copy.start()
    for copy in copies:
        copy.wait()

    def work(kind, index, first, chunks, live_at):
        size = chunks * SHORT_DEV
        live = scal[2 + live_at].astype(bf16)
        mask = allowed_mask(scal[1], members, size)
        if kind == 0:
            keys_ref, sum_ref, low_ref = keys_short, sum_short, low_short
        else:
            keys_ref, sum_ref, low_ref = keys_long, sum_long, low_long
        for place in reversed(range(heads)):
            span = (place + 1) * members
            block = keys_ref[index, 0:span].reshape(span * size, 2 * HD)
            keys, values = block[:, :HD], block[:, HD:]
            query = queries[place, pl.ds(first, chunks)].reshape(size, HD)
            grad = grads[place, pl.ds(first, chunks)].reshape(size, HD) * live
            logs = jnp.concatenate(
                [log_ref[place, first + chunk] for chunk in range(chunks)], axis=1
            )
            probs = jnp.exp(contract(keys, query, 1, 1) * SCALE - logs)
            edge = place * members * size
            last = jnp.where(mask, probs[edge:], 0.0)
            probs = jnp.concatenate([probs[:edge], last], axis=0) if place else last
            grad_probs = contract(values, grad, 1, 1)
            delta = jnp.sum(probs * grad_probs, axis=0, keepdims=True)
            grad_scores = (probs * (grad_probs - delta)).astype(bf16)
            grad_value = dot(probs.astype(bf16), grad)
            grad_key = dot(grad_scores, query) * SCALE
            turned = contract(keys, grad_scores, 0, 0) * SCALE
            queries[place, pl.ds(first, chunks)] = (
                turned.T.astype(bf16).reshape(chunks, SHORT_DEV, HD)
            )
            pair = jnp.concatenate([grad_key, grad_value], axis=1)
            if place == heads - 1:
                sum_ref[...] = pair
            else:
                sum_ref[0 : span * size] += pair
        low_ref[index] = sum_ref[...].astype(bf16).reshape(low_ref.shape[1:])

    sequence_loop(work)
    copies = row_copies(scal, own_out, queries, row_sems, heads, True)
    head, member = scal[0], scal[1]
    number = 0
    for part in range(members):
        whose = lax.rem(member + part, members)
        for slot in range(heads):
            block = (head ^ slot) * members + whose
            target = own_out[slot] if part == 0 else other_out[part - 1].at[slot]
            copies.append(
                pltpu.make_async_copy(
                    low_short.at[:, block], target.at[0:NSHORT, :, HD:], key_sems.at[number]
                )
            )
            number += 1
            for index in range(NLONG):
                first = NSHORT + 2 * index
                copies.append(
                    pltpu.make_async_copy(
                        low_long.at[index, block],
                        target.at[first : first + 2, :, HD:],
                        key_sems.at[number],
                    )
                )
                number += 1
    for copy in copies:
        copy.start()
    for copy in blanks + copies:
        copy.wait()


def attend_backward(scal, own, others, grad_slots, logs, heads, members):
    blocks = heads * members
    anywhere = pl.BlockSpec(memory_space=pl.ANY)
    result = pl.pallas_call(
        functools.partial(back_kernel, heads, members),
        out_shape=[jax.ShapeDtypeStruct((CHUNKS, SHORT_DEV, 3 * HD), bf16)] * heads
        + [jax.ShapeDtypeStruct((heads, CHUNKS, SHORT_DEV, 3 * HD), bf16)] * (members - 1),
        in_specs=[pl.BlockSpec(memory_space=pltpu.SMEM)]
        + [anywhere] * (heads + blocks)
        + [pl.BlockSpec(memory_space=pltpu.VMEM)],
        out_specs=[anywhere] * (heads + members - 1),
        scratch_shapes=[
            pltpu.VMEM((heads, CHUNKS, SHORT_DEV, HD), bf16),
            pltpu.VMEM((NSHORT, blocks, SHORT_DEV, 2 * HD), bf16),
            pltpu.VMEM((NLONG, blocks, 2, SHORT_DEV, 2 * HD), bf16),
            pltpu.VMEM((heads, CHUNKS, SHORT_DEV, HD), bf16),
            pltpu.VMEM((blocks * SHORT_DEV, 2 * HD), f32),
            pltpu.VMEM((2 * blocks * SHORT_DEV, 2 * HD), f32),
            pltpu.VMEM((NSHORT, blocks, SHORT_DEV, 2 * HD), bf16),
            pltpu.VMEM((NLONG, blocks, 2, SHORT_DEV, 2 * HD), bf16),
            pltpu.VMEM((CHUNKS, SHORT_DEV, HD), bf16),
            pltpu.SemaphoreType.DMA((heads,)),
            pltpu.SemaphoreType.DMA((heads,)),
            pltpu.SemaphoreType.DMA((3 * blocks,)),
            pltpu.SemaphoreType.DMA(((members - 1) * heads,)),
        ],
        compiler_params=pltpu.CompilerParams(vmem_limit_bytes=60 << 20),
        cost_estimate=pl.CostEstimate(
            flops=10**10, bytes_accessed=12 << 20, transcendentals=4 * 10**6
        ),
        name="attend_backward",
    )(scal, *own, *others, *grad_slots, logs)
    return (result[:heads], result[heads:])


def rotate_rows(values, cosine, sine):
    return values * cosine + pltpu.roll(values, HD // 2, 1) * sine


def project_kernel(heads, scal, tokens, gain, cosine, sine, weights, *refs):
    slots = refs[:heads]
    normed, pooled = refs[heads : heads + 2]
    held_weights, acc, held, in_sems, out_sems = refs[heads + 2 :]
    head = scal[0]
    loads = [
        pltpu.make_async_copy(weights.at[part], held_weights.at[part], in_sems.at[part])
        for part in range(3)
    ]
    for load in loads:
        load.start()
    pooled[...] = jnp.zeros(pooled.shape, f32)

    def norm(chunk, carry):
        here = pl.ds(pl.multiple_of(chunk * SHORT_DEV, SHORT_DEV), SHORT_DEV)
        hat, _ = normalize_parts(tokens[here, :].astype(f32))
        values = hat * gain[...]
        normed[here, :] = values.astype(bf16)
        at = jnp.where(chunk < NSHORT, chunk, NSHORT + (chunk - NSHORT) // 2)
        rows = lax.broadcasted_iota(jnp.int32, pooled.shape, 0)
        added = jnp.sum(values, axis=0, keepdims=True)
        pooled[...] += jnp.where(rows == at, added, 0.0)
        return carry

    lax.fori_loop(0, CHUNKS, norm, 0)
    for part in range(3):
        loads[part].wait()
        acc[...] = dot(normed[...], held_weights[part])

        def spread(chunk, carry):
            here = pl.ds(pl.multiple_of(chunk * SHORT_DEV, SHORT_DEV), SHORT_DEV)
            for index in range(heads):
                values = acc[here, index * HD : (index + 1) * HD]
                if part < 2:
                    values = rotate_rows(values, cosine[here, :], sine[here, :])
                held[index, chunk, :, part * HD : (part + 1) * HD] = values.astype(bf16)
            return carry

        lax.fori_loop(0, CHUNKS, spread, 0)
    stores = [
        pltpu.make_async_copy(held.at[head ^ slot], slots[slot], out_sems.at[slot])
        for slot in range(heads)
    ]
    for store in stores:
        store.start()
    for store in stores:
        store.wait()


def project(scal, tokens, gain, cosine, sine, weights):
    rows = tokens.shape[0]
    width = weights.shape[2]
    heads = width // HD
    anywhere = pl.BlockSpec(memory_space=pl.ANY)
    inside = pl.BlockSpec(memory_space=pltpu.VMEM)
    result = pl.pallas_call(
        functools.partial(project_kernel, heads),
        out_shape=[jax.ShapeDtypeStruct((CHUNKS, SHORT_DEV, 3 * HD), bf16)] * heads
        + [jax.ShapeDtypeStruct((rows, D), bf16), jax.ShapeDtypeStruct((8, D), f32)],
        in_specs=[pl.BlockSpec(memory_space=pltpu.SMEM)] + [inside] * 4 + [anywhere],
        out_specs=[anywhere] * heads + [inside] * 2,
        scratch_shapes=[
            pltpu.VMEM((3, D, width), bf16),
            pltpu.VMEM((rows, width), f32),
            pltpu.VMEM((heads, CHUNKS, SHORT_DEV, 3 * HD), bf16),
            pltpu.SemaphoreType.DMA((3,)),
            pltpu.SemaphoreType.DMA((heads,)),
        ],
        compiler_params=pltpu.CompilerParams(vmem_limit_bytes=50 << 20),
        cost_estimate=pl.CostEstimate(
            flops=6 * rows * D * width, bytes_accessed=16 << 20, transcendentals=rows
        ),
        name="project",
    )(scal, tokens, gain, cosine, sine, weights)
    return (result[:heads], result[heads], result[heads + 1])


def gather_kernel(heads, scal, cosine, sine, *refs):
    slots = refs[:heads]
    out, held, sems = refs[heads:]
    copies = [
        pltpu.make_async_copy(slots[slot], held.at[scal[0] ^ slot], sems.at[slot])
        for slot in range(heads)
    ]
    for copy in copies:
        copy.start()
    for copy in copies:
        copy.wait()

    def spread(chunk, carry):
        here = pl.ds(pl.multiple_of(chunk * SHORT_DEV, SHORT_DEV), SHORT_DEV)
        for index in range(heads):
            for part in range(3):
                values = held[index, chunk, :, part * HD : (part + 1) * HD]
                if part < 2:
                    values = rotate_rows(values.astype(f32), cosine[here, :], sine[here, :])
                at = (part * heads + index) * HD
                out[here, at : at + HD] = values.astype(bf16)
        return carry

    lax.fori_loop(0, CHUNKS, spread, 0)


def gather_grads(scal, cosine, sine, slots):
    heads = len(slots)
    rows = CHUNKS * SHORT_DEV
    inside = pl.BlockSpec(memory_space=pltpu.VMEM)
    return pl.pallas_call(
        functools.partial(gather_kernel, heads),
        out_shape=jax.ShapeDtypeStruct((rows, 3 * heads * HD), bf16),
        in_specs=[pl.BlockSpec(memory_space=pltpu.SMEM)]
        + [inside] * 2
        + [pl.BlockSpec(memory_space=pl.ANY)] * heads,
        out_specs=inside,
        scratch_shapes=[
            pltpu.VMEM((heads, CHUNKS, SHORT_DEV, 3 * HD), bf16),
            pltpu.SemaphoreType.DMA((heads,)),
        ],
        compiler_params=pltpu.CompilerParams(vmem_limit_bytes=24 << 20),
        cost_estimate=pl.CostEstimate(
            flops=10 * rows * heads * HD, bytes_accessed=6 << 20, transcendentals=0
        ),
        name="gather_grads",
    )(scal, cosine, sine, *slots)


def local(
    tokens,
    w_qkv,
    w_out,
    w_up,
    w_down,
    gain_attn,
    gain_ffn,
    w_router,
    head_quarters,
    ffn_quarters,
    router_targets,
    cotangent,
):
    rows = tokens.shape[0]
    seq_rank = lax.axis_index("seq")
    seq_count = lax.axis_size("seq")
    head_rank = lax.axis_index("heads")
    head_count = lax.axis_size("heads")
    head_width = w_out.shape[0]
    ffn_width = w_up.shape[1]
    heads = head_width // HD
    members = seq_count // heads
    place, member = seq_rank // members, seq_rank % members
    share = rows // head_count
    short_rows = NSHORT * SHORT_DEV

    def across(values, slot):
        pairs = [
            (h * members + m, (h ^ slot) * members + m)
            for h in range(heads)
            for m in range(members)
        ]
        return lax.ppermute(values, "seq", pairs)

    def exchange(slots):
        sent = [across(slots[slot], slot) for slot in reversed(range(1, heads))]
        return [slots[0]] + sent[::-1]

    def among(values, step):
        pairs = [
            (h * members + (m + step) % members, h * members + m)
            for h in range(heads)
            for m in range(members)
        ]
        return lax.ppermute(values, "seq", pairs)

    block = D // seq_count
    z_groups = [[h * members + m for h in range(heads)] for m in range(members)]

    def member_columns(values):
        parts = []
        for step in range(members):
            whose = (member + members - step) % members
            columns = [
                lax.dynamic_slice_in_dim(values, (h * members + whose) * block, block, 1)
                for h in range(heads)
            ]
            parts.append(jnp.concatenate(columns, axis=1))
        return parts

    def member_sum(parts, product):
        sent = [among(product(parts[step]).astype(bf16), step) for step in range(1, members)]
        return sum([v.astype(f32) for v in sent], product(parts[0]).astype(f32)).astype(bf16)

    def scatter_z(values, axis):
        return lax.psum_scatter(
            values, "seq", scatter_dimension=axis, tiled=True, axis_index_groups=z_groups
        )

    def scatter_members(values):
        size = values.shape[0] // members

        def piece(number):
            return lax.dynamic_slice_in_dim(values, number * size, size, 0)

        total = piece(member).astype(f32)
        for step in range(1, members):
            sent = piece((member + members - step) % members)
            total = total + among(sent, step).astype(f32)
        return total.astype(bf16)

    def scatter_places(values):
        size = values.shape[0] // heads
        held = {
            slot: lax.dynamic_slice_in_dim(values, (place ^ slot) * size, size, 0)
            for slot in range(heads)
        }
        bit = 1
        while bit < heads:
            slots = [slot for slot in sorted(held) if slot & bit]
            joined = jnp.concatenate([held[slot] for slot in slots], axis=0)
            joined = jnp.split(across(joined, bit), len(slots), axis=0)
            held = {
                slot ^ bit: (held[slot ^ bit].astype(f32) + v.astype(f32)).astype(bf16)
                for slot, v in zip(slots, joined)
            }
            bit *= 2
        return held[0]

    def gather_seq(values):
        held = {0: values}
        bit = heads // 2
        while bit:
            slots = sorted(held)
            joined = jnp.concatenate([held[slot] for slot in slots], axis=0)
            joined = jnp.split(across(joined, bit), len(slots), axis=0)
            held.update({slot ^ bit: v for slot, v in zip(slots, joined)})
            bit //= 2
        values = placed([held[slot] for slot in range(heads)], place, 0)
        size = values.shape[0]
        full = jnp.zeros((size * members,) + values.shape[1:], values.dtype)
        for step in range(members):
            piece = among(values, step) if step else values
            at = (member + step) % members * size
            full = lax.dynamic_update_slice_in_dim(full, piece, at, 0)
        return full

    def swap(values, slot):
        return flip(values, "heads", head_count, slot)

    def own_rows(values, slot):
        return lax.dynamic_slice_in_dim(values, (head_rank ^ slot) * share, share, 0)

    def scatter_heads(parts):
        return [parts[0]] + [
            swap(parts[slot].astype(bf16), slot) for slot in range(1, head_count)
        ]

    def gather_heads(values):
        return [values] + [swap(values, slot) for slot in range(1, head_count)]

    def gather_doubling(values):
        slots = [values]
        bit = 1
        while bit < head_count:
            slots = slots + [swap(v, bit) for v in slots]
            bit *= 2
        return slots

    def in_order(slots, kind):
        full = jnp.zeros((rows,) + slots[0].shape[1:], kind)
        for slot in range(head_count):
            full = lax.dynamic_update_slice_in_dim(
                full, slots[slot].astype(kind), (head_rank ^ slot) * share, 0
            )
        return full

    def placed(slots, key, axis):
        size = slots[0].shape[axis]
        shape = list(slots[0].shape)
        shape[axis] = size * len(slots)
        full = jnp.zeros(shape, slots[0].dtype)
        for slot, values in enumerate(slots):
            full = lax.dynamic_update_slice_in_dim(full, values, (key ^ slot) * size, axis)
        return full

    half = ffn_width // 2
    first_up = lax.all_gather(w_up[:, :half], "seq", axis=0, tiled=True)
    out_slots = gather_heads(w_out)

    column = jnp.arange(rows)
    is_short = column < short_rows
    offset = column - short_rows
    seq_id = jnp.where(is_short, column // SHORT_DEV, NSHORT + offset // (2 * SHORT_DEV))
    position = jnp.where(
        is_short,
        seq_rank * SHORT_DEV + column % SHORT_DEV,
        seq_rank * 2 * SHORT_DEV + offset % (2 * SHORT_DEV),
    )
    in_seq = seq_id[:, None] == jnp.arange(SEQS)[None, :]
    seq_length = jnp.where(
        jnp.arange(SEQS) < NSHORT, SHORT_DEV * seq_count, 2 * SHORT_DEV * seq_count
    ).astype(f32)
    ffn_level = jnp.sum(jnp.where(in_seq, ffn_quarters[None, :], 0), axis=1)
    half_dim = HD // 2
    frequency = 10000.0 ** (-jnp.arange(half_dim, dtype=f32) * 2.0 / HD)
    angle = position.astype(f32)[:, None] * frequency[None, :]
    cosine = jnp.cos(angle)
    sine = jnp.sin(angle)
    cosine = jnp.concatenate([cosine, cosine], axis=1)
    sine = jnp.concatenate([-sine, sine], axis=1)
    my_head = head_rank * heads + place
    head_live = (my_head < head_quarters * (H // LEVELS)).astype(jnp.int32)
    scal = jnp.concatenate([jnp.stack([place, member]).astype(jnp.int32), head_live])

    slots, normed_low, pooled = project(
        scal, tokens, gain_attn[None, :], cosine, sine, w_qkv.transpose(1, 0, 2)
    )
    slots = exchange(slots)
    other_slots = [among(v, step) for step in range(1, members) for v in slots]
    tokens_own = own_rows(tokens, 0).astype(f32)
    hat_own, inverse_own = normalize_parts(tokens_own)
    cotangent_rel = jnp.concatenate(
        [own_rows(cotangent, slot) for slot in range(head_count)], axis=0
    )
    hops = []
    bit = 1
    while bit < seq_count:
        hops.append(bit)
        bit *= 2

    def hop(values, bits):
        for bit in bits:
            values = values + flip(values, "seq", seq_count, bit)
        return values

    pooled = pooled[:SEQS]
    early = (slots, other_slots, out_slots[:-1], w_up[:, half:], w_down)
    early = early + (hat_own, inverse_own, cotangent_rel, pooled, member_columns(cotangent_rel))
    early = lax.optimization_barrier(early)
    slots, other_slots, out_slots[:-1], own_up, own_down = early[:5]
    hat_own, inverse_own, cotangent_rel, pooled, cotangent_parts = early[5:]
    second_up = lax.all_gather(own_up, "seq", axis=0, tiled=True)
    full_down = lax.all_gather(own_down, "seq", axis=1, tiled=True)
    pooled = hop(pooled, hops[:-1])
    full_out = jnp.concatenate(out_slots, axis=0)
    mixed_slots, logs = attend_forward(scal, slots, other_slots, heads, members)
    mixed_slots = [across(v, slot) if slot else v for slot, v in enumerate(mixed_slots)]
    mixed_slots, pooled = lax.optimization_barrier((mixed_slots, pooled))
    pooled = hop(pooled, hops[-1:])
    mixed_slots = [v.reshape(rows, HD) for v in mixed_slots]
    heads_out = placed(mixed_slots, place, 1)

    heads_rel = [own_rows(heads_out, slot) for slot in range(head_count)]
    heads_own = jnp.concatenate(
        [heads_rel[0]] + [swap(heads_rel[slot], slot) for slot in range(1, head_count)], axis=1
    )
    hidden = tokens_own + dot(heads_own, full_out)
    hat_two, inverse_two = normalize_parts(hidden)
    normed_two = gather_heads((hat_two * gain_ffn).astype(bf16))

    level_rel = jnp.concatenate([own_rows(ffn_level, slot) for slot in range(head_count)])
    unit_index = head_rank * ffn_width + jnp.arange(ffn_width)
    ffn_live = (unit_index[None, :] < (level_rel * (FF // LEVELS))[:, None]).astype(f32)
    full_up = jnp.concatenate([first_up, second_up], axis=1)
    normed_two, pooled, full_up = lax.optimization_barrier((normed_two, pooled, full_up))
    normed_two = jnp.concatenate(normed_two, axis=0)
    upward = dot(normed_two, full_up)
    kept = jnp.maximum(upward, 0.0)
    active = (jnp.square(kept) * ffn_live).astype(bf16)
    grad_down_part = member_sum(cotangent_parts, lambda v: contract(active, v, 0, 0))
    cotangent_rel, kept, grad_down_part = lax.optimization_barrier(
        (cotangent_rel, kept, grad_down_part)
    )
    grad_active = contract(cotangent_rel, full_down, 1, 1).astype(bf16)
    grad_upward = (grad_active.astype(f32) * ffn_live * 2.0 * kept).astype(bf16)
    grad_down = scatter_z(grad_down_part, 1)
    two_parts = [
        contract(grad_upward[slot * share : (slot + 1) * share], full_up, 1, 1)
        for slot in range(head_count)
    ]
    two_parts = scatter_heads(two_parts)
    grad_up_parts = [
        contract(v, grad_upward, 0, 0).astype(bf16) for v in member_columns(normed_two)
    ]

    pooled = pooled * lax.rsqrt(seq_length)[:, None]
    logits = jnp.dot(pooled, w_router, precision=highest, preferred_element_type=f32)
    logit_grads = []
    for group in range(2):
        group_logits = logits[:, LEVELS * group : LEVELS * (group + 1)]
        raised = jnp.exp(group_logits - jnp.max(group_logits, axis=1, keepdims=True))
        chosen = (jnp.arange(LEVELS)[None, :] == router_targets[:, group][:, None]).astype(f32)
        logit_grads.append(raised / jnp.sum(raised, axis=1, keepdims=True) - chosen)
    grad_logits = jnp.concatenate(logit_grads, axis=1)
    grad_router = jnp.dot(pooled.T, grad_logits, precision=highest, preferred_element_type=f32)
    grad_pooled = (
        jnp.dot(grad_logits, w_router.T, precision=highest, preferred_element_type=f32)
        * lax.rsqrt(seq_length)[:, None]
    )
    member_own = own_rows(in_seq.astype(f32), 0)
    grad_pooled_own = jnp.dot(
        member_own, grad_pooled, precision=highest, preferred_element_type=f32
    )
    two_parts, grad_up_parts, grad_router, grad_pooled_own = lax.optimization_barrier(
        (two_parts, grad_up_parts, grad_router, grad_pooled_own)
    )
    grad_up_part = member_sum(grad_up_parts, lambda v: v)

    grad_two = sum([v.astype(f32) for v in two_parts[1:]], two_parts[0])
    back_two, gain_two = normalize_back(grad_two, hat_two, inverse_two, gain_ffn)
    grad_hidden = own_rows(cotangent, 0).astype(f32) + back_two
    grad_attn_own = grad_hidden.astype(bf16)
    grad_mixed = contract(grad_attn_own, full_out, 1, 1).astype(bf16)
    grad_mixed = [
        grad_mixed[:, slot * head_width : (slot + 1) * head_width] for slot in range(head_count)
    ]
    grad_mixed = [grad_mixed[0]] + [
        swap(grad_mixed[slot], slot) for slot in range(1, head_count)
    ]
    grad_heads = placed(grad_mixed, head_rank, 0)
    grad_heads, grad_attn_own, active, grad_up_part = lax.optimization_barrier(
        (grad_heads, grad_attn_own, active, grad_up_part)
    )
    grad_up = scatter_z(grad_up_part, 0)
    grad_attn = gather_heads(grad_attn_own)
    grad_slots = []
    for slot in range(heads):
        piece = lax.dynamic_slice_in_dim(grad_heads, (place ^ slot) * HD, HD, 1)
        piece = piece.reshape(CHUNKS, SHORT_DEV, HD)
        grad_slots.append(across(piece, slot) if slot else piece)
    ffn_parts = [
        dot(active[slot * share : (slot + 1) * share], full_down) for slot in range(head_count)
    ]
    ffn_parts[1:] = [v.astype(bf16) for v in ffn_parts[1:]]
    grad_slots, ffn_parts = lax.optimization_barrier((grad_slots, ffn_parts))

    own_grads, other_grads = attend_backward(
        scal, slots, other_slots, grad_slots, logs, heads, members
    )
    own_grads, other_grads, grad_attn[:-1] = lax.optimization_barrier(
        (own_grads, other_grads, grad_attn[:-1])
    )
    other_grads = [
        among(v, members - step) for step, v in zip(range(1, members), other_grads)
    ]
    sums = []
    for slot in range(heads):
        total = own_grads[slot].astype(f32)
        sums.append(sum([v[slot].astype(f32) for v in other_grads], total).astype(bf16))
    sums, ffn_parts = lax.optimization_barrier((sums, ffn_parts))
    sums = exchange(sums)
    ffn_parts = scatter_heads(ffn_parts)
    grad_attn = jnp.concatenate(grad_attn, axis=0)
    grad_out_part = contract(jnp.concatenate(heads_rel, axis=0), grad_attn, 0, 0).astype(bf16)
    grad_out_part, sums, ffn_parts[:-1] = lax.optimization_barrier(
        (grad_out_part, sums, ffn_parts[:-1])
    )
    total_out = scatter_members(grad_out_part)
    grad_projected = gather_grads(scal, cosine, -sine, sums)
    grad_qkv_part = contract(normed_low, grad_projected, 0, 0).astype(bf16)
    grad_projected, grad_qkv_part, ffn_parts, grad_down, grad_up = lax.optimization_barrier(
        (grad_projected, grad_qkv_part, ffn_parts, grad_down, grad_up)
    )
    total_qkv = lax.psum_scatter(grad_qkv_part, "seq", scatter_dimension=0, tiled=True)
    grad_down, grad_up = grad_down.astype(f32), grad_up.astype(f32)
    output_own = (
        hidden + sum([v.astype(f32) for v in ffn_parts[1:]], ffn_parts[0])
    ).astype(bf16)
    output_slots = [output_own] + [
        swap(output_own, slot) for slot in range(1, head_count - 1)
    ]
    one_parts = [
        sum(
            contract(
                own_rows(grad_projected, slot)[:, part * head_width : (part + 1) * head_width],
                w_qkv[:, part],
                1,
                1,
            )
            for part in range(3)
        )
        for slot in range(head_count)
    ]
    one_parts[1:] = [v.astype(bf16) for v in one_parts[1:]]
    one_parts, total_out, output_slots = lax.optimization_barrier(
        (one_parts, total_out, output_slots)
    )
    one_parts = scatter_heads(one_parts)
    total_out = scatter_places(total_out)

    one_parts, total_qkv, total_out, output_slots = lax.optimization_barrier(
        (one_parts, total_qkv, total_out, output_slots)
    )
    output_slots.append(swap(output_slots[0], head_count - 1))

    grad_one = sum([v.astype(f32) for v in one_parts[1:]], one_parts[0]) + grad_pooled_own
    back_one, gain_one = normalize_back(grad_one, hat_own, inverse_own, gain_attn)
    tokens_back = (grad_hidden + back_one).astype(bf16)
    gains = butterfly(jnp.stack([gain_one, gain_two]), "heads", head_count)
    tokens_back, gains = lax.optimization_barrier((tokens_back, gains))
    total_qkv = lax.all_gather(total_qkv, "seq", axis=0, tiled=True)
    token_slots = gather_heads(tokens_back)
    grad_out = gather_seq(total_out).astype(f32)
    grad_qkv = jnp.stack(
        [
            total_qkv[:, part * head_width : (part + 1) * head_width].astype(f32)
            for part in range(3)
        ],
        axis=1,
    )
    token_slots, gains = lax.optimization_barrier((token_slots, gains))
    output = in_order(output_slots, bf16)
    gains = butterfly(gains, "seq", seq_count)
    grad_tokens = in_order(token_slots, f32)
    return (
        output,
        grad_tokens,
        grad_qkv,
        grad_out,
        grad_up,
        grad_down,
        gains[0],
        gains[1],
        grad_router,
    )


def solution(mesh):
    return jax.shard_map(
        local,
        mesh=mesh,
        in_specs=(
            P("seq", None),
            P(None, None, "heads"),
            P("heads", None),
            P("seq", "heads"),
            P("heads", "seq"),
            P(),
            P(),
            P(),
            P(),
            P(),
            P(),
            P("seq", None),
        ),
        out_specs=(
            P("seq", None),
            P("seq", None),
            P(None, None, "heads"),
            P("heads", None),
            P("seq", "heads"),
            P("heads", "seq"),
            P(),
            P(),
            P(),
        ),
        check_vma=False,
    )
```

```python
import functools

import jax
import jax.numpy as jnp
from jax import lax
from jax.experimental import pallas as pl
from jax.experimental.pallas import tpu as pltpu
from jax.sharding import PartitionSpec as P

D = 2048
H = 16
HD = 128
FF = 8192
SHORT_DEV = 128
NSHORT = 3
NLONG = 2
LEVELS = 4
SEQS = 5
CHUNKS = NSHORT + 2 * NLONG

epsilon = 1e-05
highest = lax.Precision.HIGHEST
f32 = jnp.float32
bf16 = jnp.bfloat16
SCALE = HD ** (-0.5)


def dot(left, right):
    return jnp.dot(left, right, preferred_element_type=f32)


def contract(left, right, left_dim, right_dim):
    return lax.dot_general(
        left, right, (((left_dim,), (right_dim,)), ((), ())), preferred_element_type=f32
    )


def normalize_parts(values):
    centered = values - jnp.mean(values, axis=-1, keepdims=True)
    inverse = lax.rsqrt(jnp.mean(centered * centered, axis=-1, keepdims=True) + epsilon)
    return (centered * inverse, inverse)


def normalize_back(grad_normed, normed_hat, inverse, gain):
    grad_hat = grad_normed * gain
    middle = (
        grad_hat
        - jnp.mean(grad_hat, axis=-1, keepdims=True)
        - normed_hat * jnp.mean(grad_hat * normed_hat, axis=-1, keepdims=True)
    )
    return (inverse * middle, jnp.sum(grad_normed * normed_hat, axis=0))


def flip(values, axis, size, bit):
    return lax.ppermute(values, axis, [(i, i ^ bit) for i in range(size)])


def butterfly(values, axis, size):
    bit = 1
    while bit < size:
        values = values + flip(values, axis, size, bit)
        bit *= 2
    return values


def key_copies(scal, own, others, keys_short, keys_long, sems, members, heads):
    head, member = scal[0], scal[1]
    copies = []
    for part in range(members):
        source = own if part == 0 else others[(part - 1) * heads : part * heads]
        whose = lax.rem(member + part, members)
        for slot in range(heads):
            block = (head ^ slot) * members + whose
            number = len(copies)
            copies.append(
                pltpu.make_async_copy(
                    source[slot].at[0:NSHORT, :, HD:], keys_short.at[:, block], sems.at[number]
                )
            )
            for index in range(NLONG):
                first = NSHORT + 2 * index
                number = len(copies)
                copies.append(
                    pltpu.make_async_copy(
                        source[slot].at[first : first + 2, :, HD:],
                        keys_long.at[index, block],
                        sems.at[number],
                    )
                )
    return copies


def row_copies(scal, slots, held, sems, heads, outward):
    head = scal[0]
    copies = []
    for slot in range(heads):
        ends = (slots[slot].at[:, :, 0:HD], held.at[head ^ slot])
        if outward:
            ends = ends[::-1]
        copies.append(pltpu.make_async_copy(ends[0], ends[1], sems.at[slot]))
    return copies


def sequence_loop(work):
    def short(index, carry):
        work(0, index, index, 1, index)
        return carry

    def long(index, carry):
        work(1, index, NSHORT + 2 * index, 2, NSHORT + index)
        return carry

    lax.fori_loop(0, NSHORT, short, 0)
    lax.fori_loop(0, NLONG, long, 0)


def allowed_mask(member, members, size):
    key_at = lax.broadcasted_iota(jnp.int32, (members * size, size), 0)
    query_at = lax.broadcasted_iota(jnp.int32, (members * size, size), 1) + member * size
    return key_at <= query_at


def attend_kernel(heads, members, scal, *refs):
    count = heads
    own = refs[:count]
    others = refs[count : members * count]
    rest = refs[members * count :]
    out_slots = rest[:count]
    log_ref = rest[count]
    queries, keys_short, keys_long, mixed, row_sems, key_sems = rest[count + 1 :]
    copies = row_copies(scal, own, queries, row_sems, heads, False)
    copies += key_copies(scal, own, others, keys_short, keys_long, key_sems, members, heads)
    for copy in copies:
        copy.start()
    for copy in copies:
        copy.wait()

    def work(kind, index, first, chunks, live_at):
        size = chunks * SHORT_DEV
        live = scal[2 + live_at].astype(f32)
        mask = allowed_mask(scal[1], members, size)
        for place in range(heads):
            span = (place + 1) * members
            if kind == 0:
                block = keys_short[index, 0:span]
            else:
                block = keys_long[index, 0:span]
            block = block.reshape(span * size, 2 * HD)
            keys, values = block[:, :HD], block[:, HD:]
            query = queries[place, pl.ds(first, chunks)].reshape(size, HD)
            scores = contract(keys, query, 1, 1) * SCALE
            edge = place * members * size
            last = jnp.where(mask, scores[edge:], -1e30)
            largest = jnp.max(last, axis=0, keepdims=True)
            if place:
                early = scores[:edge]
                largest = jnp.maximum(largest, jnp.max(early, axis=0, keepdims=True))
            raised = jnp.exp(last - largest)
            total = jnp.sum(raised, axis=0, keepdims=True)
            low = raised.astype(bf16)
            turned = contract(values[edge:], low, 0, 0)
            if place:
                raised = jnp.exp(early - largest)
                total = total + jnp.sum(raised, axis=0, keepdims=True)
                turned = turned + contract(values[:edge], raised.astype(bf16), 0, 0)
            turned = turned * (live / total)
            mixed[place, pl.ds(first, chunks)] = (
                turned.T.astype(bf16).reshape(chunks, SHORT_DEV, HD)
            )
            logs = largest + jnp.log(total)
            for chunk in range(chunks):
                log_ref[place, first + chunk] = logs[:, chunk * SHORT_DEV : (chunk + 1) * SHORT_DEV]

    sequence_loop(work)
    copies = row_copies(scal, out_slots, mixed, row_sems, heads, True)
    for copy in copies:
        copy.start()
    for copy in copies:
        copy.wait()


def attend_forward(scal, own, others, heads, members):
    blocks = heads * members
    anywhere = pl.BlockSpec(memory_space=pl.ANY)
    result = pl.pallas_call(
        functools.partial(attend_kernel, heads, members),
        out_shape=[jax.ShapeDtypeStruct((CHUNKS, SHORT_DEV, HD), bf16)] * heads
        + [jax.ShapeDtypeStruct((heads, CHUNKS, 1, SHORT_DEV), f32)],
        in_specs=[pl.BlockSpec(memory_space=pltpu.SMEM)]
        + [anywhere] * (len(own) + len(others)),
        out_specs=[anywhere] * heads + [pl.BlockSpec(memory_space=pltpu.VMEM)],
        scratch_shapes=[
            pltpu.VMEM((heads, CHUNKS, SHORT_DEV, HD), bf16),
            pltpu.VMEM((NSHORT, blocks, SHORT_DEV, 2 * HD), bf16),
            pltpu.VMEM((NLONG, blocks, 2, SHORT_DEV, 2 * HD), bf16),
            pltpu.VMEM((heads, CHUNKS, SHORT_DEV, HD), bf16),
            pltpu.SemaphoreType.DMA((heads,)),
            pltpu.SemaphoreType.DMA((3 * blocks,)),
        ],
        compiler_params=pltpu.CompilerParams(vmem_limit_bytes=56 << 20),
        cost_estimate=pl.CostEstimate(
            flops=4 * 10**9, bytes_accessed=7 << 20, transcendentals=4 * 10**6
        ),
        name="attend_forward",
    )(scal, *own, *others)
    return (result[:heads], result[heads])


def back_kernel(heads, members, scal, *refs):
    count = heads
    own = refs[:count]
    others = refs[count : members * count]
    rest = refs[members * count :]
    grad_slots = rest[:count]
    log_ref = rest[count]
    rest = rest[count + 1 :]
    own_out = rest[:count]
    other_out = rest[count : count + members - 1]
    scratch = rest[count + members - 1 :]
    queries, keys_short, keys_long, grads, sum_short, sum_long = scratch[:6]
    low_short, low_long, zeros, row_sems, grad_sems, key_sems, zero_sems = scratch[6:]
    copies = row_copies(scal, own, queries, row_sems, heads, False)
    copies += row_copies(scal, grad_slots, grads, grad_sems, heads, False)
    copies += key_copies(scal, own, others, keys_short, keys_long, key_sems, members, heads)
    for copy in copies:
        copy.start()
    zeros[...] = jnp.zeros(zeros.shape, bf16)
    blanks = [
        pltpu.make_async_copy(
            zeros, other_out[part].at[slot, :, :, 0:HD], zero_sems.at[part * heads + slot]
        )
        for part in range(members - 1)
        for slot in range(heads)
    ]
    for copy in blanks:
        copy.start()
    for copy in copies:
        copy.wait()

    def work(kind, index, first, chunks, live_at):
        size = chunks * SHORT_DEV
        live = scal[2 + live_at].astype(bf16)
        mask = allowed_mask(scal[1], members, size)
        if kind == 0:
            keys_ref, sum_ref, low_ref = keys_short, sum_short, low_short
        else:
            keys_ref, sum_ref, low_ref = keys_long, sum_long, low_long
        for place in reversed(range(heads)):
            span = (place + 1) * members
            block = keys_ref[index, 0:span].reshape(span * size, 2 * HD)
            keys, values = block[:, :HD], block[:, HD:]
            query = queries[place, pl.ds(first, chunks)].reshape(size, HD)
            grad = grads[place, pl.ds(first, chunks)].reshape(size, HD) * live
            logs = jnp.concatenate(
                [log_ref[place, first + chunk] for chunk in range(chunks)], axis=1
            )
            probs = jnp.exp(contract(keys, query, 1, 1) * SCALE - logs)
            edge = place * members * size
            last = jnp.where(mask, probs[edge:], 0.0)
            probs = jnp.concatenate([probs[:edge], last], axis=0) if place else last
            grad_probs = contract(values, grad, 1, 1)
            delta = jnp.sum(probs * grad_probs, axis=0, keepdims=True)
            grad_scores = (probs * (grad_probs - delta)).astype(bf16)
            grad_value = dot(probs.astype(bf16), grad)
            grad_key = dot(grad_scores, query) * SCALE
            turned = contract(keys, grad_scores, 0, 0) * SCALE
            queries[place, pl.ds(first, chunks)] = (
                turned.T.astype(bf16).reshape(chunks, SHORT_DEV, HD)
            )
            pair = jnp.concatenate([grad_key, grad_value], axis=1)
            if place == heads - 1:
                sum_ref[...] = pair
            else:
                sum_ref[0 : span * size] += pair
        low_ref[index] = sum_ref[...].astype(bf16).reshape(low_ref.shape[1:])

    sequence_loop(work)
    copies = row_copies(scal, own_out, queries, row_sems, heads, True)
    head, member = scal[0], scal[1]
    number = 0
    for part in range(members):
        whose = lax.rem(member + part, members)
        for slot in range(heads):
            block = (head ^ slot) * members + whose
            target = own_out[slot] if part == 0 else other_out[part - 1].at[slot]
            copies.append(
                pltpu.make_async_copy(
                    low_short.at[:, block], target.at[0:NSHORT, :, HD:], key_sems.at[number]
                )
            )
            number += 1
            for index in range(NLONG):
                first = NSHORT + 2 * index
                copies.append(
                    pltpu.make_async_copy(
                        low_long.at[index, block],
                        target.at[first : first + 2, :, HD:],
                        key_sems.at[number],
                    )
                )
                number += 1
    for copy in copies:
        copy.start()
    for copy in blanks + copies:
        copy.wait()


def attend_backward(scal, own, others, grad_slots, logs, heads, members):
    blocks = heads * members
    anywhere = pl.BlockSpec(memory_space=pl.ANY)
    result = pl.pallas_call(
        functools.partial(back_kernel, heads, members),
        out_shape=[jax.ShapeDtypeStruct((CHUNKS, SHORT_DEV, 3 * HD), bf16)] * heads
        + [jax.ShapeDtypeStruct((heads, CHUNKS, SHORT_DEV, 3 * HD), bf16)] * (members - 1),
        in_specs=[pl.BlockSpec(memory_space=pltpu.SMEM)]
        + [anywhere] * (heads + blocks)
        + [pl.BlockSpec(memory_space=pltpu.VMEM)],
        out_specs=[anywhere] * (heads + members - 1),
        scratch_shapes=[
            pltpu.VMEM((heads, CHUNKS, SHORT_DEV, HD), bf16),
            pltpu.VMEM((NSHORT, blocks, SHORT_DEV, 2 * HD), bf16),
            pltpu.VMEM((NLONG, blocks, 2, SHORT_DEV, 2 * HD), bf16),
            pltpu.VMEM((heads, CHUNKS, SHORT_DEV, HD), bf16),
            pltpu.VMEM((blocks * SHORT_DEV, 2 * HD), f32),
            pltpu.VMEM((2 * blocks * SHORT_DEV, 2 * HD), f32),
            pltpu.VMEM((NSHORT, blocks, SHORT_DEV, 2 * HD), bf16),
            pltpu.VMEM((NLONG, blocks, 2, SHORT_DEV, 2 * HD), bf16),
            pltpu.VMEM((CHUNKS, SHORT_DEV, HD), bf16),
            pltpu.SemaphoreType.DMA((heads,)),
            pltpu.SemaphoreType.DMA((heads,)),
            pltpu.SemaphoreType.DMA((3 * blocks,)),
            pltpu.SemaphoreType.DMA(((members - 1) * heads,)),
        ],
        compiler_params=pltpu.CompilerParams(vmem_limit_bytes=60 << 20),
        cost_estimate=pl.CostEstimate(
            flops=10**10, bytes_accessed=12 << 20, transcendentals=4 * 10**6
        ),
        name="attend_backward",
    )(scal, *own, *others, *grad_slots, logs)
    return (result[:heads], result[heads:])


def rotate_rows(values, cosine, sine):
    return values * cosine + pltpu.roll(values, HD // 2, 1) * sine


def project_kernel(heads, scal, tokens, gain, cosine, sine, weights, *refs):
    slots = refs[:heads]
    normed, pooled = refs[heads : heads + 2]
    held_weights, acc, held, in_sems, out_sems = refs[heads + 2 :]
    head = scal[0]
    loads = [
        pltpu.make_async_copy(weights.at[part], held_weights.at[part], in_sems.at[part])
        for part in range(3)
    ]
    for load in loads:
        load.start()
    pooled[...] = jnp.zeros(pooled.shape, f32)

    def norm(chunk, carry):
        here = pl.ds(pl.multiple_of(chunk * SHORT_DEV, SHORT_DEV), SHORT_DEV)
        hat, _ = normalize_parts(tokens[here, :].astype(f32))
        values = hat * gain[...]
        normed[here, :] = values.astype(bf16)
        at = jnp.where(chunk < NSHORT, chunk, NSHORT + (chunk - NSHORT) // 2)
        rows = lax.broadcasted_iota(jnp.int32, pooled.shape, 0)
        added = jnp.sum(values, axis=0, keepdims=True)
        pooled[...] += jnp.where(rows == at, added, 0.0)
        return carry

    lax.fori_loop(0, CHUNKS, norm, 0)
    for part in range(3):
        loads[part].wait()
        acc[...] = dot(normed[...], held_weights[part])

        def spread(chunk, carry):
            here = pl.ds(pl.multiple_of(chunk * SHORT_DEV, SHORT_DEV), SHORT_DEV)
            for index in range(heads):
                values = acc[here, index * HD : (index + 1) * HD]
                if part < 2:
                    values = rotate_rows(values, cosine[here, :], sine[here, :])
                held[index, chunk, :, part * HD : (part + 1) * HD] = values.astype(bf16)
            return carry

        lax.fori_loop(0, CHUNKS, spread, 0)
    stores = [
        pltpu.make_async_copy(held.at[head ^ slot], slots[slot], out_sems.at[slot])
        for slot in range(heads)
    ]
    for store in stores:
        store.start()
    for store in stores:
        store.wait()


def project(scal, tokens, gain, cosine, sine, weights):
    rows = tokens.shape[0]
    width = weights.shape[2]
    heads = width // HD
    anywhere = pl.BlockSpec(memory_space=pl.ANY)
    inside = pl.BlockSpec(memory_space=pltpu.VMEM)
    result = pl.pallas_call(
        functools.partial(project_kernel, heads),
        out_shape=[jax.ShapeDtypeStruct((CHUNKS, SHORT_DEV, 3 * HD), bf16)] * heads
        + [jax.ShapeDtypeStruct((rows, D), bf16), jax.ShapeDtypeStruct((8, D), f32)],
        in_specs=[pl.BlockSpec(memory_space=pltpu.SMEM)] + [inside] * 4 + [anywhere],
        out_specs=[anywhere] * heads + [inside] * 2,
        scratch_shapes=[
            pltpu.VMEM((3, D, width), bf16),
            pltpu.VMEM((rows, width), f32),
            pltpu.VMEM((heads, CHUNKS, SHORT_DEV, 3 * HD), bf16),
            pltpu.SemaphoreType.DMA((3,)),
            pltpu.SemaphoreType.DMA((heads,)),
        ],
        compiler_params=pltpu.CompilerParams(vmem_limit_bytes=50 << 20),
        cost_estimate=pl.CostEstimate(
            flops=6 * rows * D * width, bytes_accessed=16 << 20, transcendentals=rows
        ),
        name="project",
    )(scal, tokens, gain, cosine, sine, weights)
    return (result[:heads], result[heads], result[heads + 1])


def gather_kernel(heads, scal, cosine, sine, *refs):
    slots = refs[:heads]
    out, held, sems = refs[heads:]
    copies = [
        pltpu.make_async_copy(slots[slot], held.at[scal[0] ^ slot], sems.at[slot])
        for slot in range(heads)
    ]
    for copy in copies:
        copy.start()
    for copy in copies:
        copy.wait()

    def spread(chunk, carry):
        here = pl.ds(pl.multiple_of(chunk * SHORT_DEV, SHORT_DEV), SHORT_DEV)
        for index in range(heads):
            for part in range(3):
                values = held[index, chunk, :, part * HD : (part + 1) * HD]
                if part < 2:
                    values = rotate_rows(values.astype(f32), cosine[here, :], sine[here, :])
                at = (part * heads + index) * HD
                out[here, at : at + HD] = values.astype(bf16)
        return carry

    lax.fori_loop(0, CHUNKS, spread, 0)


def gather_grads(scal, cosine, sine, slots):
    heads = len(slots)
    rows = CHUNKS * SHORT_DEV
    inside = pl.BlockSpec(memory_space=pltpu.VMEM)
    return pl.pallas_call(
        functools.partial(gather_kernel, heads),
        out_shape=jax.ShapeDtypeStruct((rows, 3 * heads * HD), bf16),
        in_specs=[pl.BlockSpec(memory_space=pltpu.SMEM)]
        + [inside] * 2
        + [pl.BlockSpec(memory_space=pl.ANY)] * heads,
        out_specs=inside,
        scratch_shapes=[
            pltpu.VMEM((heads, CHUNKS, SHORT_DEV, 3 * HD), bf16),
            pltpu.SemaphoreType.DMA((heads,)),
        ],
        compiler_params=pltpu.CompilerParams(vmem_limit_bytes=24 << 20),
        cost_estimate=pl.CostEstimate(
            flops=10 * rows * heads * HD, bytes_accessed=6 << 20, transcendentals=0
        ),
        name="gather_grads",
    )(scal, cosine, sine, *slots)


def local(
    tokens,
    w_qkv,
    w_out,
    w_up,
    w_down,
    gain_attn,
    gain_ffn,
    w_router,
    head_quarters,
    ffn_quarters,
    router_targets,
    cotangent,
):
    rows = tokens.shape[0]
    seq_rank = lax.axis_index("seq")
    seq_count = lax.axis_size("seq")
    head_rank = lax.axis_index("heads")
    head_count = lax.axis_size("heads")
    head_width = w_out.shape[0]
    ffn_width = w_up.shape[1]
    heads = head_width // HD
    members = seq_count // heads
    place, member = seq_rank // members, seq_rank % members
    share = rows // head_count
    short_rows = NSHORT * SHORT_DEV

    def across(values, slot):
        pairs = [
            (h * members + m, (h ^ slot) * members + m)
            for h in range(heads)
            for m in range(members)
        ]
        return lax.ppermute(values, "seq", pairs)

    def exchange(slots):
        sent = [across(slots[slot], slot) for slot in reversed(range(1, heads))]
        return [slots[0]] + sent[::-1]

    def among(values, step):
        pairs = [
            (h * members + (m + step) % members, h * members + m)
            for h in range(heads)
            for m in range(members)
        ]
        return lax.ppermute(values, "seq", pairs)

    block = D // seq_count
    z_groups = [[h * members + m for h in range(heads)] for m in range(members)]

    def member_columns(values):
        parts = []
        for step in range(members):
            whose = (member + members - step) % members
            columns = [
                lax.dynamic_slice_in_dim(values, (h * members + whose) * block, block, 1)
                for h in range(heads)
            ]
            parts.append(jnp.concatenate(columns, axis=1))
        return parts

    def member_sum(parts, product):
        sent = [among(product(parts[step]).astype(bf16), step) for step in range(1, members)]
        return sum([v.astype(f32) for v in sent], product(parts[0]).astype(f32)).astype(bf16)

    def scatter_z(values, axis):
        return lax.psum_scatter(
            values, "seq", scatter_dimension=axis, tiled=True, axis_index_groups=z_groups
        )

    def scatter_members(values):
        size = values.shape[0] // members

        def piece(number):
            return lax.dynamic_slice_in_dim(values, number * size, size, 0)

        total = piece(member).astype(f32)
        for step in range(1, members):
            sent = piece((member + members - step) % members)
            total = total + among(sent, step).astype(f32)
        return total.astype(bf16)

    def scatter_places(values):
        size = values.shape[0] // heads
        held = {
            slot: lax.dynamic_slice_in_dim(values, (place ^ slot) * size, size, 0)
            for slot in range(heads)
        }
        bit = 1
        while bit < heads:
            slots = [slot for slot in sorted(held) if slot & bit]
            joined = jnp.concatenate([held[slot] for slot in slots], axis=0)
            joined = jnp.split(across(joined, bit), len(slots), axis=0)
            held = {
                slot ^ bit: (held[slot ^ bit].astype(f32) + v.astype(f32)).astype(bf16)
                for slot, v in zip(slots, joined)
            }
            bit *= 2
        return held[0]

    def gather_seq(values):
        held = {0: values}
        bit = heads // 2
        while bit:
            slots = sorted(held)
            joined = jnp.concatenate([held[slot] for slot in slots], axis=0)
            joined = jnp.split(across(joined, bit), len(slots), axis=0)
            held.update({slot ^ bit: v for slot, v in zip(slots, joined)})
            bit //= 2
        values = placed([held[slot] for slot in range(heads)], place, 0)
        size = values.shape[0]
        full = jnp.zeros((size * members,) + values.shape[1:], values.dtype)
        for step in range(members):
            piece = among(values, step) if step else values
            at = (member + step) % members * size
            full = lax.dynamic_update_slice_in_dim(full, piece, at, 0)
        return full

    def swap(values, slot):
        return flip(values, "heads", head_count, slot)

    def own_rows(values, slot):
        return lax.dynamic_slice_in_dim(values, (head_rank ^ slot) * share, share, 0)

    def scatter_heads(parts):
        return [parts[0]] + [
            swap(parts[slot].astype(bf16), slot) for slot in range(1, head_count)
        ]

    def gather_heads(values):
        return [values] + [swap(values, slot) for slot in range(1, head_count)]

    def gather_doubling(values):
        slots = [values]
        bit = 1
        while bit < head_count:
            slots = slots + [swap(v, bit) for v in slots]
            bit *= 2
        return slots

    def in_order(slots, kind):
        full = jnp.zeros((rows,) + slots[0].shape[1:], kind)
        for slot in range(head_count):
            full = lax.dynamic_update_slice_in_dim(
                full, slots[slot].astype(kind), (head_rank ^ slot) * share, 0
            )
        return full

    def placed(slots, key, axis):
        size = slots[0].shape[axis]
        shape = list(slots[0].shape)
        shape[axis] = size * len(slots)
        full = jnp.zeros(shape, slots[0].dtype)
        for slot, values in enumerate(slots):
            full = lax.dynamic_update_slice_in_dim(full, values, (key ^ slot) * size, axis)
        return full

    half = ffn_width // 2
    first_up = lax.all_gather(w_up[:, :half], "seq", axis=0, tiled=True)
    out_slots = gather_heads(w_out)

    column = jnp.arange(rows)
    is_short = column < short_rows
    offset = column - short_rows
    seq_id = jnp.where(is_short, column // SHORT_DEV, NSHORT + offset // (2 * SHORT_DEV))
    position = jnp.where(
        is_short,
        seq_rank * SHORT_DEV + column % SHORT_DEV,
        seq_rank * 2 * SHORT_DEV + offset % (2 * SHORT_DEV),
    )
    in_seq = seq_id[:, None] == jnp.arange(SEQS)[None, :]
    seq_length = jnp.where(
        jnp.arange(SEQS) < NSHORT, SHORT_DEV * seq_count, 2 * SHORT_DEV * seq_count
    ).astype(f32)
    ffn_level = jnp.sum(jnp.where(in_seq, ffn_quarters[None, :], 0), axis=1)
    half_dim = HD // 2
    frequency = 10000.0 ** (-jnp.arange(half_dim, dtype=f32) * 2.0 / HD)
    angle = position.astype(f32)[:, None] * frequency[None, :]
    cosine = jnp.cos(angle)
    sine = jnp.sin(angle)
    cosine = jnp.concatenate([cosine, cosine], axis=1)
    sine = jnp.concatenate([-sine, sine], axis=1)
    my_head = head_rank * heads + place
    head_live = (my_head < head_quarters * (H // LEVELS)).astype(jnp.int32)
    scal = jnp.concatenate([jnp.stack([place, member]).astype(jnp.int32), head_live])

    slots, normed_low, pooled = project(
        scal, tokens, gain_attn[None, :], cosine, sine, w_qkv.transpose(1, 0, 2)
    )
    slots = exchange(slots)
    other_slots = [among(v, step) for step in range(1, members) for v in slots]
    tokens_own = own_rows(tokens, 0).astype(f32)
    hat_own, inverse_own = normalize_parts(tokens_own)
    cotangent_rel = jnp.concatenate(
        [own_rows(cotangent, slot) for slot in range(head_count)], axis=0
    )
    hops = []
    bit = 1
    while bit < seq_count:
        hops.append(bit)
        bit *= 2

    def hop(values, bits):
        for bit in bits:
            values = values + flip(values, "seq", seq_count, bit)
        return values

    pooled = pooled[:SEQS]
    early = (slots, other_slots, out_slots[:-1], w_up[:, half:], w_down)
    early = early + (hat_own, inverse_own, cotangent_rel, pooled, member_columns(cotangent_rel))
    early = lax.optimization_barrier(early)
    slots, other_slots, out_slots[:-1], own_up, own_down = early[:5]
    hat_own, inverse_own, cotangent_rel, pooled, cotangent_parts = early[5:]
    second_up = lax.all_gather(own_up, "seq", axis=0, tiled=True)
    full_down = lax.all_gather(own_down, "seq", axis=1, tiled=True)
    pooled = hop(pooled, hops[:-1])
    full_out = jnp.concatenate(out_slots, axis=0)
    mixed_slots, logs = attend_forward(scal, slots, other_slots, heads, members)
    mixed_slots = [across(v, slot) if slot else v for slot, v in enumerate(mixed_slots)]
    mixed_slots, pooled = lax.optimization_barrier((mixed_slots, pooled))
    pooled = hop(pooled, hops[-1:])
    mixed_slots = [v.reshape(rows, HD) for v in mixed_slots]
    heads_out = placed(mixed_slots, place, 1)

    heads_rel = [own_rows(heads_out, slot) for slot in range(head_count)]
    heads_own = jnp.concatenate(
        [heads_rel[0]] + [swap(heads_rel[slot], slot) for slot in range(1, head_count)], axis=1
    )
    hidden = tokens_own + dot(heads_own, full_out)
    hat_two, inverse_two = normalize_parts(hidden)
    normed_two = gather_heads((hat_two * gain_ffn).astype(bf16))

    level_rel = jnp.concatenate([own_rows(ffn_level, slot) for slot in range(head_count)])
    unit_index = head_rank * ffn_width + jnp.arange(ffn_width)
    ffn_live = (unit_index[None, :] < (level_rel * (FF // LEVELS))[:, None]).astype(f32)
    full_up = jnp.concatenate([first_up, second_up], axis=1)
    normed_two, pooled, full_up = lax.optimization_barrier((normed_two, pooled, full_up))
    normed_two = jnp.concatenate(normed_two, axis=0)
    upward = dot(normed_two, full_up)
    kept = jnp.maximum(upward, 0.0)
    active = (jnp.square(kept) * ffn_live).astype(bf16)
    grad_down_part = member_sum(cotangent_parts, lambda v: contract(active, v, 0, 0))
    cotangent_rel, kept, grad_down_part = lax.optimization_barrier(
        (cotangent_rel, kept, grad_down_part)
    )
    grad_active = contract(cotangent_rel, full_down, 1, 1).astype(bf16)
    grad_upward = (grad_active.astype(f32) * ffn_live * 2.0 * kept).astype(bf16)
    grad_down = scatter_z(grad_down_part, 1)
    two_parts = [
        contract(grad_upward[slot * share : (slot + 1) * share], full_up, 1, 1)
        for slot in range(head_count)
    ]
    two_parts = scatter_heads(two_parts)
    grad_up_parts = [
        contract(v, grad_upward, 0, 0).astype(bf16) for v in member_columns(normed_two)
    ]

    pooled = pooled * lax.rsqrt(seq_length)[:, None]
    logits = jnp.dot(pooled, w_router, precision=highest, preferred_element_type=f32)
    logit_grads = []
    for group in range(2):
        group_logits = logits[:, LEVELS * group : LEVELS * (group + 1)]
        raised = jnp.exp(group_logits - jnp.max(group_logits, axis=1, keepdims=True))
        chosen = (jnp.arange(LEVELS)[None, :] == router_targets[:, group][:, None]).astype(f32)
        logit_grads.append(raised / jnp.sum(raised, axis=1, keepdims=True) - chosen)
    grad_logits = jnp.concatenate(logit_grads, axis=1)
    grad_router = jnp.dot(pooled.T, grad_logits, precision=highest, preferred_element_type=f32)
    grad_pooled = (
        jnp.dot(grad_logits, w_router.T, precision=highest, preferred_element_type=f32)
        * lax.rsqrt(seq_length)[:, None]
    )
    member_own = own_rows(in_seq.astype(f32), 0)
    grad_pooled_own = jnp.dot(
        member_own, grad_pooled, precision=highest, preferred_element_type=f32
    )
    two_parts, grad_up_parts, grad_router, grad_pooled_own = lax.optimization_barrier(
        (two_parts, grad_up_parts, grad_router, grad_pooled_own)
    )
    grad_up_part = member_sum(grad_up_parts, lambda v: v)
    grad_up = scatter_z(grad_up_part, 0)

    grad_two = sum([v.astype(f32) for v in two_parts[1:]], two_parts[0])
    back_two, gain_two = normalize_back(grad_two, hat_two, inverse_two, gain_ffn)
    grad_hidden = own_rows(cotangent, 0).astype(f32) + back_two
    grad_attn_own = grad_hidden.astype(bf16)
    grad_mixed = contract(grad_attn_own, full_out, 1, 1).astype(bf16)
    grad_mixed = [
        grad_mixed[:, slot * head_width : (slot + 1) * head_width] for slot in range(head_count)
    ]
    grad_mixed = [grad_mixed[0]] + [
        swap(grad_mixed[slot], slot) for slot in range(1, head_count)
    ]
    grad_heads = placed(grad_mixed, head_rank, 0)
    grad_heads, grad_attn_own, active = lax.optimization_barrier(
        (grad_heads, grad_attn_own, active)
    )
    grad_attn = gather_heads(grad_attn_own)
    grad_slots = []
    for slot in range(heads):
        piece = lax.dynamic_slice_in_dim(grad_heads, (place ^ slot) * HD, HD, 1)
        piece = piece.reshape(CHUNKS, SHORT_DEV, HD)
        grad_slots.append(across(piece, slot) if slot else piece)
    ffn_parts = [
        dot(active[slot * share : (slot + 1) * share], full_down) for slot in range(head_count)
    ]
    ffn_parts[1:] = [v.astype(bf16) for v in ffn_parts[1:]]
    grad_slots, ffn_parts = lax.optimization_barrier((grad_slots, ffn_parts))

    own_grads, other_grads = attend_backward(
        scal, slots, other_slots, grad_slots, logs, heads, members
    )
    own_grads, other_grads, grad_attn[:-1] = lax.optimization_barrier(
        (own_grads, other_grads, grad_attn[:-1])
    )
    other_grads = [
        among(v, members - step) for step, v in zip(range(1, members), other_grads)
    ]
    sums = []
    for slot in range(heads):
        total = own_grads[slot].astype(f32)
        sums.append(sum([v[slot].astype(f32) for v in other_grads], total).astype(bf16))
    sums, ffn_parts = lax.optimization_barrier((sums, ffn_parts))
    sums = exchange(sums)
    ffn_parts = scatter_heads(ffn_parts)
    grad_attn = jnp.concatenate(grad_attn, axis=0)
    grad_out_part = contract(jnp.concatenate(heads_rel, axis=0), grad_attn, 0, 0).astype(bf16)
    grad_out_part, sums, ffn_parts[:-1] = lax.optimization_barrier(
        (grad_out_part, sums, ffn_parts[:-1])
    )
    total_out = scatter_members(grad_out_part)
    grad_projected = gather_grads(scal, cosine, -sine, sums)
    grad_qkv_part = contract(normed_low, grad_projected, 0, 0).astype(bf16)
    grad_projected, grad_qkv_part, ffn_parts, grad_down, grad_up = lax.optimization_barrier(
        (grad_projected, grad_qkv_part, ffn_parts, grad_down, grad_up)
    )
    total_qkv = lax.psum_scatter(grad_qkv_part, "seq", scatter_dimension=0, tiled=True)
    grad_down, grad_up = grad_down.astype(f32), grad_up.astype(f32)
    output_own = (
        hidden + sum([v.astype(f32) for v in ffn_parts[1:]], ffn_parts[0])
    ).astype(bf16)
    output_slots = [output_own] + [
        swap(output_own, slot) for slot in range(1, head_count - 1)
    ]
    one_parts = [
        sum(
            contract(
                own_rows(grad_projected, slot)[:, part * head_width : (part + 1) * head_width],
                w_qkv[:, part],
                1,
                1,
            )
            for part in range(3)
        )
        for slot in range(head_count)
    ]
    one_parts[1:] = [v.astype(bf16) for v in one_parts[1:]]
    one_parts, total_out, output_slots = lax.optimization_barrier(
        (one_parts, total_out, output_slots)
    )
    one_parts = scatter_heads(one_parts)
    output_slots.append(swap(output_slots[0], head_count - 1))
    total_out = scatter_places(total_out)

    grad_one = sum([v.astype(f32) for v in one_parts[1:]], one_parts[0]) + grad_pooled_own
    back_one, gain_one = normalize_back(grad_one, hat_own, inverse_own, gain_attn)
    tokens_back = (grad_hidden + back_one).astype(bf16)
    gains = butterfly(jnp.stack([gain_one, gain_two]), "heads", head_count)
    tokens_back, total_qkv, total_out, gains, output_slots = lax.optimization_barrier(
        (tokens_back, total_qkv, total_out, gains, output_slots)
    )
    total_qkv = lax.all_gather(total_qkv, "seq", axis=0, tiled=True)
    token_slots = gather_heads(tokens_back)
    grad_out = gather_seq(total_out).astype(f32)
    grad_qkv = jnp.stack(
        [
            total_qkv[:, part * head_width : (part + 1) * head_width].astype(f32)
            for part in range(3)
        ],
        axis=1,
    )
    token_slots, gains = lax.optimization_barrier((token_slots, gains))
    output = in_order(output_slots, bf16)
    gains = butterfly(gains, "seq", seq_count)
    grad_tokens = in_order(token_slots, f32)
    return (
        output,
        grad_tokens,
        grad_qkv,
        grad_out,
        grad_up,
        grad_down,
        gains[0],
        gains[1],
        grad_router,
    )


def solution(mesh):
    return jax.shard_map(
        local,
        mesh=mesh,
        in_specs=(
            P("seq", None),
            P(None, None, "heads"),
            P("heads", None),
            P("seq", "heads"),
            P("heads", "seq"),
            P(),
            P(),
            P(),
            P(),
            P(),
            P(),
            P("seq", None),
        ),
        out_specs=(
            P("seq", None),
            P("seq", None),
            P(None, None, "heads"),
            P("heads", None),
            P("seq", "heads"),
            P("heads", "seq"),
            P(),
            P(),
            P(),
        ),
        check_vma=False,
    )
```

```python
import functools

import jax
import jax.numpy as jnp
from jax import lax
from jax.experimental import pallas as pl
from jax.experimental.pallas import tpu as pltpu
from jax.sharding import PartitionSpec as P

D = 2048
H = 16
HD = 128
FF = 8192
SHORT_DEV = 128
NSHORT = 3
NLONG = 2
LEVELS = 4
SEQS = 5
CHUNKS = NSHORT + 2 * NLONG

epsilon = 1e-05
highest = lax.Precision.HIGHEST
f32 = jnp.float32
bf16 = jnp.bfloat16
SCALE = HD ** (-0.5)


def dot(left, right):
    return jnp.dot(left, right, preferred_element_type=f32)


def contract(left, right, left_dim, right_dim):
    return lax.dot_general(
        left, right, (((left_dim,), (right_dim,)), ((), ())), preferred_element_type=f32
    )


def normalize_parts(values):
    centered = values - jnp.mean(values, axis=-1, keepdims=True)
    inverse = lax.rsqrt(jnp.mean(centered * centered, axis=-1, keepdims=True) + epsilon)
    return (centered * inverse, inverse)


def normalize_back(grad_normed, normed_hat, inverse, gain):
    grad_hat = grad_normed * gain
    middle = (
        grad_hat
        - jnp.mean(grad_hat, axis=-1, keepdims=True)
        - normed_hat * jnp.mean(grad_hat * normed_hat, axis=-1, keepdims=True)
    )
    return (inverse * middle, jnp.sum(grad_normed * normed_hat, axis=0))


def flip(values, axis, size, bit):
    return lax.ppermute(values, axis, [(i, i ^ bit) for i in range(size)])


def butterfly(values, axis, size):
    bit = 1
    while bit < size:
        values = values + flip(values, axis, size, bit)
        bit *= 2
    return values


def key_copies(scal, own, others, keys_short, keys_long, sems, members, heads):
    head, member = scal[0], scal[1]
    copies = []
    for part in range(members):
        source = own if part == 0 else others[(part - 1) * heads : part * heads]
        whose = lax.rem(member + part, members)
        for slot in range(heads):
            block = (head ^ slot) * members + whose
            number = len(copies)
            copies.append(
                pltpu.make_async_copy(
                    source[slot].at[0:NSHORT, :, HD:], keys_short.at[:, block], sems.at[number]
                )
            )
            for index in range(NLONG):
                first = NSHORT + 2 * index
                number = len(copies)
                copies.append(
                    pltpu.make_async_copy(
                        source[slot].at[first : first + 2, :, HD:],
                        keys_long.at[index, block],
                        sems.at[number],
                    )
                )
    return copies


def row_copies(scal, slots, held, sems, heads, outward):
    head = scal[0]
    copies = []
    for slot in range(heads):
        ends = (slots[slot].at[:, :, 0:HD], held.at[head ^ slot])
        if outward:
            ends = ends[::-1]
        copies.append(pltpu.make_async_copy(ends[0], ends[1], sems.at[slot]))
    return copies


def sequence_loop(work):
    def short(index, carry):
        work(0, index, index, 1, index)
        return carry

    def long(index, carry):
        work(1, index, NSHORT + 2 * index, 2, NSHORT + index)
        return carry

    lax.fori_loop(0, NSHORT, short, 0)
    lax.fori_loop(0, NLONG, long, 0)


def allowed_mask(member, members, size):
    key_at = lax.broadcasted_iota(jnp.int32, (members * size, size), 0)
    query_at = lax.broadcasted_iota(jnp.int32, (members * size, size), 1) + member * size
    return key_at <= query_at


def attend_kernel(heads, members, scal, *refs):
    count = heads
    own = refs[:count]
    others = refs[count : members * count]
    rest = refs[members * count :]
    out_slots = rest[:count]
    log_ref = rest[count]
    queries, keys_short, keys_long, mixed, row_sems, key_sems = rest[count + 1 :]
    copies = row_copies(scal, own, queries, row_sems, heads, False)
    copies += key_copies(scal, own, others, keys_short, keys_long, key_sems, members, heads)
    for copy in copies:
        copy.start()
    for copy in copies:
        copy.wait()

    def work(kind, index, first, chunks, live_at):
        size = chunks * SHORT_DEV
        live = scal[2 + live_at].astype(f32)
        mask = allowed_mask(scal[1], members, size)
        for place in range(heads):
            span = (place + 1) * members
            if kind == 0:
                block = keys_short[index, 0:span]
            else:
                block = keys_long[index, 0:span]
            block = block.reshape(span * size, 2 * HD)
            keys, values = block[:, :HD], block[:, HD:]
            query = queries[place, pl.ds(first, chunks)].reshape(size, HD)
            scores = contract(keys, query, 1, 1) * SCALE
            edge = place * members * size
            last = jnp.where(mask, scores[edge:], -1e30)
            largest = jnp.max(last, axis=0, keepdims=True)
            if place:
                early = scores[:edge]
                largest = jnp.maximum(largest, jnp.max(early, axis=0, keepdims=True))
            raised = jnp.exp(last - largest)
            total = jnp.sum(raised, axis=0, keepdims=True)
            low = raised.astype(bf16)
            turned = contract(values[edge:], low, 0, 0)
            if place:
                raised = jnp.exp(early - largest)
                total = total + jnp.sum(raised, axis=0, keepdims=True)
                turned = turned + contract(values[:edge], raised.astype(bf16), 0, 0)
            turned = turned * (live / total)
            mixed[place, pl.ds(first, chunks)] = (
                turned.T.astype(bf16).reshape(chunks, SHORT_DEV, HD)
            )
            logs = largest + jnp.log(total)
            for chunk in range(chunks):
                log_ref[place, first + chunk] = logs[:, chunk * SHORT_DEV : (chunk + 1) * SHORT_DEV]

    sequence_loop(work)
    copies = row_copies(scal, out_slots, mixed, row_sems, heads, True)
    for copy in copies:
        copy.start()
    for copy in copies:
        copy.wait()


def attend_forward(scal, own, others, heads, members):
    blocks = heads * members
    anywhere = pl.BlockSpec(memory_space=pl.ANY)
    result = pl.pallas_call(
        functools.partial(attend_kernel, heads, members),
        out_shape=[jax.ShapeDtypeStruct((CHUNKS, SHORT_DEV, HD), bf16)] * heads
        + [jax.ShapeDtypeStruct((heads, CHUNKS, 1, SHORT_DEV), f32)],
        in_specs=[pl.BlockSpec(memory_space=pltpu.SMEM)]
        + [anywhere] * (len(own) + len(others)),
        out_specs=[anywhere] * heads + [pl.BlockSpec(memory_space=pltpu.VMEM)],
        scratch_shapes=[
            pltpu.VMEM((heads, CHUNKS, SHORT_DEV, HD), bf16),
            pltpu.VMEM((NSHORT, blocks, SHORT_DEV, 2 * HD), bf16),
            pltpu.VMEM((NLONG, blocks, 2, SHORT_DEV, 2 * HD), bf16),
            pltpu.VMEM((heads, CHUNKS, SHORT_DEV, HD), bf16),
            pltpu.SemaphoreType.DMA((heads,)),
            pltpu.SemaphoreType.DMA((3 * blocks,)),
        ],
        compiler_params=pltpu.CompilerParams(vmem_limit_bytes=56 << 20),
        cost_estimate=pl.CostEstimate(
            flops=4 * 10**9, bytes_accessed=7 << 20, transcendentals=4 * 10**6
        ),
        name="attend_forward",
    )(scal, *own, *others)
    return (result[:heads], result[heads])


def back_kernel(heads, members, scal, *refs):
    count = heads
    own = refs[:count]
    others = refs[count : members * count]
    rest = refs[members * count :]
    grad_slots = rest[:count]
    log_ref = rest[count]
    rest = rest[count + 1 :]
    own_out = rest[:count]
    other_out = rest[count : count + members - 1]
    scratch = rest[count + members - 1 :]
    queries, keys_short, keys_long, grads, sum_short, sum_long = scratch[:6]
    low_short, low_long, zeros, row_sems, grad_sems, key_sems, zero_sems = scratch[6:]
    copies = row_copies(scal, own, queries, row_sems, heads, False)
    copies += row_copies(scal, grad_slots, grads, grad_sems, heads, False)
    copies += key_copies(scal, own, others, keys_short, keys_long, key_sems, members, heads)
    for copy in copies:
        copy.start()
    zeros[...] = jnp.zeros(zeros.shape, bf16)
    blanks = [
        pltpu.make_async_copy(
            zeros, other_out[part].at[slot, :, :, 0:HD], zero_sems.at[part * heads + slot]
        )
        for part in range(members - 1)
        for slot in range(heads)
    ]
    for copy in blanks:
        copy.start()
    for copy in copies:
        copy.wait()

    def work(kind, index, first, chunks, live_at):
        size = chunks * SHORT_DEV
        live = scal[2 + live_at].astype(bf16)
        mask = allowed_mask(scal[1], members, size)
        if kind == 0:
            keys_ref, sum_ref, low_ref = keys_short, sum_short, low_short
        else:
            keys_ref, sum_ref, low_ref = keys_long, sum_long, low_long
        for place in reversed(range(heads)):
            span = (place + 1) * members
            block = keys_ref[index, 0:span].reshape(span * size, 2 * HD)
            keys, values = block[:, :HD], block[:, HD:]
            query = queries[place, pl.ds(first, chunks)].reshape(size, HD)
            grad = grads[place, pl.ds(first, chunks)].reshape(size, HD) * live
            logs = jnp.concatenate(
                [log_ref[place, first + chunk] for chunk in range(chunks)], axis=1
            )
            probs = jnp.exp(contract(keys, query, 1, 1) * SCALE - logs)
            edge = place * members * size
            last = jnp.where(mask, probs[edge:], 0.0)
            probs = jnp.concatenate([probs[:edge], last], axis=0) if place else last
            grad_probs = contract(values, grad, 1, 1)
            delta = jnp.sum(probs * grad_probs, axis=0, keepdims=True)
            grad_scores = (probs * (grad_probs - delta)).astype(bf16)
            grad_value = dot(probs.astype(bf16), grad)
            grad_key = dot(grad_scores, query) * SCALE
            turned = contract(keys, grad_scores, 0, 0) * SCALE
            queries[place, pl.ds(first, chunks)] = (
                turned.T.astype(bf16).reshape(chunks, SHORT_DEV, HD)
            )
            pair = jnp.concatenate([grad_key, grad_value], axis=1)
            if place == heads - 1:
                sum_ref[...] = pair
            else:
                sum_ref[0 : span * size] += pair
        low_ref[index] = sum_ref[...].astype(bf16).reshape(low_ref.shape[1:])

    sequence_loop(work)
    copies = row_copies(scal, own_out, queries, row_sems, heads, True)
    head, member = scal[0], scal[1]
    number = 0
    for part in range(members):
        whose = lax.rem(member + part, members)
        for slot in range(heads):
            block = (head ^ slot) * members + whose
            target = own_out[slot] if part == 0 else other_out[part - 1].at[slot]
            copies.append(
                pltpu.make_async_copy(
                    low_short.at[:, block], target.at[0:NSHORT, :, HD:], key_sems.at[number]
                )
            )
            number += 1
            for index in range(NLONG):
                first = NSHORT + 2 * index
                copies.append(
                    pltpu.make_async_copy(
                        low_long.at[index, block],
                        target.at[first : first + 2, :, HD:],
                        key_sems.at[number],
                    )
                )
                number += 1
    for copy in copies:
        copy.start()
    for copy in blanks + copies:
        copy.wait()


def attend_backward(scal, own, others, grad_slots, logs, heads, members):
    blocks = heads * members
    anywhere = pl.BlockSpec(memory_space=pl.ANY)
    result = pl.pallas_call(
        functools.partial(back_kernel, heads, members),
        out_shape=[jax.ShapeDtypeStruct((CHUNKS, SHORT_DEV, 3 * HD), bf16)] * heads
        + [jax.ShapeDtypeStruct((heads, CHUNKS, SHORT_DEV, 3 * HD), bf16)] * (members - 1),
        in_specs=[pl.BlockSpec(memory_space=pltpu.SMEM)]
        + [anywhere] * (heads + blocks)
        + [pl.BlockSpec(memory_space=pltpu.VMEM)],
        out_specs=[anywhere] * (heads + members - 1),
        scratch_shapes=[
            pltpu.VMEM((heads, CHUNKS, SHORT_DEV, HD), bf16),
            pltpu.VMEM((NSHORT, blocks, SHORT_DEV, 2 * HD), bf16),
            pltpu.VMEM((NLONG, blocks, 2, SHORT_DEV, 2 * HD), bf16),
            pltpu.VMEM((heads, CHUNKS, SHORT_DEV, HD), bf16),
            pltpu.VMEM((blocks * SHORT_DEV, 2 * HD), f32),
            pltpu.VMEM((2 * blocks * SHORT_DEV, 2 * HD), f32),
            pltpu.VMEM((NSHORT, blocks, SHORT_DEV, 2 * HD), bf16),
            pltpu.VMEM((NLONG, blocks, 2, SHORT_DEV, 2 * HD), bf16),
            pltpu.VMEM((CHUNKS, SHORT_DEV, HD), bf16),
            pltpu.SemaphoreType.DMA((heads,)),
            pltpu.SemaphoreType.DMA((heads,)),
            pltpu.SemaphoreType.DMA((3 * blocks,)),
            pltpu.SemaphoreType.DMA(((members - 1) * heads,)),
        ],
        compiler_params=pltpu.CompilerParams(vmem_limit_bytes=60 << 20),
        cost_estimate=pl.CostEstimate(
            flops=10**10, bytes_accessed=12 << 20, transcendentals=4 * 10**6
        ),
        name="attend_backward",
    )(scal, *own, *others, *grad_slots, logs)
    return (result[:heads], result[heads:])


def rotate_rows(values, cosine, sine):
    return values * cosine + pltpu.roll(values, HD // 2, 1) * sine


def project_kernel(heads, scal, tokens, gain, cosine, sine, weights, *refs):
    slots = refs[:heads]
    normed, pooled = refs[heads : heads + 2]
    held_weights, acc, held, in_sems, out_sems = refs[heads + 2 :]
    head = scal[0]
    loads = [
        pltpu.make_async_copy(weights.at[part], held_weights.at[part], in_sems.at[part])
        for part in range(3)
    ]
    for load in loads:
        load.start()
    pooled[...] = jnp.zeros(pooled.shape, f32)

    def norm(chunk, carry):
        here = pl.ds(pl.multiple_of(chunk * SHORT_DEV, SHORT_DEV), SHORT_DEV)
        hat, _ = normalize_parts(tokens[here, :].astype(f32))
        values = hat * gain[...]
        normed[here, :] = values.astype(bf16)
        at = jnp.where(chunk < NSHORT, chunk, NSHORT + (chunk - NSHORT) // 2)
        rows = lax.broadcasted_iota(jnp.int32, pooled.shape, 0)
        added = jnp.sum(values, axis=0, keepdims=True)
        pooled[...] += jnp.where(rows == at, added, 0.0)
        return carry

    lax.fori_loop(0, CHUNKS, norm, 0)
    for part in range(3):
        loads[part].wait()
        acc[...] = dot(normed[...], held_weights[part])

        def spread(chunk, carry):
            here = pl.ds(pl.multiple_of(chunk * SHORT_DEV, SHORT_DEV), SHORT_DEV)
            for index in range(heads):
                values = acc[here, index * HD : (index + 1) * HD]
                if part < 2:
                    values = rotate_rows(values, cosine[here, :], sine[here, :])
                held[index, chunk, :, part * HD : (part + 1) * HD] = values.astype(bf16)
            return carry

        lax.fori_loop(0, CHUNKS, spread, 0)
    stores = [
        pltpu.make_async_copy(held.at[head ^ slot], slots[slot], out_sems.at[slot])
        for slot in range(heads)
    ]
    for store in stores:
        store.start()
    for store in stores:
        store.wait()


def project(scal, tokens, gain, cosine, sine, weights):
    rows = tokens.shape[0]
    width = weights.shape[2]
    heads = width // HD
    anywhere = pl.BlockSpec(memory_space=pl.ANY)
    inside = pl.BlockSpec(memory_space=pltpu.VMEM)
    result = pl.pallas_call(
        functools.partial(project_kernel, heads),
        out_shape=[jax.ShapeDtypeStruct((CHUNKS, SHORT_DEV, 3 * HD), bf16)] * heads
        + [jax.ShapeDtypeStruct((rows, D), bf16), jax.ShapeDtypeStruct((8, D), f32)],
        in_specs=[pl.BlockSpec(memory_space=pltpu.SMEM)] + [inside] * 4 + [anywhere],
        out_specs=[anywhere] * heads + [inside] * 2,
        scratch_shapes=[
            pltpu.VMEM((3, D, width), bf16),
            pltpu.VMEM((rows, width), f32),
            pltpu.VMEM((heads, CHUNKS, SHORT_DEV, 3 * HD), bf16),
            pltpu.SemaphoreType.DMA((3,)),
            pltpu.SemaphoreType.DMA((heads,)),
        ],
        compiler_params=pltpu.CompilerParams(vmem_limit_bytes=50 << 20),
        cost_estimate=pl.CostEstimate(
            flops=6 * rows * D * width, bytes_accessed=16 << 20, transcendentals=rows
        ),
        name="project",
    )(scal, tokens, gain, cosine, sine, weights)
    return (result[:heads], result[heads], result[heads + 1])


def gather_kernel(heads, scal, cosine, sine, *refs):
    slots = refs[:heads]
    out, held, sems = refs[heads:]
    copies = [
        pltpu.make_async_copy(slots[slot], held.at[scal[0] ^ slot], sems.at[slot])
        for slot in range(heads)
    ]
    for copy in copies:
        copy.start()
    for copy in copies:
        copy.wait()

    def spread(chunk, carry):
        here = pl.ds(pl.multiple_of(chunk * SHORT_DEV, SHORT_DEV), SHORT_DEV)
        for index in range(heads):
            for part in range(3):
                values = held[index, chunk, :, part * HD : (part + 1) * HD]
                if part < 2:
                    values = rotate_rows(values.astype(f32), cosine[here, :], sine[here, :])
                at = (part * heads + index) * HD
                out[here, at : at + HD] = values.astype(bf16)
        return carry

    lax.fori_loop(0, CHUNKS, spread, 0)


def gather_grads(scal, cosine, sine, slots):
    heads = len(slots)
    rows = CHUNKS * SHORT_DEV
    inside = pl.BlockSpec(memory_space=pltpu.VMEM)
    return pl.pallas_call(
        functools.partial(gather_kernel, heads),
        out_shape=jax.ShapeDtypeStruct((rows, 3 * heads * HD), bf16),
        in_specs=[pl.BlockSpec(memory_space=pltpu.SMEM)]
        + [inside] * 2
        + [pl.BlockSpec(memory_space=pl.ANY)] * heads,
        out_specs=inside,
        scratch_shapes=[
            pltpu.VMEM((heads, CHUNKS, SHORT_DEV, 3 * HD), bf16),
            pltpu.SemaphoreType.DMA((heads,)),
        ],
        compiler_params=pltpu.CompilerParams(vmem_limit_bytes=24 << 20),
        cost_estimate=pl.CostEstimate(
            flops=10 * rows * heads * HD, bytes_accessed=6 << 20, transcendentals=0
        ),
        name="gather_grads",
    )(scal, cosine, sine, *slots)


def widen_kernel(source, target):
    width = target.shape[2]
    for part in range(3):
        target[part] = source[:, part * width : (part + 1) * width].astype(f32)


def widen(values):
    rows, width = values.shape[0], values.shape[1] // 3
    tile = rows // 8
    return pl.pallas_call(
        widen_kernel,
        grid=(8,),
        out_shape=jax.ShapeDtypeStruct((3, rows, width), f32),
        in_specs=[pl.BlockSpec((tile, 3 * width), lambda i: (i, 0))],
        out_specs=pl.BlockSpec((3, tile, width), lambda i: (0, i, 0)),
        cost_estimate=pl.CostEstimate(
            flops=3 * rows * width, bytes_accessed=18 * rows * width, transcendentals=0
        ),
        name="widen",
    )(values)


def local(
    tokens,
    w_qkv,
    w_out,
    w_up,
    w_down,
    gain_attn,
    gain_ffn,
    w_router,
    head_quarters,
    ffn_quarters,
    router_targets,
    cotangent,
):
    rows = tokens.shape[0]
    seq_rank = lax.axis_index("seq")
    seq_count = lax.axis_size("seq")
    head_rank = lax.axis_index("heads")
    head_count = lax.axis_size("heads")
    head_width = w_out.shape[0]
    ffn_width = w_up.shape[1]
    heads = head_width // HD
    members = seq_count // heads
    place, member = seq_rank // members, seq_rank % members
    share = rows // head_count
    short_rows = NSHORT * SHORT_DEV

    def across(values, slot):
        pairs = [
            (h * members + m, (h ^ slot) * members + m)
            for h in range(heads)
            for m in range(members)
        ]
        return lax.ppermute(values, "seq", pairs)

    def exchange(slots):
        sent = [across(slots[slot], slot) for slot in reversed(range(1, heads))]
        return [slots[0]] + sent[::-1]

    def among(values, step):
        pairs = [
            (h * members + (m + step) % members, h * members + m)
            for h in range(heads)
            for m in range(members)
        ]
        return lax.ppermute(values, "seq", pairs)

    block = D // seq_count
    z_groups = [[h * members + m for h in range(heads)] for m in range(members)]

    def member_columns(values):
        parts = []
        for step in range(members):
            whose = (member + members - step) % members
            columns = [
                lax.dynamic_slice_in_dim(values, (h * members + whose) * block, block, 1)
                for h in range(heads)
            ]
            parts.append(jnp.concatenate(columns, axis=1))
        return parts

    def member_sum(parts, product):
        sent = [among(product(parts[step]).astype(bf16), step) for step in range(1, members)]
        return sum([v.astype(f32) for v in sent], product(parts[0]).astype(f32)).astype(bf16)

    def scatter_z(values, axis):
        return lax.psum_scatter(
            values, "seq", scatter_dimension=axis, tiled=True, axis_index_groups=z_groups
        )

    def scatter_members(values):
        size = values.shape[0] // members

        def piece(number):
            return lax.dynamic_slice_in_dim(values, number * size, size, 0)

        total = piece(member).astype(f32)
        for step in range(1, members):
            sent = piece((member + members - step) % members)
            total = total + among(sent, step).astype(f32)
        return total.astype(bf16)

    def scatter_places(values):
        size = values.shape[0] // heads
        pieces = [
            lax.dynamic_slice_in_dim(values, (place ^ slot) * size, size, 0) for slot in range(heads)
        ]
        pieces = [v.astype(f32) for v in exchange(pieces)]
        return sum(pieces[1:], pieces[0]).astype(bf16)

    def gather_seq(values):
        values = placed(exchange([values] * heads), place, 0)
        size = values.shape[0]
        full = jnp.zeros((size * members,) + values.shape[1:], values.dtype)
        for step in range(members):
            piece = among(values, step) if step else values
            at = (member + step) % members * size
            full = lax.dynamic_update_slice_in_dim(full, piece, at, 0)
        return full

    def swap(values, slot):
        return flip(values, "heads", head_count, slot)

    def own_rows(values, slot):
        return lax.dynamic_slice_in_dim(values, (head_rank ^ slot) * share, share, 0)

    def scatter_heads(parts):
        return [parts[0]] + [
            swap(parts[slot].astype(bf16), slot) for slot in range(1, head_count)
        ]

    def gather_heads(values):
        return [values] + [swap(values, slot) for slot in range(1, head_count)]

    def gather_doubling(values):
        slots = [values]
        bit = 1
        while bit < head_count:
            slots = slots + [swap(v, bit) for v in slots]
            bit *= 2
        return slots

    def in_order(slots, kind):
        full = jnp.zeros((rows,) + slots[0].shape[1:], kind)
        for slot in range(head_count):
            full = lax.dynamic_update_slice_in_dim(
                full, slots[slot].astype(kind), (head_rank ^ slot) * share, 0
            )
        return full

    def placed(slots, key, axis):
        size = slots[0].shape[axis]
        shape = list(slots[0].shape)
        shape[axis] = size * len(slots)
        full = jnp.zeros(shape, slots[0].dtype)
        for slot, values in enumerate(slots):
            full = lax.dynamic_update_slice_in_dim(full, values, (key ^ slot) * size, axis)
        return full

    half = ffn_width // 2
    first_up = lax.all_gather(w_up[:, :half], "seq", axis=0, tiled=True)
    out_slots = gather_heads(w_out)

    column = jnp.arange(rows)
    is_short = column < short_rows
    offset = column - short_rows
    seq_id = jnp.where(is_short, column // SHORT_DEV, NSHORT + offset // (2 * SHORT_DEV))
    position = jnp.where(
        is_short,
        seq_rank * SHORT_DEV + column % SHORT_DEV,
        seq_rank * 2 * SHORT_DEV + offset % (2 * SHORT_DEV),
    )
    in_seq = seq_id[:, None] == jnp.arange(SEQS)[None, :]
    seq_length = jnp.where(
        jnp.arange(SEQS) < NSHORT, SHORT_DEV * seq_count, 2 * SHORT_DEV * seq_count
    ).astype(f32)
    ffn_level = jnp.sum(jnp.where(in_seq, ffn_quarters[None, :], 0), axis=1)
    half_dim = HD // 2
    frequency = 10000.0 ** (-jnp.arange(half_dim, dtype=f32) * 2.0 / HD)
    angle = position.astype(f32)[:, None] * frequency[None, :]
    cosine = jnp.cos(angle)
    sine = jnp.sin(angle)
    cosine = jnp.concatenate([cosine, cosine], axis=1)
    sine = jnp.concatenate([-sine, sine], axis=1)
    my_head = head_rank * heads + place
    head_live = (my_head < head_quarters * (H // LEVELS)).astype(jnp.int32)
    scal = jnp.concatenate([jnp.stack([place, member]).astype(jnp.int32), head_live])

    slots, normed_low, pooled = project(
        scal, tokens, gain_attn[None, :], cosine, sine, w_qkv.transpose(1, 0, 2)
    )
    slots = exchange(slots)
    other_slots = [among(v, step) for step in range(1, members) for v in slots]
    tokens_own = own_rows(tokens, 0).astype(f32)
    hat_own, inverse_own = normalize_parts(tokens_own)
    cotangent_rel = jnp.concatenate(
        [own_rows(cotangent, slot) for slot in range(head_count)], axis=0
    )
    hops = []
    bit = 1
    while bit < seq_count:
        hops.append(bit)
        bit *= 2

    def hop(values, bits):
        for bit in bits:
            values = values + flip(values, "seq", seq_count, bit)
        return values

    pooled = pooled[:SEQS]
    early = (slots, other_slots, out_slots[:-1], w_up[:, half:], w_down)
    early = early + (hat_own, inverse_own, cotangent_rel, pooled, member_columns(cotangent_rel))
    early = lax.optimization_barrier(early)
    slots, other_slots, out_slots[:-1], own_up, own_down = early[:5]
    hat_own, inverse_own, cotangent_rel, pooled, cotangent_parts = early[5:]
    second_up = lax.all_gather(own_up, "seq", axis=0, tiled=True)
    full_down = lax.all_gather(own_down, "seq", axis=1, tiled=True)
    pooled = hop(pooled, hops[:-1])
    full_out = jnp.concatenate(out_slots, axis=0)
    mixed_slots, logs = attend_forward(scal, slots, other_slots, heads, members)
    mixed_slots = [across(v, slot) if slot else v for slot, v in enumerate(mixed_slots)]
    mixed_slots, pooled = lax.optimization_barrier((mixed_slots, pooled))
    pooled = hop(pooled, hops[-1:])
    mixed_slots = [v.reshape(rows, HD) for v in mixed_slots]
    heads_out = placed(mixed_slots, place, 1)

    heads_rel = [own_rows(heads_out, slot) for slot in range(head_count)]
    heads_own = jnp.concatenate(
        [heads_rel[0]] + [swap(heads_rel[slot], slot) for slot in range(1, head_count)], axis=1
    )
    hidden = tokens_own + dot(heads_own, full_out)
    hat_two, inverse_two = normalize_parts(hidden)
    normed_two = gather_heads((hat_two * gain_ffn).astype(bf16))

    level_rel = jnp.concatenate([own_rows(ffn_level, slot) for slot in range(head_count)])
    unit_index = head_rank * ffn_width + jnp.arange(ffn_width)
    ffn_live = (unit_index[None, :] < (level_rel * (FF // LEVELS))[:, None]).astype(f32)
    full_up = jnp.concatenate([first_up, second_up], axis=1)
    normed_two, pooled, full_up = lax.optimization_barrier((normed_two, pooled, full_up))
    normed_two = jnp.concatenate(normed_two, axis=0)
    upward = dot(normed_two, full_up)
    kept = jnp.maximum(upward, 0.0)
    active = (jnp.square(kept) * ffn_live).astype(bf16)
    grad_down_part = member_sum(cotangent_parts, lambda v: contract(active, v, 0, 0))
    cotangent_rel, kept, grad_down_part = lax.optimization_barrier(
        (cotangent_rel, kept, grad_down_part)
    )
    grad_active = contract(cotangent_rel, full_down, 1, 1).astype(bf16)
    grad_upward = (grad_active.astype(f32) * ffn_live * 2.0 * kept).astype(bf16)
    grad_down = scatter_z(grad_down_part, 1)
    two_parts = [
        contract(grad_upward[slot * share : (slot + 1) * share], full_up, 1, 1)
        for slot in range(head_count)
    ]
    two_parts = scatter_heads(two_parts)
    grad_up_parts = [
        contract(v, grad_upward, 0, 0).astype(bf16) for v in member_columns(normed_two)
    ]

    pooled = pooled * lax.rsqrt(seq_length)[:, None]
    logits = jnp.dot(pooled, w_router, precision=highest, preferred_element_type=f32)
    logit_grads = []
    for group in range(2):
        group_logits = logits[:, LEVELS * group : LEVELS * (group + 1)]
        raised = jnp.exp(group_logits - jnp.max(group_logits, axis=1, keepdims=True))
        chosen = (jnp.arange(LEVELS)[None, :] == router_targets[:, group][:, None]).astype(f32)
        logit_grads.append(raised / jnp.sum(raised, axis=1, keepdims=True) - chosen)
    grad_logits = jnp.concatenate(logit_grads, axis=1)
    grad_router = jnp.dot(pooled.T, grad_logits, precision=highest, preferred_element_type=f32)
    grad_pooled = (
        jnp.dot(grad_logits, w_router.T, precision=highest, preferred_element_type=f32)
        * lax.rsqrt(seq_length)[:, None]
    )
    member_own = own_rows(in_seq.astype(f32), 0)
    grad_pooled_own = jnp.dot(
        member_own, grad_pooled, precision=highest, preferred_element_type=f32
    )
    two_parts, grad_up_parts, grad_router, grad_pooled_own = lax.optimization_barrier(
        (two_parts, grad_up_parts, grad_router, grad_pooled_own)
    )
    grad_up_part = member_sum(grad_up_parts, lambda v: v)
    grad_up = scatter_z(grad_up_part, 0)

    grad_two = sum([v.astype(f32) for v in two_parts[1:]], two_parts[0])
    back_two, gain_two = normalize_back(grad_two, hat_two, inverse_two, gain_ffn)
    grad_hidden = own_rows(cotangent, 0).astype(f32) + back_two
    grad_attn_own = grad_hidden.astype(bf16)
    grad_mixed = contract(grad_attn_own, full_out, 1, 1).astype(bf16)
    grad_mixed = [
        grad_mixed[:, slot * head_width : (slot + 1) * head_width] for slot in range(head_count)
    ]
    active, grad_mixed = lax.optimization_barrier((active, grad_mixed))
    grad_mixed = [grad_mixed[0]] + [
        swap(grad_mixed[slot], slot) for slot in range(1, head_count)
    ]
    grad_heads = placed(grad_mixed, head_rank, 0)
    grad_heads, grad_attn_own = lax.optimization_barrier((grad_heads, grad_attn_own))
    grad_attn = gather_heads(grad_attn_own)
    grad_slots = []
    for slot in range(heads):
        piece = lax.dynamic_slice_in_dim(grad_heads, (place ^ slot) * HD, HD, 1)
        piece = piece.reshape(CHUNKS, SHORT_DEV, HD)
        grad_slots.append(across(piece, slot) if slot else piece)
    ffn_parts = [
        dot(active[slot * share : (slot + 1) * share], full_down) for slot in range(head_count)
    ]
    ffn_parts[1:] = [v.astype(bf16) for v in ffn_parts[1:]]
    grad_slots, ffn_parts = lax.optimization_barrier((grad_slots, ffn_parts))

    own_grads, other_grads = attend_backward(
        scal, slots, other_slots, grad_slots, logs, heads, members
    )
    own_grads, other_grads, grad_attn[:-1] = lax.optimization_barrier(
        (own_grads, other_grads, grad_attn[:-1])
    )
    other_grads = [
        among(v, members - step) for step, v in zip(range(1, members), other_grads)
    ]
    sums = []
    for slot in range(heads):
        total = own_grads[slot].astype(f32)
        sums.append(sum([v[slot].astype(f32) for v in other_grads], total).astype(bf16))
    sums, ffn_parts = lax.optimization_barrier((sums, ffn_parts))
    sums = exchange(sums)
    ffn_parts = scatter_heads(ffn_parts)
    grad_attn = jnp.concatenate(grad_attn, axis=0)
    grad_out_part = contract(jnp.concatenate(heads_rel, axis=0), grad_attn, 0, 0).astype(bf16)
    grad_out_part, sums, ffn_parts[:-1] = lax.optimization_barrier(
        (grad_out_part, sums, ffn_parts[:-1])
    )
    total_out = scatter_members(grad_out_part)
    grad_projected = gather_grads(scal, cosine, -sine, sums)
    grad_qkv_part = contract(normed_low, grad_projected, 0, 0).astype(bf16)
    grad_projected, grad_qkv_part, ffn_parts, grad_down, grad_up = lax.optimization_barrier(
        (grad_projected, grad_qkv_part, ffn_parts, grad_down, grad_up)
    )
    total_qkv = lax.psum_scatter(grad_qkv_part, "seq", scatter_dimension=0, tiled=True)
    grad_down, grad_up = grad_down.astype(f32), grad_up.astype(f32)
    output_own = (
        hidden + sum([v.astype(f32) for v in ffn_parts[1:]], ffn_parts[0])
    ).astype(bf16)
    output_slots = [output_own] + [
        swap(output_own, slot) for slot in range(1, head_count - 1)
    ]
    one_parts = [
        sum(
            contract(
                own_rows(grad_projected, slot)[:, part * head_width : (part + 1) * head_width],
                w_qkv[:, part],
                1,
                1,
            )
            for part in range(3)
        )
        for slot in range(head_count)
    ]
    one_parts[1:] = [v.astype(bf16) for v in one_parts[1:]]
    one_parts, total_out, output_slots = lax.optimization_barrier(
        (one_parts, total_out, output_slots)
    )
    one_parts = scatter_heads(one_parts)
    total_out = scatter_places(total_out)

    grad_one = sum([v.astype(f32) for v in one_parts[1:]], one_parts[0]) + grad_pooled_own
    back_one, gain_one = normalize_back(grad_one, hat_own, inverse_own, gain_attn)
    tokens_back = (grad_hidden + back_one).astype(bf16)
    gains = butterfly(jnp.stack([gain_one, gain_two]), "heads", head_count)
    tokens_back, total_qkv, total_out, gains = lax.optimization_barrier(
        (tokens_back, total_qkv, total_out, gains)
    )
    total_qkv = lax.all_gather(total_qkv, "seq", axis=0, tiled=True)
    token_slots = gather_heads(tokens_back)
    grad_out = gather_seq(total_out).astype(f32)
    grad_qkv = widen(total_qkv).transpose(1, 0, 2)
    token_slots, gains, output_slots = lax.optimization_barrier(
        (token_slots, gains, output_slots)
    )
    output_slots.append(swap(output_slots[0], head_count - 1))
    output = in_order(output_slots, bf16)
    gains = butterfly(gains, "seq", seq_count)
    grad_tokens = in_order(token_slots, f32)
    return (
        output,
        grad_tokens,
        grad_qkv,
        grad_out,
        grad_up,
        grad_down,
        gains[0],
        gains[1],
        grad_router,
    )


def solution(mesh):
    return jax.shard_map(
        local,
        mesh=mesh,
        in_specs=(
            P("seq", None),
            P(None, None, "heads"),
            P("heads", None),
            P("seq", "heads"),
            P("heads", "seq"),
            P(),
            P(),
            P(),
            P(),
            P(),
            P(),
            P("seq", None),
        ),
        out_specs=(
            P("seq", None),
            P("seq", None),
            P(None, None, "heads"),
            P("heads", None),
            P("seq", "heads"),
            P("heads", "seq"),
            P(),
            P(),
            P(),
        ),
        check_vma=False,
    )
```
